32 devices in a mesh: dp: 8 (over y, x, core), tensor: 4 (over z).
Axes of the slice: x: 2, y: 2, z: 4, core: 2. Of those that a mesh axis runs over, the one named last changes fastest.
Arguments:
- tokens: bfloat16 [4096, 2048], P('dp'), may hold values from -6 to 6
- seq_ids: int32 [4096], replicated, may hold values from 0 to 3, never falling along the last dimension, each value on 1 to 2048 neighbouring positions
- route_ids: int32 [4096, 6], P('dp'), may hold values from 0 to 63, all different within a row; in each aligned block of 512 rows (0 to 511, 512 to 1023, ...) at most 72 rows name the same one
- cotangent: bfloat16 [4096, 2048], P('dp'), may hold values from -6 to 6
- input_gain: float32 [2048], replicated, may hold values from 0.5 to 1.5
- w_query: bfloat16 [2048, 3072], P(None, 'tensor'), may hold values from -0.125 to 0.125
- w_latent: bfloat16 [2048, 576], replicated, may hold values from -0.125 to 0.125
- latent_gain: float32 [512], replicated, may hold values from 0.5 to 1.5
- w_expand: bfloat16 [512, 4096], P(None, 'tensor'), may hold values from -0.25 to 0.25
- w_out: bfloat16 [2048, 2048], P('tensor'), may hold values from -0.5 to 0.5
- middle_gain: float32 [2048], replicated, may hold values from 0.5 to 1.5
- w_router: bfloat16 [2048, 64], replicated, may hold values from -0.0390625 to 0.0390625
- expert_gate: bfloat16 [64, 2048, 1408], P('dp', None, 'tensor'), may hold values from -0.125 to 0.125
- expert_up: bfloat16 [64, 2048, 1408], P('dp', None, 'tensor'), may hold values from -0.125 to 0.125
- expert_down: bfloat16 [64, 1408, 2048], P('dp', 'tensor'), may hold values from -2.5 to 2.5
- shared_gate: bfloat16 [2048, 2816], P(None, 'tensor'), may hold values from -0.125 to 0.125
- shared_up: bfloat16 [2048, 2816], P(None, 'tensor'), may hold values from -0.125 to 0.125
- shared_down: bfloat16 [2816, 2048], P('tensor'), may hold values from -0.21875 to 0.21875
Outputs:
- output: bfloat16 [4096, 2048], P('dp')
- token_grad: bfloat16 [4096, 2048], P('dp')
- grad_input_gain: float32 [2048], P('dp')
- grad_query: float32 [2048, 3072], P('dp', 'tensor')
- grad_latent: float32 [2048, 576], P('dp')
- grad_latent_gain: float32 [512], P('dp')
- grad_expand: float32 [512, 4096], P('dp', 'tensor')
- grad_out_proj: float32 [2048, 2048], P('tensor', 'dp')
- grad_middle_gain: float32 [2048], P('dp')
- grad_router: float32 [2048, 64], P('dp')
- grad_expert_gate: float32 [64, 2048, 1408], P('dp', None, 'tensor')
- grad_expert_up: float32 [64, 2048, 1408], P('dp', None, 'tensor')
- grad_expert_down: float32 [64, 1408, 2048], P('dp', 'tensor')
- grad_shared_gate: float32 [2048, 2816], P('dp', 'tensor')
- grad_shared_up: float32 [2048, 2816], P('dp', 'tensor')
- grad_shared_down: float32 [2816, 2048], P('tensor', 'dp')
The draws below stay inside these ranges and needn't reach their ends.
Inputs may be any that keep to these rules, and one draw needn't show every extreme that they name: seq_ids never fall; each sequence has 1 to 2048 tokens, one has exactly 2048. `route_ids`: each row names 6 different experts; in the rows of one data block (512 tokens) no expert is named by more than 72 rows, a bound that some block reaches.
All inputs are finite; a program needn't handle non-finite values.
Results may differ from the reference program's by a relative error of at most 0.025.
Values may be sent and summed in bfloat16 or wider, within the bound.
No kernel may reach another device: no remote copies, remote signals or barrier semaphores. Data moves between devices by JAX's collectives and lax.ppermute only.
A program may use at most 448 MiB of HBM per device.

```python
import math
import jax
import jax.numpy as jnp
import numpy as np
from jax import lax

MODEL_DIM = 2048
H = 16
DN = 128
DR = 64
DV = 128
KVR = 512
ROUTED_EXPERTS = 64
FF = 1408
TOP = 6
SHARED = 2
TOK_DEV = 512
SEQ_LEN = 2048
TOKENS = 4096
SEQS = 4
REACH = 4
CAP = 72
N_DP = 8
N_TENSOR = 4


def level_of(rng, shape, cuts, smallest, high):
    gain = 1.0
    for dim, blocks in cuts:
        draws = jax.random.uniform(jax.random.fold_in(jax.random.fold_in(rng, 6), dim), (blocks,), jnp.float32, smallest / len(cuts), high / len(cuts))
        gain = gain * jnp.repeat(jnp.exp(draws), shape[dim] // blocks).reshape((-1,) + (1,) * (len(shape) - 1 - dim))
    return gain


def length_profile(count, total, reach, lean):
    loads = [(1 << 20) // math.isqrt(standing ** lean) + 1 for standing in range(2, count + 1)]
    surplus, counts = total - reach - (count - 1), [1] * (count - 1)
    while surplus > 0:
        movable = [i for i in range(count - 1) if counts[i] < reach]
        pool, left = sum([loads[i] for i in movable]), surplus
        for i in movable:
            addition = min(reach - counts[i], max(1, left * loads[i] // pool), surplus)
            counts[i] = counts[i] + addition
            surplus = surplus - addition
    return np.array([reach] + counts)


def uneven_parts(own_key, number_of, total, bound, skew):
    if number_of == 2:
        one = jax.random.randint(own_key, (), max(1, total - bound), min(bound, total - 1) + 1)
        return jnp.stack([one, total - one])
    tallies = jnp.asarray(length_profile(number_of, total, bound, skew), jnp.int32)
    couples = (number_of - 1) // 2
    donor, sink = tallies[1:1 + 2 * couples:2], tallies[2:2 + 2 * couples:2]
    slack = jnp.minimum(donor - 1, bound - sink)
    shifted = jax.random.randint(jax.random.fold_in(own_key, 1), (couples,), 0, 1 << 20) % (slack + 1)
    tallies = tallies.at[1:1 + 2 * couples:2].set(donor - shifted).at[2:2 + 2 * couples:2].set(sink + shifted)
    return tallies[jax.random.permutation(jax.random.fold_in(own_key, 2), number_of)]


def deal_out(rng, own, number, rows, amount, top, limit, skew):
    sequence = jax.random.permutation(rng, amount)
    crowded, common = load_shares(amount, rows * top, limit, skew, True), load_shares(amount, rows * top, limit, skew, False)
    places = jnp.arange(amount)

    def named(lengths, rotation):
        used = int((lengths > 0).sum())
        fixed = max(1, used // 4)
        passed = fixed + (places - fixed + rotation * (used - fixed)) % max(1, amount - fixed)
        return jnp.zeros((amount,), jnp.int32).at[sequence[jnp.where(places < fixed, places, passed)]].set(jnp.asarray(lengths, jnp.int32))

    lengths = jnp.where(number % 4 == 0, named(crowded, number // 4), named(common, number - number // 4 - 1))
    mixed = jax.random.permutation(jax.random.fold_in(own, 3), amount)
    donor, sink = mixed[0:amount // 2 * 2:2], mixed[1:amount // 2 * 2:2]
    margin = jnp.minimum(lengths[donor] - 1, limit - lengths[sink]) // 2
    margin = jnp.where((donor == sequence[0]) | (sink == sequence[0]) | (lengths[sink] == 0), 0, jnp.maximum(margin, 0))
    passed = jax.random.randint(jax.random.fold_in(own, 4), (amount // 2,), 0, 1 << 20) % (margin + 1)
    lengths = lengths.at[donor].add(-passed).at[sink].add(passed)
    members = jnp.searchsorted(jnp.cumsum(lengths), jnp.arange(rows * top), side="right").astype(jnp.int32)
    grid = members.reshape(top, rows).T
    grid = grid[jax.random.permutation(jax.random.fold_in(own, 1), rows)]
    rotation = jax.random.randint(jax.random.fold_in(own, 2), (rows, 1), 0, top)
    return jnp.take_along_axis(grid, (jnp.arange(top)[None, :] + rotation) % top, axis=1)


def load_shares(number_of, total, reach, skew, full):
    loads = [(1 << 20) // math.isqrt(standing ** skew) + 1 for standing in range(1, number_of + 1)]
    largest = reach if full else min(reach, max(-(-total // number_of), total * loads[0] // sum(loads)))
    least = 1 if total - largest >= number_of - 1 else 0
    given, rest = [largest] + [least] * (number_of - 1), total - largest - least * (number_of - 1)
    while rest > 0:
        free = [i for i in range(1, number_of) if given[i] < largest] or [i for i in range(1, number_of) if given[i] < reach]
        pool, budget = sum([loads[i] for i in free]), rest
        for i in free:
            extra = min(reach - given[i], max(1, budget * loads[i] // pool), rest)
            given[i] = given[i] + extra
            rest = rest - extra
    return np.array(given)


def centred(own_key, extent, spread, limit, split=(), kind=jnp.bfloat16):
    result = spread * jax.random.normal(own_key, extent, jnp.float32)
    if split:
        result = result * level_of(own_key, extent, split, -0.22, 0.18)
    return jnp.clip(result, -limit, limit).astype(kind)


def setup_inputs(seed: int = 0) -> dict:
    keys = jax.random.split(jax.random.key(seed), 19)
    tokens = centred(keys[0], (TOKENS, MODEL_DIM), 1.0, 6.0, ((0, 8),))
    seq_ids = jnp.searchsorted(jnp.cumsum(uneven_parts(keys[1], SEQS, TOKENS, SEQ_LEN, 1)), jnp.arange(TOKENS), side="right").astype(jnp.int32)
    route_ids_keys = jax.random.split(jax.random.fold_in(keys[2], 1), TOKENS // TOK_DEV)
    route_ids_turns = jax.random.permutation(jax.random.fold_in(keys[2], 3), TOKENS // TOK_DEV)
    route_ids = jax.vmap(lambda own, number: deal_out(jax.random.fold_in(keys[2], 2), own, number, TOK_DEV, ROUTED_EXPERTS, TOP, CAP, 1))(route_ids_keys, route_ids_turns).reshape((TOKENS, TOP))
    cotangent = centred(keys[3], (TOKENS, MODEL_DIM), 1.0, 6.0, ((0, 8),))
    input_gain = jnp.clip(1.0 + 0.1 * jax.random.normal(keys[4], (MODEL_DIM,), jnp.float32), 0.5, 1.5)
    w_query = centred(keys[5], (MODEL_DIM, H * (DN + DR)), MODEL_DIM ** -0.5, 0.125, ((1, 4),))
    w_latent = centred(keys[6], (MODEL_DIM, KVR + DR), MODEL_DIM ** -0.5, 0.125)
    latent_gain = jnp.clip(1.0 + 0.1 * jax.random.normal(keys[7], (KVR,), jnp.float32), 0.5, 1.5)
    w_expand = centred(keys[8], (KVR, H * (DN + DV)), KVR ** -0.5, 0.25, ((1, 4),))
    w_out = centred(keys[9], (H * DV, MODEL_DIM), (H * DV // 16) ** -0.5, 0.5, ((0, 4),))
    middle_gain = jnp.clip(1.0 + 0.1 * jax.random.normal(keys[10], (MODEL_DIM,), jnp.float32), 0.5, 1.5)
    w_router = centred(keys[11], (MODEL_DIM, ROUTED_EXPERTS), (MODEL_DIM * 11) ** -0.5, 0.0390625)
    expert_gate = centred(keys[12], (ROUTED_EXPERTS, MODEL_DIM, FF), MODEL_DIM ** -0.5, 0.125, ((0, 8), (2, 4)))
    expert_up = centred(keys[13], (ROUTED_EXPERTS, MODEL_DIM, FF), MODEL_DIM ** -0.5, 0.125, ((0, 8), (2, 4)))
    expert_down = centred(keys[14], (ROUTED_EXPERTS, FF, MODEL_DIM), (FF // 256 + 1) ** -0.5, 2.5, ((0, 8), (1, 4)))
    shared_gate = centred(keys[15], (MODEL_DIM, SHARED * FF), MODEL_DIM ** -0.5, 0.125, ((1, 4),))
    shared_up = centred(keys[16], (MODEL_DIM, SHARED * FF), MODEL_DIM ** -0.5, 0.125, ((1, 4),))
    shared_down = centred(keys[17], (SHARED * FF, MODEL_DIM), (SHARED * FF // 4) ** -0.5, 0.21875, ((0, 4),))
    return {"tokens": tokens, "seq_ids": seq_ids, "route_ids": route_ids, "cotangent": cotangent, "input_gain": input_gain, "w_query": w_query, "w_latent": w_latent, "latent_gain": latent_gain, "w_expand": w_expand, "w_out": w_out, "middle_gain": middle_gain, "w_router": w_router, "expert_gate": expert_gate, "expert_up": expert_up, "expert_down": expert_down, "shared_gate": shared_gate, "shared_up": shared_up, "shared_down": shared_down}


@jax.custom_vjp
def low(v):
    return lax.optimization_barrier(v.astype(jnp.bfloat16)).astype(jnp.float32)

@jax.custom_vjp
def low_back(v):
    return v

def low_keep(v):
    return (low(v), None)

def low_pass(kept, grad):
    return (grad,)

def back_keep(v):
    return (v, None)

def back_low(kept, grad):
    return (low(grad),)
low.defvjp(low_keep, low_pass)
low_back.defvjp(back_keep, back_low)
epsilon = 1e-06
highest = lax.Precision.HIGHEST

def matmul(left, right):
    return jnp.dot(left, right, precision=highest, preferred_element_type=jnp.float32)

def normed(values, norm_gain):
    return values * lax.rsqrt(lax.optimization_barrier(jnp.mean(values * values, axis=-1, keepdims=True)) + epsilon) * norm_gain

def rotate(values, cosine, sine_table):
    half_width = values.shape[-1] // 2
    front_half = values[..., :half_width]
    back_half = values[..., half_width:]
    return jnp.concatenate([front_half * cosine - back_half * sine_table, back_half * cosine + front_half * sine_table], axis=-1)

def silu_gate(gate_val, up_val):
    return gate_val * jax.nn.sigmoid(gate_val) * up_val

def rope_tables(seq_all, seq_here, index_here):
    starts = jnp.searchsorted(seq_all, seq_here, side='left').astype(jnp.int32)
    position = (index_here - starts).astype(jnp.float32)
    frequency = 10000.0 ** (-(jnp.arange(DR // 2, dtype=jnp.float32) * 2.0) / DR)
    angle = position[:, None] * frequency[None, :]
    return (jnp.cos(angle), jnp.sin(angle))

def reference(tokens, seq_ids, route_ids, cotangent, input_gain, w_query, w_latent, latent_gain, w_expand, w_out, middle_gain, w_router, expert_gate, expert_up, expert_down, shared_gate, shared_up, shared_down):
    index_all = jnp.arange(TOKENS, dtype=jnp.int32)
    cosine, sine_table = rope_tables(seq_ids, seq_ids, index_all)
    each_expert = N_DP * CAP
    flat_expert = route_ids.reshape(-1).astype(jnp.int32)
    onehot = (flat_expert.reshape(N_DP, TOK_DEV * TOP)[:, :, None] == jnp.arange(ROUTED_EXPERTS, dtype=jnp.int32)[None, None, :]).astype(jnp.int32)
    rank_within = lax.optimization_barrier(jnp.sum((jnp.cumsum(onehot, axis=1) - onehot) * onehot, axis=2)).reshape(-1)
    source_block = jnp.arange(TOKENS * TOP, dtype=jnp.int32) // (TOK_DEV * TOP)
    slot_index = flat_expert * each_expert + source_block * CAP + rank_within
    slot_source = jnp.zeros((ROUTED_EXPERTS * each_expert,), jnp.int32).at[slot_index].set(jnp.arange(TOKENS * TOP, dtype=jnp.int32) + 1)
    filled = slot_source > 0
    slot_entry = jnp.maximum(slot_source - 1, 0)
    slot_token = slot_entry // TOP
    pad_rows = REACH * TOK_DEV
    window = (REACH + 1) * TOK_DEV
    seq_padded = jnp.concatenate([jnp.full((pad_rows,), -1, jnp.int32), seq_ids.astype(jnp.int32)])
    scale = (DN + DR) ** (-0.5)
    slice_width = FF // N_TENSOR

    def forward_pass(token_features, input_norm_gain, query_weight, latent_weight, latent_norm_gain, expand_weight, output_weight, middle_norm_gain, router_weight, expert_gate_weight, expert_up_weight, expert_down_weight, shared_gate_weight, shared_up_weight, shared_down_weight):
        hidden_in = low(normed(token_features, input_norm_gain))
        query_pre = low_back(matmul(hidden_in, query_weight)).reshape(TOKENS, H, DN + DR)
        queries = low(jnp.concatenate([query_pre[..., :DN], rotate(query_pre[..., DN:], cosine[:, None, :], sine_table[:, None, :])], axis=-1))
        latent_full = low_back(matmul(hidden_in, latent_weight))
        latent = low(normed(latent_full[:, :KVR], latent_norm_gain))
        rope_key = low(rotate(latent_full[:, KVR:], cosine, sine_table))
        expanded = low(matmul(latent, expand_weight)).reshape(TOKENS, H, DN + DV)
        expanded_pad = jnp.concatenate([jnp.zeros((pad_rows, H, DN + DV), jnp.float32), expanded], axis=0)
        rope_pad = jnp.concatenate([jnp.zeros((pad_rows, DR), jnp.float32), rope_key], axis=0)

        def attend(block):
            start = (block * TOK_DEV).astype(jnp.int32)
            query_block = lax.dynamic_slice_in_dim(queries, start, TOK_DEV, 0)
            keys_block = low_back(lax.dynamic_slice_in_dim(expanded_pad, start, window, 0))
            rope_block = lax.dynamic_slice_in_dim(rope_pad, start, window, 0)
            seq_query = lax.dynamic_slice_in_dim(seq_ids.astype(jnp.int32), start, TOK_DEV, 0)
            seq_keys = lax.dynamic_slice_in_dim(seq_padded, start, window, 0)
            query_pos = jnp.arange(TOK_DEV, dtype=jnp.int32) + pad_rows
            key_pos = jnp.arange(window, dtype=jnp.int32)
            allowed = (seq_query[:, None] == seq_keys[None, :]) & (key_pos[None, :] <= query_pos[:, None])
            scores = jnp.einsum('qhd,khd->hqk', query_block[..., :DN], keys_block[..., :DN], precision=highest) + jnp.einsum('qhd,kd->hqk', query_block[..., DN:], rope_block, precision=highest)
            scores = low_back(scores * scale)
            scores = jnp.where(allowed[None], scores, -1e+30)
            probs = low(jax.nn.softmax(scores, axis=-1))
            mixed = jnp.einsum('hqk,khd->qhd', probs, keys_block[..., DN:], precision=highest)
            return low_back(low(mixed)).reshape(TOK_DEV, H * DV)
        attended = lax.map(jax.checkpoint(attend), jnp.arange(N_DP, dtype=jnp.int32)).reshape(TOKENS, H * DV)
        attention = low_back(matmul(attended, output_weight))
        middle = token_features + attention
        hidden_mid = low(normed(middle, middle_norm_gain))
        logits = low_back(matmul(hidden_mid, router_weight))
        router_probs = jax.nn.softmax(logits, axis=-1)
        gates = jnp.take_along_axis(router_probs, route_ids.astype(jnp.int32), axis=1)
        rows_per_expert = jnp.where(filled[:, None], hidden_mid[slot_token], 0.0).reshape(ROUTED_EXPERTS, each_expert, MODEL_DIM)

        def apply_expert(packed):
            rows_here, gate_here, up_here, down_here = packed

            def slice_apply(gate_part, up_part, down_part):
                taken = low_back(rows_here)
                gate_val = low_back(matmul(taken, gate_part))
                up_val = low_back(matmul(taken, up_part))
                active = low(silu_gate(gate_val, up_val))
                return low_back(low(matmul(active, down_part)))
            pieces = jax.vmap(slice_apply)(gate_here.reshape(MODEL_DIM, N_TENSOR, slice_width).transpose(1, 0, 2), up_here.reshape(MODEL_DIM, N_TENSOR, slice_width).transpose(1, 0, 2), down_here.reshape(N_TENSOR, slice_width, MODEL_DIM))
            return lax.optimization_barrier(jnp.sum(pieces, axis=0))
        expert_output = lax.map(jax.checkpoint(apply_expert), (rows_per_expert, expert_gate_weight, expert_up_weight, expert_down_weight)).reshape(ROUTED_EXPERTS * each_expert, MODEL_DIM)
        slot_gate = jnp.where(filled, gates.reshape(-1)[slot_entry], 0.0)
        routed = jnp.zeros((TOKENS, MODEL_DIM), jnp.float32).at[slot_token].add(expert_output * slot_gate[:, None])
        shared_gate_val = low_back(matmul(hidden_mid, shared_gate_weight))
        shared_up_val = low_back(matmul(hidden_mid, shared_up_weight))
        shared_active = low(silu_gate(shared_gate_val, shared_up_val))
        shared_out = matmul(shared_active, shared_down_weight)
        return middle + routed + shared_out
    floats = tuple((value.astype(jnp.float32) for value in (tokens, input_gain, w_query, w_latent, latent_gain, w_expand, w_out, middle_gain, w_router, expert_gate, expert_up, expert_down, shared_gate, shared_up, shared_down)))
    output, pullback = jax.vjp(forward_pass, *floats)
    grads = pullback(cotangent.astype(jnp.float32))
    return (output.astype(jnp.bfloat16), grads[0].astype(jnp.bfloat16), grads[1], grads[2], grads[3], grads[4], grads[5], grads[6], grads[7], grads[8], grads[9], grads[10], grads[11], grads[12], grads[13], grads[14])
```

```python
import jax
import jax.numpy as jnp
from jax import lax
from jax.sharding import PartitionSpec as P

DN = 128
DR = 64
DV = 128
KVR = 512
REACH = 4
CAP = 72
BF = jnp.bfloat16
F32 = jnp.float32

epsilon = 1e-06


def dot(eq, a, b):
    return jnp.einsum(eq, a, b, preferred_element_type=F32)


def passed_along(shard, axis, by):
    peers = lax.axis_size(axis)
    pairs = [(i, i + by) for i in range(peers) if 0 <= i + by < peers]
    return lax.ppermute(shard, axis, pairs)


def normed(values, norm_gain):
    return (
        values * lax.rsqrt(jnp.mean(values * values, axis=-1, keepdims=True) + epsilon) * norm_gain
    )


def norm_backward(values, norm_gain, upstream):
    _, pullback = jax.vjp(normed, values, norm_gain)
    return pullback(upstream)


def rotate(values, cosine, sine):
    half = values.shape[-1] // 2
    front, back = values[..., :half], values[..., half:]
    return jnp.concatenate([front * cosine - back * sine, back * cosine + front * sine], axis=-1)


def rotate_back(upstream, cosine, sine):
    return rotate(upstream, cosine, -sine)


def silu_gate(gate_val, up_val):
    return gate_val * jax.nn.sigmoid(gate_val) * up_val


def silu_backward(gate_val, up_val, upstream):
    _, pullback = jax.vjp(silu_gate, gate_val, up_val)
    return pullback(upstream)


def rope_tables(seq_all, seq_here, index_here):
    starts = jnp.sum((seq_all[None, :] < seq_here[:, None]).astype(jnp.int32), axis=1)
    position = (index_here - starts).astype(F32)
    frequency = 10000.0 ** (-(jnp.arange(DR // 2, dtype=F32) * 2.0) / DR)
    angle = position[:, None] * frequency[None, :]
    return jnp.cos(angle), jnp.sin(angle)


def scatter_sum(parts):
    joined = jnp.concatenate(parts, axis=1)
    summed = lax.psum_scatter(joined, "dp", scatter_dimension=0, tiled=True)
    out, at = [], 0
    for part in parts:
        out.append(summed[:, at : at + part.shape[1]].astype(F32))
        at += part.shape[1]
    return out


def shards(
    tokens,
    seq_ids,
    route_ids,
    cotangent,
    input_gain,
    w_query,
    w_latent,
    latent_gain,
    w_expand,
    w_out,
    middle_gain,
    w_router,
    expert_gate,
    expert_up,
    expert_down,
    shared_gate,
    shared_up,
    shared_down,
):
    devices = lax.axis_size("dp")
    rank_dp = lax.axis_index("dp")
    tok_rows, width = tokens.shape
    experts_local = expert_gate.shape[0]
    heads_local = w_query.shape[1] // (DN + DR)
    reach = min(REACH, devices - 1)
    window = (reach + 1) * tok_rows
    scale = (DN + DR) ** (-0.5)

    cot_all = lax.all_gather(cotangent, "dp", tiled=True)
    route_all = lax.all_gather(route_ids, "dp", tiled=True)

    index_here = rank_dp * tok_rows + jnp.arange(tok_rows, dtype=jnp.int32)
    seq_here = lax.dynamic_slice_in_dim(seq_ids, rank_dp * tok_rows, tok_rows, 0)
    cosine, sine = rope_tables(seq_ids, seq_here, index_here)
    key_index = (rank_dp - reach) * tok_rows + jnp.arange(window, dtype=jnp.int32)
    seq_padded = jnp.concatenate([jnp.full((reach * tok_rows,), -1, jnp.int32), seq_ids])
    seq_keys = lax.dynamic_slice_in_dim(seq_padded, rank_dp * tok_rows, window, 0)
    allowed = (seq_here[:, None] == seq_keys[None, :]) & (key_index[None, :] <= index_here[:, None])

    token_features = tokens.astype(F32)
    grad_output = cotangent.astype(F32)
    hidden_in = normed(token_features, input_gain).astype(BF)
    latent_full = jnp.dot(hidden_in, w_latent, preferred_element_type=F32)
    latent_raw = latent_full[:, :KVR]
    latent = normed(latent_raw, latent_gain).astype(BF)
    rope_key = rotate(latent_full[:, KVR:], cosine, sine).astype(BF)
    own_keys = jnp.concatenate([latent, rope_key], axis=1)
    earlier = [passed_along(own_keys, "dp", back) for back in range(reach, 0, -1)]
    keys_window = jnp.concatenate(earlier + [own_keys], axis=0)
    latent_window = keys_window[:, :KVR]
    rope_window = keys_window[:, KVR:]
    query_pre = jnp.dot(hidden_in, w_query, preferred_element_type=F32).reshape(
        tok_rows, heads_local, DN + DR
    )
    queries = jnp.concatenate(
        [
            query_pre[..., :DN],
            rotate(query_pre[..., DN:], cosine[:, None, :], sine[:, None, :]),
        ],
        axis=-1,
    ).astype(BF)
    expanded = (
        jnp.dot(latent_window, w_expand, preferred_element_type=F32)
        .astype(BF)
        .reshape(window, heads_local, DN + DV)
    )
    key_nope = expanded[..., :DN]
    key_value = expanded[..., DN:]
    scores = dot("qhd,khd->hqk", queries[..., :DN], key_nope) + dot(
        "qhd,kd->hqk", queries[..., DN:], rope_window
    )
    scores = jnp.where(allowed[None], scores * scale, -1e30)
    probs = jax.nn.softmax(scores, axis=-1)
    probs_low = probs.astype(BF)
    attended = (
        dot("hqk,khd->qhd", probs_low, key_value).astype(BF).reshape(tok_rows, heads_local * DV)
    )
    attention = lax.psum(
        jnp.dot(attended, w_out, preferred_element_type=F32).astype(BF), "tensor"
    ).astype(F32)
    middle = token_features + attention
    hidden_mid = normed(middle, middle_gain).astype(BF)
    hidden_all = lax.all_gather(hidden_mid, "dp", tiled=True)

    shared_gate_val = jnp.dot(hidden_mid, shared_gate, preferred_element_type=F32)
    shared_up_val = jnp.dot(hidden_mid, shared_up, preferred_element_type=F32)
    shared_active = silu_gate(shared_gate_val, shared_up_val).astype(BF)
    shared_result = jnp.dot(shared_active, shared_down, preferred_element_type=F32)
    shared_active_grad = dot("td,fd->tf", cotangent, shared_down)
    shared_gate_grad, shared_up_grad = silu_backward(
        shared_gate_val, shared_up_val, shared_active_grad
    )
    shared_gate_grad = shared_gate_grad.astype(BF)
    shared_up_grad = shared_up_grad.astype(BF)
    mid_from_shared = dot("tf,df->td", shared_gate_grad, shared_gate) + dot(
        "tf,df->td", shared_up_grad, shared_up
    )
    grad_shared_down = dot("td,tf->df", cotangent, shared_active).astype(BF)
    grad_shared_gate = dot("td,tf->df", hidden_mid, shared_gate_grad).astype(BF)
    grad_shared_up = dot("td,tf->df", hidden_mid, shared_up_grad).astype(BF)

    local_ids = rank_dp * experts_local + jnp.arange(experts_local, dtype=jnp.int32)
    named = jnp.any(route_all[:, :, None] == local_ids[None, None, :], axis=1)
    named_block = named.reshape(devices, tok_rows, experts_local)
    before = jnp.tril(jnp.ones((tok_rows, tok_rows), BF), -1)
    rank_within = dot("ts,bse->bet", before, named_block.astype(BF)).astype(jnp.int32)
    slot = jnp.where(named_block.transpose(0, 2, 1), rank_within, -1)
    chosen = (slot[:, :, None, :] == jnp.arange(CAP, dtype=jnp.int32)[None, None, :, None]).astype(
        BF
    )

    logits = jnp.dot(hidden_all, w_router, preferred_element_type=F32)
    router_probs = jax.nn.softmax(logits, axis=-1)
    local_probs = lax.dynamic_slice_in_dim(
        router_probs, rank_dp * experts_local, experts_local, 1
    ).reshape(devices, tok_rows, experts_local)
    slot_gates = jnp.sum(
        chosen.astype(F32) * local_probs.transpose(0, 2, 1)[:, :, None, :], axis=-1
    )

    cot_rows = dot("bect,btd->becd", chosen, cot_all.reshape(devices, tok_rows, width)).astype(BF)
    rows = dot("bect,btd->becd", chosen, hidden_all.reshape(devices, tok_rows, width)).astype(BF)
    gate_val = dot("becd,edf->becf", rows, expert_gate)
    up_val = dot("becd,edf->becf", rows, expert_up)
    down_back = dot("becd,efd->becf", cot_rows, expert_down)
    active = silu_gate(gate_val, up_val).astype(BF)
    gated_active = active.astype(F32) * slot_gates[..., None]
    gate_grad = jnp.sum(active.astype(F32) * down_back, axis=-1)
    gate_val_grad, up_val_grad = silu_backward(gate_val, up_val, down_back * slot_gates[..., None])
    gate_val_grad = gate_val_grad.astype(BF)
    up_val_grad = up_val_grad.astype(BF)
    gated_active = gated_active.astype(BF)
    row_grad = (
        dot("becf,edf->becd", gate_val_grad, expert_gate)
        + dot("becf,edf->becd", up_val_grad, expert_up)
    ).astype(BF)
    row_out = dot("becf,efd->becd", gated_active, expert_down).astype(BF)

    probs_grad = dot("bect,bec->bte", chosen, gate_grad.astype(BF)).reshape(-1, experts_local)
    probs_grad = lax.dynamic_update_slice_in_dim(
        jnp.zeros_like(router_probs), probs_grad, rank_dp * experts_local, 1
    )
    logit_grad = (
        router_probs * (probs_grad - jnp.sum(router_probs * probs_grad, axis=-1, keepdims=True))
    ).astype(BF)
    grad_router = dot("td,te->de", hidden_all, logit_grad)
    mid_part = dot("bect,becd->btd", chosen, row_grad).reshape(-1, width) + dot(
        "te,de->td", logit_grad, w_router
    )
    mid_block = lax.psum_scatter(mid_part.astype(BF), "dp", scatter_dimension=0, tiled=True)
    mid_grad = lax.psum((mid_block.astype(F32) + mid_from_shared).astype(BF), "tensor").astype(F32)

    routed_part = dot("bect,becd->btd", chosen, row_out).reshape(-1, width).astype(BF)
    routed_part, _ = lax.optimization_barrier((routed_part, mid_block))
    routed_block = lax.psum_scatter(routed_part, "dp", scatter_dimension=0, tiled=True)

    grad_expert_down = dot("becf,becd->efd", gated_active, cot_rows)
    grad_expert_gate = dot("becd,becf->edf", rows, gate_val_grad)
    grad_expert_up = dot("becd,becf->edf", rows, up_val_grad)

    middle_from_norm, grad_middle_gain = norm_backward(middle, middle_gain, mid_grad)
    middle_grad = grad_output + middle_from_norm
    middle_low = middle_grad.astype(BF)
    grad_out_proj = dot("td,tc->dc", middle_low, attended).astype(BF)
    attended_grad = (
        dot("td,cd->tc", middle_low, w_out).astype(BF).reshape(tok_rows, heads_local, DV)
    )
    probs_grad_att = dot("qhd,khd->hqk", attended_grad, key_value)
    score_grad = (
        probs * (probs_grad_att - jnp.sum(probs * probs_grad_att, axis=-1, keepdims=True))
    ).astype(BF)
    query_nope_grad = dot("hqk,khd->qhd", score_grad, key_nope) * scale
    query_rope_grad = dot("hqk,kd->qhd", score_grad, rope_window) * scale
    key_nope_grad = dot("hqk,qhd->khd", score_grad, queries[..., :DN]) * scale
    rope_window_grad = dot("hqk,qhd->kd", score_grad, queries[..., DN:]) * scale
    value_grad = dot("hqk,qhd->khd", probs_low, attended_grad)
    expanded_grad = (
        jnp.concatenate([key_nope_grad, value_grad], axis=-1)
        .astype(BF)
        .reshape(window, heads_local * (DN + DV))
    )
    latent_window_grad = dot("wc,kc->wk", expanded_grad, w_expand)
    grad_expand = dot("wk,wc->kc", latent_window, expanded_grad).astype(BF)
    window_grad = jnp.concatenate([latent_window_grad, rope_window_grad], axis=1)
    keys_grad = window_grad[reach * tok_rows :]
    for back in range(reach, 0, -1):
        start = (reach - back) * tok_rows
        piece = window_grad[start : start + tok_rows].astype(BF)
        keys_grad = keys_grad + passed_along(piece, "dp", -back).astype(F32)
    query_grad = (
        jnp.concatenate(
            [
                query_nope_grad,
                rotate_back(query_rope_grad, cosine[:, None, :], sine[:, None, :]),
            ],
            axis=-1,
        )
        .astype(BF)
        .reshape(tok_rows, heads_local * (DN + DR))
    )
    grad_query = dot("td,tc->dc", hidden_in, query_grad).astype(BF)
    input_from_query = dot("tc,dc->td", query_grad, w_query)
    keys_grad = lax.psum(keys_grad.astype(BF), "tensor").astype(F32)
    latent_raw_grad, grad_latent_gain = norm_backward(latent_raw, latent_gain, keys_grad[:, :KVR])
    rope_raw_grad = rotate_back(keys_grad[:, KVR:], cosine, sine)
    latent_full_grad = jnp.concatenate([latent_raw_grad, rope_raw_grad], axis=-1).astype(BF)
    grad_latent = dot("td,tc->dc", hidden_in, latent_full_grad).astype(BF)
    input_grad = lax.psum(input_from_query.astype(BF), "tensor").astype(F32) + dot(
        "tc,dc->td", latent_full_grad, w_latent
    )
    token_from_norm, grad_input_gain = norm_backward(token_features, input_gain, input_grad)
    token_grad = (middle_grad + token_from_norm).astype(BF)

    routed_block, _ = lax.optimization_barrier((routed_block, mid_grad))
    feedforward = lax.psum((routed_block.astype(F32) + shared_result).astype(BF), "tensor")
    output = (middle + feedforward.astype(F32)).astype(BF)

    grad_shared_down, grad_shared_gate, grad_shared_up = scatter_sum(
        [grad_shared_down, grad_shared_gate, grad_shared_up]
    )
    grad_router = lax.psum(grad_router.astype(BF), "tensor")
    gains = jnp.stack(
        [grad_middle_gain, grad_input_gain, jnp.repeat(grad_latent_gain, width // KVR)], axis=1
    ).astype(BF)
    grad_out_proj, grad_query, grad_latent, grad_expand, grad_router, gains = scatter_sum(
        [
            grad_out_proj,
            grad_query,
            grad_latent,
            grad_expand.reshape(width, -1),
            grad_router,
            gains,
        ]
    )
    grad_expand = grad_expand.reshape(KVR // devices, -1)
    return (
        output,
        token_grad,
        gains[:, 1],
        grad_query,
        grad_latent,
        gains[:: width // KVR, 2],
        grad_expand,
        grad_out_proj.T,
        gains[:, 0],
        grad_router,
        grad_expert_gate,
        grad_expert_up,
        grad_expert_down,
        grad_shared_gate,
        grad_shared_up,
        grad_shared_down.T,
    )


def solution(mesh):
    placed = (
        P("dp", None),
        P(),
        P("dp", None),
        P("dp", None),
        P(),
        P(None, "tensor"),
        P(),
        P(),
        P(None, "tensor"),
        P("tensor", None),
        P(),
        P(),
        P("dp", None, "tensor"),
        P("dp", None, "tensor"),
        P("dp", "tensor", None),
        P(None, "tensor"),
        P(None, "tensor"),
        P("tensor", None),
    )
    return jax.shard_map(
        shards,
        mesh=mesh,
        in_specs=placed,
        out_specs=(
            P("dp", None),
            P("dp", None),
            P("dp"),
            P("dp", "tensor"),
            P("dp", None),
            P("dp"),
            P("dp", "tensor"),
            P("tensor", "dp"),
            P("dp"),
            P("dp", None),
            P("dp", None, "tensor"),
            P("dp", None, "tensor"),
            P("dp", "tensor", None),
            P("dp", "tensor"),
            P("dp", "tensor"),
            P("tensor", "dp"),
        ),
        check_vma=False,
    )
```

```python
import functools

import jax
import jax.numpy as jnp
from jax import lax
from jax.experimental import pallas as pl
from jax.experimental.pallas import tpu as pltpu
from jax.sharding import PartitionSpec as P

DN = 128
DR = 64
DV = 128
KVR = 512
REACH = 4
SLOTS = 80
BF = jnp.bfloat16
F32 = jnp.float32
VMEM_BYTES = 60 * 1024 * 1024
epsilon = 1e-06


def mm(a, b, ca, cb):
    return lax.dot_general(a, b, (((ca,), (cb,)), ((), ())), preferred_element_type=F32)


def cost(flops, nbytes, trans=0):
    return pl.CostEstimate(flops=int(flops), bytes_accessed=int(nbytes), transcendentals=int(trans))


def bias_rows(seq_q, seq_k, pos_q, pos_k):
    return jnp.where((seq_q == seq_k) & (pos_k <= pos_q), 0.0, -1e30)


def attend_kernel(scale, step, q_ref, kv_ref, kr_ref, sq_ref, sk_ref, o_ref, lse_ref, key_ref, bias_ref):
    rows = q_ref.shape[1]

    @pl.when(pl.program_id(0) == 0)
    def _():
        for at in range(0, rows, step):
            part = pl.ds(at, step)
            bias_ref[part, :] = bias_rows(
                sq_ref[part, 0:1], sk_ref[0:1, :], sq_ref[part, 1:2], sk_ref[1:2, :]
            ).astype(BF)
        key_ref[:, DN:] = kr_ref[...]

    key_ref[:, :DN] = kv_ref[:, :DN]
    for at in range(0, rows, step):
        part = pl.ds(at, step)
        s = mm(q_ref[0, part, :], key_ref[...], 1, 1) * scale + bias_ref[part, :].astype(F32)
        top = jnp.max(s, axis=-1, keepdims=True)
        p = jnp.exp(s - top)
        total = jnp.sum(p, axis=-1, keepdims=True)
        o = mm((p * (1.0 / total)).astype(BF), kv_ref[:, DN:], 1, 0)
        o_ref[part, :] = o.astype(BF)
        lse_ref[0, part, :] = top + jnp.log(total)


def attend(queries, expanded, rope_window, seq_pos_q, seq_pos_k):
    heads, rows, qw = queries.shape
    window = expanded.shape[0]
    kvw = DN + DV
    step = rows // 2
    return pl.pallas_call(
        functools.partial(attend_kernel, qw ** (-0.5), step),
        name="attend",
        grid=(heads,),
        in_specs=[
            pl.BlockSpec((1, rows, qw), lambda h: (h, 0, 0)),
            pl.BlockSpec((window, kvw), lambda h: (0, h)),
            pl.BlockSpec((window, DR), lambda h: (0, 0)),
            pl.BlockSpec(seq_pos_q.shape, lambda h: (0, 0)),
            pl.BlockSpec(seq_pos_k.shape, lambda h: (0, 0)),
        ],
        out_specs=[
            pl.BlockSpec((rows, DV), lambda h: (0, h)),
            pl.BlockSpec((1, rows, 1), lambda h: (h, 0, 0)),
        ],
        out_shape=[
            jax.ShapeDtypeStruct((rows, heads * DV), BF),
            jax.ShapeDtypeStruct((heads, rows, 1), F32),
        ],
        scratch_shapes=[pltpu.VMEM((window, qw), BF), pltpu.VMEM((rows, window), BF)],
        compiler_params=pltpu.CompilerParams(vmem_limit_bytes=VMEM_BYTES),
        cost_estimate=cost(
            2 * heads * rows * window * 512, heads * window * 512, heads * rows * window
        ),
    )(queries, expanded, rope_window, seq_pos_q, seq_pos_k)


def attend_back_kernel(
    scale, step, q_ref, kv_ref, kr_ref, sq_ref, sk_ref, lse_ref, do_ref,
    dq_ref, dkv_ref, dkr_ref, key_ref, bias_ref, dk_ref, dv_ref,
):
    rows = q_ref.shape[1]
    head = pl.program_id(0)

    @pl.when(head == 0)
    def _():
        for at in range(0, rows, step):
            part = pl.ds(at, step)
            bias_ref[part, :] = bias_rows(
                sq_ref[part, 0:1], sk_ref[0:1, :], sq_ref[part, 1:2], sk_ref[1:2, :]
            ).astype(BF)
        key_ref[:, DN:] = kr_ref[...]

    key_ref[:, :DN] = kv_ref[:, :DN]
    for at in range(0, rows, step):
        part = pl.ds(at, step)
        q = q_ref[0, part, :]
        do = do_ref[part, :]
        s = mm(q, key_ref[...], 1, 1) * scale + bias_ref[part, :].astype(F32)
        p = jnp.exp(s - lse_ref[0, part, :])
        dp = mm(do, kv_ref[:, DN:], 1, 1)
        ds = (p * (dp - jnp.sum(p * dp, axis=-1, keepdims=True))).astype(BF)
        dq_ref[0, part, :] = mm(ds, key_ref[...], 1, 0) * scale
        dk = mm(ds, q, 0, 0) * scale
        dv = mm(p.astype(BF), do, 0, 0)
        if at == 0:
            dk_ref[...] = dk
            dv_ref[...] = dv
        else:
            dk_ref[...] += dk
            dv_ref[...] += dv
    dkv_ref[:, :DN] = dk_ref[:, :DN].astype(BF)
    dkv_ref[:, DN:] = dv_ref[...].astype(BF)

    @pl.when(head == 0)
    def _():
        dkr_ref[...] = dk_ref[:, DN:]

    @pl.when(head != 0)
    def _():
        dkr_ref[...] += dk_ref[:, DN:]


def attend_back(queries, expanded, rope_window, seq_pos_q, seq_pos_k, lse, attended_grad):
    heads, rows, qw = queries.shape
    window = expanded.shape[0]
    kvw = DN + DV
    step = rows // 2
    return pl.pallas_call(
        functools.partial(attend_back_kernel, qw ** (-0.5), step),
        name="attend_back",
        grid=(heads,),
        in_specs=[
            pl.BlockSpec((1, rows, qw), lambda h: (h, 0, 0)),
            pl.BlockSpec((window, kvw), lambda h: (0, h)),
            pl.BlockSpec((window, DR), lambda h: (0, 0)),
            pl.BlockSpec(seq_pos_q.shape, lambda h: (0, 0)),
            pl.BlockSpec(seq_pos_k.shape, lambda h: (0, 0)),
            pl.BlockSpec((1, rows, 1), lambda h: (h, 0, 0)),
            pl.BlockSpec((rows, DV), lambda h: (0, h)),
        ],
        out_specs=[
            pl.BlockSpec((1, rows, qw), lambda h: (h, 0, 0)),
            pl.BlockSpec((window, kvw), lambda h: (0, h)),
            pl.BlockSpec((window, DR), lambda h: (0, 0)),
        ],
        out_shape=[
            jax.ShapeDtypeStruct((heads, rows, qw), F32),
            jax.ShapeDtypeStruct((window, heads * kvw), BF),
            jax.ShapeDtypeStruct((window, DR), F32),
        ],
        scratch_shapes=[
            pltpu.VMEM((window, qw), BF),
            pltpu.VMEM((rows, window), BF),
            pltpu.VMEM((window, qw), F32),
            pltpu.VMEM((window, DV), F32),
        ],
        compiler_params=pltpu.CompilerParams(vmem_limit_bytes=VMEM_BYTES),
        cost_estimate=cost(
            2 * heads * rows * window * 1280, heads * window * 1024, heads * rows * window
        ),
    )(queries, expanded, rope_window, seq_pos_q, seq_pos_k, lse, attended_grad)


def one_hot(slot_ref):
    experts, rows = slot_ref.shape[0], slot_ref.shape[-1]
    place = lax.broadcasted_iota(jnp.int32, (SLOTS, rows), 0)
    return jnp.concatenate(
        [(slot_ref[e, 0] == place).astype(F32).astype(BF) for e in range(experts)], axis=0
    )


def pick_kernel(slot_ref, x_ref, o_ref):
    experts = slot_ref.shape[0]
    picked = mm(one_hot(slot_ref), x_ref[...], 1, 0).astype(BF)
    o_ref[...] = picked.reshape(o_ref.shape)


def pick(slot, values):
    experts, blocks, _, rows = slot.shape
    width = values.shape[1]
    return pl.pallas_call(
        pick_kernel,
        name="pick",
        grid=(blocks,),
        in_specs=[
            pl.BlockSpec((experts, 1, 1, rows), lambda b: (0, b, 0, 0)),
            pl.BlockSpec((rows, width), lambda b: (b, 0)),
        ],
        out_specs=pl.BlockSpec((experts, 1, SLOTS, width), lambda b: (0, b, 0, 0)),
        out_shape=jax.ShapeDtypeStruct((experts, blocks, SLOTS, width), BF),
        compiler_params=pltpu.CompilerParams(vmem_limit_bytes=VMEM_BYTES),
        cost_estimate=cost(
            2 * experts * blocks * SLOTS * rows * width,
            2 * blocks * width * (rows + experts * SLOTS),
        ),
    )(slot, values)


def put_kernel(place_ref, r_ref, *rest):
    total = mm(place_ref[0], r_ref[...].reshape(-1, r_ref.shape[-1]), 1, 0)
    if len(rest) == 3:
        total += mm(rest[0][...], rest[1][...], 1, 0)
    rest[-1][...] = total.astype(BF)


def put(places, picked, extra=()):
    blocks, rows, slots = places.shape
    experts, width = picked.shape[0], picked.shape[3]
    specs = [
        pl.BlockSpec((1, rows, slots), lambda b: (b, 0, 0)),
        pl.BlockSpec((experts, 1, SLOTS, width), lambda b: (0, b, 0, 0)),
    ]
    if extra:
        lanes = extra[0].shape[1]
        specs += [
            pl.BlockSpec((rows, lanes), lambda b: (b, 0)),
            pl.BlockSpec((lanes, width), lambda b: (0, 0)),
        ]
    return pl.pallas_call(
        put_kernel,
        name="put",
        grid=(blocks,),
        in_specs=specs,
        out_specs=pl.BlockSpec((rows, width), lambda b: (b, 0)),
        out_shape=jax.ShapeDtypeStruct((blocks * rows, width), BF),
        compiler_params=pltpu.CompilerParams(vmem_limit_bytes=VMEM_BYTES),
        cost_estimate=cost(
            2 * blocks * slots * rows * width, 2 * blocks * width * (rows + slots)
        ),
    )(places, picked, *extra)


def down_back_kernel(x_ref, w_ref, o_ref):
    ff = w_ref.shape[1]
    wide = o_ref.shape[-1]
    back = mm(x_ref[...].reshape(-1, x_ref.shape[-1]), w_ref[0], 1, 1)
    o_ref[0, :, :ff] = back
    if wide > ff:
        o_ref[0, :, ff:] = jnp.zeros((o_ref.shape[1], wide - ff), F32)


def down_back(rows, down):
    experts, blocks, slots, width = rows.shape
    ff = down.shape[1]
    wide = -(-ff // 128) * 128
    count = blocks * slots
    return pl.pallas_call(
        down_back_kernel,
        name="down_back",
        grid=(experts,),
        in_specs=[
            pl.BlockSpec((1, blocks, slots, width), lambda e: (e, 0, 0, 0)),
            pl.BlockSpec((1, ff, width), lambda e: (e, 0, 0)),
        ],
        out_specs=pl.BlockSpec((1, count, wide), lambda e: (e, 0, 0)),
        out_shape=jax.ShapeDtypeStruct((experts, count, wide), F32),
        compiler_params=pltpu.CompilerParams(vmem_limit_bytes=VMEM_BYTES),
        cost_estimate=cost(
            2 * experts * count * width * ff,
            experts * (2 * count * width + 2 * ff * width + 4 * count * wide),
        ),
    )(rows, down)


def row_out_kernel(x_ref, w_ref, o_ref):
    ff = w_ref.shape[1]
    o_ref[...] = mm(x_ref[0, :, :ff], w_ref[0], 1, 0).astype(BF).reshape(o_ref.shape)


def row_out(active, down, blocks):
    experts, count, wide = active.shape
    ff, width = down.shape[1:]
    slots = count // blocks
    return pl.pallas_call(
        row_out_kernel,
        name="row_out",
        grid=(experts,),
        in_specs=[
            pl.BlockSpec((1, count, wide), lambda e: (e, 0, 0)),
            pl.BlockSpec((1, ff, width), lambda e: (e, 0, 0)),
        ],
        out_specs=pl.BlockSpec((1, blocks, slots, width), lambda e: (e, 0, 0, 0)),
        out_shape=jax.ShapeDtypeStruct((experts, blocks, slots, width), BF),
        compiler_params=pltpu.CompilerParams(vmem_limit_bytes=VMEM_BYTES),
        cost_estimate=cost(
            2 * experts * count * width * ff,
            2 * experts * (count * width + ff * width + count * wide),
        ),
    )(active, down)


def expert_kernel(
    x_ref, gate_ref, up_ref, back_ref, slot_ref, prob_ref,
    ga_ref, dg_ref, du_ref, dx_ref, pg_ref, w_ref, d_ref,
):
    ff = gate_ref.shape[1]
    wide = back_ref.shape[2]
    blocks, rows = slot_ref.shape[1], slot_ref.shape[3]

    @pl.when(pl.program_id(0) == 0)
    def _():
        w_ref[...] = jnp.zeros_like(w_ref)

    w_ref[:ff, :] = gate_ref[0]
    w_ref[wide : wide + ff, :] = up_ref[0]
    x = x_ref[...].reshape(-1, x_ref.shape[-1])
    both = mm(x, w_ref[...], 1, 1)
    a = both[:, :wide]
    b = both[:, wide:]
    place = lax.broadcasted_iota(jnp.int32, (SLOTS, rows), 0)
    slot_gate = jnp.concatenate(
        [
            jnp.sum(
                jnp.where(slot_ref[0, i] == place, prob_ref[0, i], 0.0), axis=-1, keepdims=True
            )
            for i in range(blocks)
        ],
        axis=0,
    )
    back = back_ref[0]
    sig = jax.nn.sigmoid(a)
    swish = a * sig
    active = swish * b
    gate_grad = jnp.sum(active * back, axis=-1, keepdims=True)
    for i in range(blocks):
        part = gate_grad[i * SLOTS : (i + 1) * SLOTS, :]
        pg_ref[0, i] = jnp.sum(
            jnp.where(slot_ref[0, i] == place, part, 0.0), axis=0, keepdims=True
        )
    gated = back * slot_gate
    ga_ref[0] = (active * slot_gate).astype(BF)
    dg = (gated * b * (sig + swish * (1.0 - sig))).astype(BF)
    du = (gated * swish).astype(BF)
    dg_ref[0] = dg
    du_ref[0] = du
    d_ref[:, :wide] = dg
    d_ref[:, wide:] = du
    dx_ref[...] = mm(d_ref[...], w_ref[...], 1, 0).astype(BF).reshape(dx_ref.shape)


def expert_step(rows, gate_t, up_t, back, slot, probs):
    experts, blocks, slots, width = rows.shape
    ff = gate_t.shape[1]
    wide = back.shape[2]
    count = blocks * slots
    whole = pl.BlockSpec((1, blocks, slots, width), lambda e: (e, 0, 0, 0))
    flat = lambda n: pl.BlockSpec((1, count, n), lambda e: (e, 0, 0))
    shape = lambda n, dtype: jax.ShapeDtypeStruct((experts, count, n), dtype)
    weight = pl.BlockSpec((1, ff, width), lambda e: (e, 0, 0))
    by_token = pl.BlockSpec((1,) + slot.shape[1:], lambda e: (e, 0, 0, 0))
    return pl.pallas_call(
        expert_kernel,
        name="expert_step",
        grid=(experts,),
        in_specs=[whole, weight, weight, flat(wide), by_token, by_token],
        out_specs=[flat(wide), flat(wide), flat(wide), whole, by_token],
        out_shape=[
            shape(wide, BF),
            shape(wide, BF),
            shape(wide, BF),
            jax.ShapeDtypeStruct(rows.shape, BF),
            jax.ShapeDtypeStruct(slot.shape, F32),
        ],
        scratch_shapes=[pltpu.VMEM((2 * wide, width), BF), pltpu.VMEM((count, 2 * wide), BF)],
        compiler_params=pltpu.CompilerParams(vmem_limit_bytes=VMEM_BYTES),
        cost_estimate=cost(
            8 * experts * count * width * wide,
            2 * experts * (2 * count * width + 2 * width * wide + 5 * count * wide),
            experts * count * wide,
        ),
    )(rows, gate_t, up_t, back, slot, probs)


def dot(eq, a, b):
    return jnp.einsum(eq, a, b, preferred_element_type=F32)


def passed_along(shard, axis, by):
    peers = lax.axis_size(axis)
    pairs = [(i, i + by) for i in range(peers) if 0 <= i + by < peers]
    return lax.ppermute(shard, axis, pairs)


def normed(values, norm_gain):
    return (
        values * lax.rsqrt(jnp.mean(values * values, axis=-1, keepdims=True) + epsilon) * norm_gain
    )


def norm_backward(values, norm_gain, upstream):
    _, pullback = jax.vjp(normed, values, norm_gain)
    return pullback(upstream)


def rotate(values, cosine, sine):
    half = values.shape[-1] // 2
    front, back = values[..., :half], values[..., half:]
    return jnp.concatenate([front * cosine - back * sine, back * cosine + front * sine], axis=-1)


def rotate_back(upstream, cosine, sine):
    return rotate(upstream, cosine, -sine)


def silu_gate(gate_val, up_val):
    return gate_val * jax.nn.sigmoid(gate_val) * up_val


def silu_backward(gate_val, up_val, upstream):
    _, pullback = jax.vjp(silu_gate, gate_val, up_val)
    return pullback(upstream)


def rope_tables(seq_all, seq_here, index_here):
    starts = jnp.sum((seq_all[None, :] < seq_here[:, None]).astype(jnp.int32), axis=1)
    position = (index_here - starts).astype(F32)
    frequency = 10000.0 ** (-(jnp.arange(DR // 2, dtype=F32) * 2.0) / DR)
    angle = position[:, None] * frequency[None, :]
    return jnp.cos(angle), jnp.sin(angle)


def after(value, *others):
    return lax.optimization_barrier((value,) + others)[0]


def scatter_sum(parts):
    joined = parts if not isinstance(parts, list) else jnp.concatenate(parts, axis=1)
    return lax.psum_scatter(joined, "dp", scatter_dimension=0, tiled=True)


def shards(
    tokens,
    seq_ids,
    route_ids,
    cotangent,
    input_gain,
    w_query,
    w_latent,
    latent_gain,
    w_expand,
    w_out,
    middle_gain,
    w_router,
    expert_gate,
    expert_up,
    expert_down,
    shared_gate,
    shared_up,
    shared_down,
):
    devices = lax.axis_size("dp")
    rank_dp = lax.axis_index("dp")
    tok_rows, width = tokens.shape
    experts_local = expert_gate.shape[0]
    all_experts = w_router.shape[1]
    ff_local = expert_gate.shape[2]
    heads_local = w_query.shape[1] // (DN + DR)
    reach = min(REACH, devices - 1)
    window = (reach + 1) * tok_rows

    cot_all = lax.all_gather(cotangent, "dp", tiled=True)
    route_all = lax.all_gather(route_ids, "dp", tiled=True)

    index_here = rank_dp * tok_rows + jnp.arange(tok_rows, dtype=jnp.int32)
    seq_here = lax.dynamic_slice_in_dim(seq_ids, rank_dp * tok_rows, tok_rows, 0)
    cosine, sine = rope_tables(seq_ids, seq_here, index_here)
    key_index = (rank_dp - reach) * tok_rows + jnp.arange(window, dtype=jnp.int32)
    seq_padded = jnp.concatenate([jnp.full((reach * tok_rows,), -1, jnp.int32), seq_ids])
    seq_keys = lax.dynamic_slice_in_dim(seq_padded, rank_dp * tok_rows, window, 0)
    place_q = jnp.stack([seq_here, index_here], axis=1)
    place_k = jnp.stack([seq_keys, key_index], axis=0)

    token_features = tokens.astype(F32)
    grad_output = cotangent.astype(F32)
    hidden_in = normed(token_features, input_gain).astype(BF)
    latent_full = jnp.dot(hidden_in, w_latent, preferred_element_type=F32)
    latent_raw = latent_full[:, :KVR]
    latent = normed(latent_raw, latent_gain).astype(BF)
    rope_key = rotate(latent_full[:, KVR:], cosine, sine).astype(BF)
    own_keys = jnp.concatenate([latent, rope_key], axis=1)
    earlier = [passed_along(own_keys, "dp", back) for back in range(reach, 0, -1)]
    keys_window = jnp.concatenate(earlier + [own_keys], axis=0)
    latent_window = keys_window[:, :KVR]
    rope_window = keys_window[:, KVR:]
    query_pre = jnp.dot(hidden_in, w_query, preferred_element_type=F32).reshape(
        tok_rows, heads_local, DN + DR
    )
    queries = (
        jnp.concatenate(
            [
                query_pre[..., :DN],
                rotate(query_pre[..., DN:], cosine[:, None, :], sine[:, None, :]),
            ],
            axis=-1,
        )
        .astype(BF)
        .transpose(1, 0, 2)
    )
    expanded = jnp.dot(latent_window, w_expand, preferred_element_type=F32).astype(BF)
    attended, lse = attend(queries, expanded, rope_window, place_q, place_k)
    attention = lax.psum(
        jnp.dot(attended, w_out, preferred_element_type=F32).astype(BF), "tensor"
    )
    attention = after(attention, cot_all)
    middle = token_features + attention.astype(F32)
    hidden_mid = normed(middle, middle_gain).astype(BF)
    hidden_all = lax.all_gather(hidden_mid, "dp", tiled=True)

    local_ids = rank_dp * experts_local + jnp.arange(experts_local, dtype=jnp.int32)
    named = jnp.any(route_all[:, :, None] == local_ids[None, None, :], axis=1)
    named_block = named.reshape(devices, tok_rows, experts_local)
    before = jnp.tril(jnp.ones((tok_rows, tok_rows), BF), -1)
    rank_within = dot("ts,bse->bte", before, named_block.astype(BF))
    slot_of = jnp.where(named_block, rank_within, -1.0)
    slot = slot_of.astype(jnp.int32).transpose(2, 0, 1)[:, :, None, :]
    columns = jnp.arange(experts_local * SLOTS, dtype=jnp.int32)
    spread = (columns[None, :] // SLOTS == jnp.arange(experts_local, dtype=jnp.int32)[:, None]).astype(
        BF
    )
    places = (
        dot("bte,en->btn", slot_of.astype(BF), spread) == (columns % SLOTS).astype(F32)
    ).astype(BF)
    gate_t = expert_gate.swapaxes(1, 2)
    up_t = expert_up.swapaxes(1, 2)
    cot_rows = pick(slot, cot_all)
    back = down_back(cot_rows, expert_down)

    shared_gate_val = jnp.dot(hidden_mid, shared_gate, preferred_element_type=F32)
    shared_up_val = jnp.dot(hidden_mid, shared_up, preferred_element_type=F32)
    shared_active = silu_gate(shared_gate_val, shared_up_val).astype(BF)
    shared_result = jnp.dot(shared_active, shared_down, preferred_element_type=F32)
    shared_active_grad = dot("td,fd->tf", cotangent, shared_down)
    shared_gate_grad, shared_up_grad = silu_backward(
        shared_gate_val, shared_up_val, shared_active_grad
    )
    shared_gate_grad = shared_gate_grad.astype(BF)
    shared_up_grad = shared_up_grad.astype(BF)
    mid_from_shared = dot("tf,df->td", shared_gate_grad, shared_gate) + dot(
        "tf,df->td", shared_up_grad, shared_up
    )
    shared_grads = jnp.concatenate(
        [
            dot("td,tf->df", cotangent, shared_active).astype(BF),
            dot("td,tf->df", hidden_mid, shared_gate_grad).astype(BF),
            dot("td,tf->df", hidden_mid, shared_up_grad).astype(BF),
        ],
        axis=1,
    )

    hidden_all = after(hidden_all, back, shared_grads)
    logits = jnp.dot(hidden_all, w_router, preferred_element_type=F32)
    router_probs = jax.nn.softmax(logits, axis=-1)
    local_probs = (
        lax.dynamic_slice_in_dim(router_probs, rank_dp * experts_local, experts_local, 1)
        .reshape(devices, tok_rows, experts_local)
        .transpose(2, 0, 1)[:, :, None, :]
    )
    rows = pick(slot, hidden_all)
    shared_sums = scatter_sum(shared_grads)
    gated_active, gate_val_grad, up_val_grad, row_grad, probs_grad = expert_step(
        rows, gate_t, up_t, back, slot, local_probs
    )
    probs_grad = lax.dynamic_update_slice_in_dim(
        jnp.zeros_like(router_probs),
        probs_grad[:, :, 0, :].transpose(1, 2, 0).reshape(-1, experts_local),
        rank_dp * experts_local,
        1,
    )
    logit_grad = (
        router_probs * (probs_grad - jnp.sum(router_probs * probs_grad, axis=-1, keepdims=True))
    ).astype(BF)
    lanes = -(-all_experts // 128) * 128 - all_experts
    mid_part = put(
        places,
        row_grad,
        (jnp.pad(logit_grad, ((0, 0), (0, lanes))), jnp.pad(w_router.T, ((0, lanes), (0, 0)))),
    )
    mid_part = after(mid_part, shared_sums)
    mid_block = lax.psum_scatter(mid_part, "dp", scatter_dimension=0, tiled=True)
    grad_router = dot("td,te->de", hidden_all, logit_grad).astype(BF)
    routed_part = put(places, row_out(gated_active, expert_down, devices))
    rows_flat = rows.reshape(experts_local, -1, width)
    grad_expert_down = dot(
        "ecf,ecd->efd",
        gated_active[..., :ff_local],
        cot_rows.reshape(experts_local, -1, width),
    )
    grad_expert_gate = dot("ecd,ecf->edf", rows_flat, gate_val_grad[..., :ff_local])
    grad_expert_up = dot("ecd,ecf->edf", rows_flat, up_val_grad[..., :ff_local])

    routed_block = scatter_sum(after(routed_part, mid_block))
    mid_block = after(
        mid_block, routed_part, grad_router, grad_expert_down, grad_expert_gate, grad_expert_up
    )
    mid_grad = lax.psum((mid_block.astype(F32) + mid_from_shared).astype(BF), "tensor")
    routed_block = after(routed_block, mid_grad)
    mid_grad = mid_grad.astype(F32)

    middle_from_norm, grad_middle_gain = norm_backward(middle, middle_gain, mid_grad)
    middle_grad = grad_output + middle_from_norm
    middle_low = middle_grad.astype(BF)
    attended_grad = dot("td,cd->tc", middle_low, w_out).astype(BF)
    query_back, expanded_grad, rope_window_grad = attend_back(
        queries, expanded, rope_window, place_q, place_k, lse, attended_grad
    )
    ff_part = (routed_block.astype(F32) + shared_result).astype(BF)
    expanded_grad = after(expanded_grad, ff_part)
    window_grad = jnp.concatenate(
        [dot("wc,kc->wk", expanded_grad, w_expand), rope_window_grad], axis=1
    )
    keys_grad = window_grad[reach * tok_rows :]
    for step in range(reach, 0, -1):
        start = (reach - step) * tok_rows
        piece = window_grad[start : start + tok_rows].astype(BF)
        keys_grad = keys_grad + passed_along(piece, "dp", -step).astype(F32)
    query_back = query_back.transpose(1, 0, 2)
    query_grad = (
        jnp.concatenate(
            [
                query_back[..., :DN],
                rotate_back(query_back[..., DN:], cosine[:, None, :], sine[:, None, :]),
            ],
            axis=-1,
        )
        .astype(BF)
        .reshape(tok_rows, heads_local * (DN + DR))
    )
    latent_raw_grad, grad_latent_gain = norm_backward(latent_raw, latent_gain, keys_grad[:, :KVR])
    rope_raw_grad = rotate_back(keys_grad[:, KVR:], cosine, sine)
    latent_full_grad = jnp.concatenate([latent_raw_grad, rope_raw_grad], axis=-1).astype(BF)
    input_part = dot("tc,dc->td", query_grad, w_query) + dot(
        "tc,dc->td", latent_full_grad, w_latent
    )
    _, grad_input_gain = norm_backward(token_features, input_gain, input_part)

    feedforward = lax.psum(ff_part, "tensor")
    output = (middle + feedforward.astype(F32)).astype(BF)
    input_part, grad_input_gain = lax.optimization_barrier((input_part.astype(BF), grad_input_gain))
    input_part = after(input_part, feedforward)
    input_grad = lax.psum(input_part, "tensor").astype(F32)
    token_from_norm, _ = norm_backward(token_features, input_gain, input_grad)
    token_grad = (middle_grad + token_from_norm).astype(BF)

    gains = jnp.concatenate(
        [
            grad_middle_gain[None, :],
            grad_input_gain[None, :],
            jnp.repeat(grad_latent_gain, width // KVR)[None, :],
            jnp.zeros((125, width), F32),
        ],
        axis=0,
    )
    query_width = heads_local * (DN + DR)
    out_width = heads_local * DV
    expand_width = w_expand.shape[1] * KVR // width
    latent_width = KVR + DR
    sums = scatter_sum(
        [
            dot("td,tc->dc", middle_low, attended).astype(BF),
            dot("td,tc->dc", hidden_in, query_grad).astype(BF),
            dot("wk,wc->kc", latent_window, expanded_grad).astype(BF).reshape(width, expand_width),
            dot("td,tc->dc", hidden_in, latent_full_grad).astype(BF),
            grad_router,
            gains.astype(BF).T,
        ]
    )
    at = out_width + query_width + expand_width
    grad_out_proj = sums[:, :out_width].astype(F32).T
    grad_query = sums[:, out_width : out_width + query_width].astype(F32)
    grad_expand = sums[:, out_width + query_width : at].astype(F32).reshape(KVR // devices, -1)
    gain_at = at + latent_width + all_experts
    grad_middle_gain = sums[:, gain_at].astype(F32)
    partial_sums = lax.psum(sums[:, at : gain_at + 3].astype(F32), "tensor")
    shared_sums = shared_sums.astype(F32)
    sw = shared_gate.shape[1]
    return (
        output,
        token_grad,
        partial_sums[:, -2],
        grad_query,
        partial_sums[:, :latent_width],
        partial_sums[:: width // KVR, -1],
        grad_expand,
        grad_out_proj,
        grad_middle_gain,
        partial_sums[:, latent_width : latent_width + all_experts],
        grad_expert_gate,
        grad_expert_up,
        grad_expert_down,
        shared_sums[:, sw : 2 * sw],
        shared_sums[:, 2 * sw :],
        shared_sums[:, :sw].T,
    )


def solution(mesh):
    placed = (
        P("dp", None),
        P(),
        P("dp", None),
        P("dp", None),
        P(),
        P(None, "tensor"),
        P(),
        P(),
        P(None, "tensor"),
        P("tensor", None),
        P(),
        P(),
        P("dp", None, "tensor"),
        P("dp", None, "tensor"),
        P("dp", "tensor", None),
        P(None, "tensor"),
        P(None, "tensor"),
        P("tensor", None),
    )
    return jax.shard_map(
        shards,
        mesh=mesh,
        in_specs=placed,
        out_specs=(
            P("dp", None),
            P("dp", None),
            P("dp"),
            P("dp", "tensor"),
            P("dp", None),
            P("dp"),
            P("dp", "tensor"),
            P("tensor", "dp"),
            P("dp"),
            P("dp", None),
            P("dp", None, "tensor"),
            P("dp", None, "tensor"),
            P("dp", "tensor", None),
            P("dp", "tensor"),
            P("dp", "tensor"),
            P("tensor", "dp"),
        ),
        check_vma=False,
    )
```

```python
import functools

import jax
import jax.numpy as jnp
from jax import lax
from jax.experimental import pallas as pl
from jax.experimental.pallas import tpu as pltpu
from jax.sharding import PartitionSpec as P

DN = 128
DR = 64
DV = 128
KVR = 512
REACH = 4
SLOTS = 80
BF = jnp.bfloat16
F32 = jnp.float32
VMEM_BYTES = 60 * 1024 * 1024
epsilon = 1e-06


def mm(a, b, ca, cb):
    return lax.dot_general(a, b, (((ca,), (cb,)), ((), ())), preferred_element_type=F32)


def cost(flops, nbytes, trans=0):
    return pl.CostEstimate(flops=int(flops), bytes_accessed=int(nbytes), transcendentals=int(trans))


def smem():
    return pl.BlockSpec(memory_space=pltpu.SMEM)


def fixed(shape):
    return pl.BlockSpec(shape, lambda *at: (0,) * len(shape))


def params():
    return pltpu.CompilerParams(vmem_limit_bytes=VMEM_BYTES)


def attend_setup(
    head, heads, step, qp_ref, cos_ref, sin_ref, wx_ref, sq_ref, sk_ref, keys,
    q_ref, key_ref, v_ref, bias_ref,
):
    rows = qp_ref.shape[0]

    @pl.when(head == 0)
    def _():
        for at in range(0, rows, step):
            part = pl.ds(at, step)
            allowed = (sq_ref[part, 0:1] == sk_ref[0:1, :]) & (
                sk_ref[1:2, :] <= sq_ref[part, 1:2]
            )
            bias_ref[part, :] = jnp.where(allowed, 0.0, -1e30).astype(BF)
        for i, key in enumerate(keys):
            key_ref[i * rows : (i + 1) * rows, DN:] = key[:, KVR : KVR + DR]

    for k in range(heads):

        @pl.when(head == k)
        def _():
            at = k * (DN + DR)
            front = qp_ref[:, at + DN : at + DN + DR // 2]
            back = qp_ref[:, at + DN + DR // 2 : at + DN + DR]
            cosine, sine = cos_ref[...], sin_ref[...]
            q_ref[:, :DN] = qp_ref[:, at : at + DN].astype(BF)
            q_ref[:, DN : DN + DR // 2] = (front * cosine - back * sine).astype(BF)
            q_ref[:, DN + DR // 2 :] = (back * cosine + front * sine).astype(BF)

    for i, key in enumerate(keys):
        kv = mm(key[:, :KVR], wx_ref[...], 1, 0).astype(BF)
        key_ref[i * rows : (i + 1) * rows, :DN] = kv[:, :DN]
        v_ref[i * rows : (i + 1) * rows, :] = kv[:, DN:]


def attend_kernel(heads, step, qp_ref, cos_ref, sin_ref, wx_ref, sq_ref, sk_ref, *rest):
    keys, (o_ref, lse_ref, q_ref, key_ref, v_ref, bias_ref) = rest[:-6], rest[-6:]
    rows = qp_ref.shape[0]
    scale = (DN + DR) ** (-0.5)
    attend_setup(
        pl.program_id(0), heads, step, qp_ref, cos_ref, sin_ref, wx_ref, sq_ref, sk_ref, keys,
        q_ref, key_ref, v_ref, bias_ref,
    )
    for at in range(0, rows, step):
        part = pl.ds(at, step)
        s = mm(q_ref[part, :], key_ref[...], 1, 1) * scale + bias_ref[part, :].astype(F32)
        top = jnp.max(s, axis=-1, keepdims=True)
        p = jnp.exp(s - top)
        total = jnp.sum(p, axis=-1, keepdims=True)
        o_ref[part, :] = mm((p * (1.0 / total)).astype(BF), v_ref[...], 1, 0).astype(BF)
        lse_ref[0, part, :] = top + jnp.log(total)


def attend_specs(query_pre, cosine, w_expand, place_q, place_k, keys):
    return [
        fixed(query_pre.shape),
        fixed(cosine.shape),
        fixed(cosine.shape),
        pl.BlockSpec((KVR, DN + DV), lambda h: (0, h)),
        fixed(place_q.shape),
        fixed(place_k.shape),
    ], [fixed(keys[0].shape) for _ in keys]


def attend(query_pre, cosine, sine, w_expand, place_q, place_k, keys):
    rows = query_pre.shape[0]
    heads = query_pre.shape[1] // (DN + DR)
    window = rows * len(keys)
    specs, key_specs = attend_specs(query_pre, cosine, w_expand, place_q, place_k, keys)
    return pl.pallas_call(
        functools.partial(attend_kernel, heads, rows // 2),
        name="attend",
        grid=(heads,),
        in_specs=specs + key_specs,
        out_specs=[
            pl.BlockSpec((rows, DV), lambda h: (0, h)),
            pl.BlockSpec((1, rows, 1), lambda h: (h, 0, 0)),
        ],
        out_shape=[
            jax.ShapeDtypeStruct((rows, heads * DV), BF),
            jax.ShapeDtypeStruct((heads, rows, 1), F32),
        ],
        scratch_shapes=[
            pltpu.VMEM((rows, DN + DR), BF),
            pltpu.VMEM((window, DN + DR), BF),
            pltpu.VMEM((window, DV), BF),
            pltpu.VMEM((rows, window), BF),
        ],
        compiler_params=params(),
        cost_estimate=cost(
            2 * heads * window * (rows * 384 + KVR * 256), 2 * window * 640, heads * rows * window
        ),
    )(query_pre, cosine, sine, w_expand, place_q, place_k, *keys)


def attend_back_kernel(
    heads, step, count, qp_ref, cos_ref, sin_ref, wx_ref, sq_ref, sk_ref, lse_ref, do_ref, *rest
):
    keys, rest = rest[:count], rest[count:]
    dq_ref, gx_ref = rest[:2]
    grads = rest[2 : 2 + count]
    q_ref, key_ref, v_ref, bias_ref, dk_ref, dv_ref, dkv_ref, acc_ref, dqs_ref = rest[2 + count :]
    rows = qp_ref.shape[0]
    head = pl.program_id(0)
    scale = (DN + DR) ** (-0.5)
    attend_setup(
        head, heads, step, qp_ref, cos_ref, sin_ref, wx_ref, sq_ref, sk_ref, keys,
        q_ref, key_ref, v_ref, bias_ref,
    )

    @pl.when(head == 0)
    def _():
        acc_ref[...] = jnp.zeros_like(acc_ref)

    for at in range(0, rows, step):
        part = pl.ds(at, step)
        q = q_ref[part, :]
        do = do_ref[part, :]
        s = mm(q, key_ref[...], 1, 1) * scale + bias_ref[part, :].astype(F32)
        p = jnp.exp(s - lse_ref[0, part, :])
        dp = mm(do, v_ref[...], 1, 1)
        ds = (p * (dp - jnp.sum(p * dp, axis=-1, keepdims=True))).astype(BF)
        dqs_ref[part, :] = mm(ds, key_ref[...], 1, 0) * scale
        dk = mm(ds, q, 0, 0) * scale
        dv = mm(p.astype(BF), do, 0, 0)
        if at == 0:
            dk_ref[...] = dk
            dv_ref[...] = dv
        else:
            dk_ref[...] += dk
            dv_ref[...] += dv
    dkv_ref[:, :DN] = dk_ref[:, :DN].astype(BF)
    dkv_ref[:, DN:] = dv_ref[...].astype(BF)
    acc_ref[:, :KVR] += mm(dkv_ref[...], wx_ref[...], 1, 1)
    acc_ref[:, KVR : KVR + DR] += dk_ref[:, DN:]
    expand_grad = jnp.zeros((KVR, DN + DV), F32)
    for i, key in enumerate(keys):
        expand_grad += mm(key[:, :KVR], dkv_ref[i * rows : (i + 1) * rows, :], 0, 0)
    gx_ref[...] = expand_grad.astype(BF)
    for k in range(heads):

        @pl.when(head == k)
        def _():
            at = k * (DN + DR)
            front = dqs_ref[:, DN : DN + DR // 2]
            back = dqs_ref[:, DN + DR // 2 :]
            cosine, sine = cos_ref[...], sin_ref[...]
            dq_ref[:, at : at + DN] = dqs_ref[:, :DN].astype(BF)
            dq_ref[:, at + DN : at + DN + DR // 2] = (front * cosine + back * sine).astype(BF)
            dq_ref[:, at + DN + DR // 2 : at + DN + DR] = (back * cosine - front * sine).astype(BF)

    @pl.when(head == heads - 1)
    def _():
        for i, grad in enumerate(grads):
            grad[...] = acc_ref[i * rows : (i + 1) * rows, :].astype(grad.dtype)


def attend_back(query_pre, cosine, sine, w_expand, place_q, place_k, lse, attended_grad, keys):
    rows = query_pre.shape[0]
    heads = query_pre.shape[1] // (DN + DR)
    window = rows * len(keys)
    count = len(keys)
    specs, key_specs = attend_specs(query_pre, cosine, w_expand, place_q, place_k, keys)
    wide = keys[0].shape[1]
    return pl.pallas_call(
        functools.partial(attend_back_kernel, heads, rows // 2, count),
        name="attend_back",
        grid=(heads,),
        in_specs=specs
        + [
            pl.BlockSpec((1, rows, 1), lambda h: (h, 0, 0)),
            pl.BlockSpec((rows, DV), lambda h: (0, h)),
        ]
        + key_specs,
        out_specs=[fixed(query_pre.shape), pl.BlockSpec((KVR, DN + DV), lambda h: (0, h))]
        + [fixed((rows, wide)) for _ in keys],
        out_shape=[
            jax.ShapeDtypeStruct(query_pre.shape, BF),
            jax.ShapeDtypeStruct(w_expand.shape, BF),
        ]
        + [jax.ShapeDtypeStruct((rows, wide), BF) for _ in keys[1:]]
        + [jax.ShapeDtypeStruct((rows, wide), F32)],
        scratch_shapes=[
            pltpu.VMEM((rows, DN + DR), BF),
            pltpu.VMEM((window, DN + DR), BF),
            pltpu.VMEM((window, DV), BF),
            pltpu.VMEM((rows, window), BF),
            pltpu.VMEM((window, DN + DR), F32),
            pltpu.VMEM((window, DV), F32),
            pltpu.VMEM((window, DN + DV), BF),
            pltpu.VMEM((window, wide), F32),
            pltpu.VMEM((rows, DN + DR), F32),
        ],
        compiler_params=params(),
        cost_estimate=cost(
            2 * heads * window * (rows * 1024 + KVR * 768), 4 * window * 640, heads * rows * window
        ),
    )(query_pre, cosine, sine, w_expand, place_q, place_k, lse, attended_grad, *keys)


def one_hot(slot_ref):
    experts, rows = slot_ref.shape[0], slot_ref.shape[-1]
    place = lax.broadcasted_iota(jnp.int32, (SLOTS, rows), 0)
    return jnp.concatenate(
        [(slot_ref[e, 0] == place).astype(F32).astype(BF) for e in range(experts)], axis=0
    )


def pick_kernel(slot_ref, x_ref, o_ref):
    o_ref[...] = mm(one_hot(slot_ref), x_ref[...], 1, 0).astype(BF).reshape(o_ref.shape)


def pick_route_kernel(count, first_ref, slot_ref, x_ref, w_ref, o_ref, p_ref, g_ref):
    x = x_ref[...]
    logits = mm(x, w_ref[...], 1, 1)
    lane = lax.broadcasted_iota(jnp.int32, logits.shape, 1)
    logits = jnp.where(lane < count, logits, -1e30)
    e = jnp.exp(logits - jnp.max(logits, axis=-1, keepdims=True))
    probs = e / jnp.sum(e, axis=-1, keepdims=True)
    p_ref[...] = probs
    high = probs.astype(BF)
    low = (probs - high.astype(F32)).astype(BF)
    chosen = one_hot(slot_ref)
    o_ref[...] = mm(chosen, x, 1, 0).astype(BF).reshape(o_ref.shape)
    taken = mm(chosen, high, 1, 0) + mm(chosen, low, 1, 0)
    lane = lax.broadcasted_iota(jnp.int32, (SLOTS, taken.shape[1]), 1)
    for i in range(slot_ref.shape[0]):
        part = taken[i * SLOTS : (i + 1) * SLOTS, :]
        g_ref[i, 0] = jnp.sum(
            jnp.where(lane == first_ref[0] + i, part, 0.0), axis=-1, keepdims=True
        )


def pick(slot, values):
    experts, blocks, _, rows = slot.shape
    width = values.shape[1]
    return pl.pallas_call(
        pick_kernel,
        name="pick",
        grid=(blocks,),
        in_specs=[
            pl.BlockSpec((experts, 1, 1, rows), lambda b: (0, b, 0, 0)),
            pl.BlockSpec((rows, width), lambda b: (b, 0)),
        ],
        out_specs=pl.BlockSpec((experts, 1, SLOTS, width), lambda b: (0, b, 0, 0)),
        out_shape=jax.ShapeDtypeStruct((experts, blocks, SLOTS, width), BF),
        compiler_params=params(),
        cost_estimate=cost(
            2 * experts * blocks * SLOTS * rows * width,
            2 * blocks * width * (rows + experts * SLOTS),
        ),
    )(slot, values)


def pick_route(first, slot, values, router_rows, count):
    experts, blocks, _, rows = slot.shape
    width = values.shape[1]
    lanes = router_rows.shape[0]
    return pl.pallas_call(
        functools.partial(pick_route_kernel, count),
        name="pick_route",
        grid=(blocks,),
        in_specs=[
            smem(),
            pl.BlockSpec((experts, 1, 1, rows), lambda b: (0, b, 0, 0)),
            pl.BlockSpec((rows, width), lambda b: (b, 0)),
            fixed(router_rows.shape),
        ],
        out_specs=[
            pl.BlockSpec((experts, 1, SLOTS, width), lambda b: (0, b, 0, 0)),
            pl.BlockSpec((rows, lanes), lambda b: (b, 0)),
            pl.BlockSpec((experts, 1, SLOTS, 1), lambda b: (0, b, 0, 0)),
        ],
        out_shape=[
            jax.ShapeDtypeStruct((experts, blocks, SLOTS, width), BF),
            jax.ShapeDtypeStruct((blocks * rows, lanes), F32),
            jax.ShapeDtypeStruct((experts, blocks, SLOTS, 1), F32),
        ],
        compiler_params=params(),
        cost_estimate=cost(
            2 * experts * blocks * SLOTS * rows * width,
            2 * blocks * width * (rows + experts * SLOTS),
        ),
    )(first, slot, values, router_rows)


def put_kernel(place_ref, r_ref, o_ref):
    o_ref[...] = mm(place_ref[0], r_ref[...].reshape(-1, r_ref.shape[-1]), 1, 0).astype(BF)


def put_route_kernel(first_ref, place_ref, r_ref, p_ref, pg_ref, w_ref, o_ref, lg_ref):
    experts, rows = pg_ref.shape[0], pg_ref.shape[3]
    by_expert = jnp.concatenate(
        [pg_ref[i, 0] for i in range(experts)] + [jnp.zeros((1, rows), F32)] * (-experts % 8), axis=0
    )
    high = by_expert.astype(BF)
    low = (by_expert - high.astype(F32)).astype(BF)
    probs = p_ref[...]
    shape = (by_expert.shape[0], probs.shape[1])
    expert = lax.broadcasted_iota(jnp.int32, shape, 0)
    lane = lax.broadcasted_iota(jnp.int32, shape, 1)
    spread = (lane == first_ref[0] + expert) & (expert < experts)
    spread = spread.astype(F32).astype(BF)
    grad = mm(high, spread, 0, 0) + mm(low, spread, 0, 0)
    back = (probs * (grad - jnp.sum(probs * grad, axis=-1, keepdims=True))).astype(BF)
    lg_ref[...] = back
    total = mm(place_ref[0], r_ref[...].reshape(-1, r_ref.shape[-1]), 1, 0)
    o_ref[...] = (total + mm(back, w_ref[...], 1, 0)).astype(BF)


def put_specs(places, picked):
    blocks, rows, slots = places.shape
    experts, width = picked.shape[0], picked.shape[3]
    return [
        pl.BlockSpec((1, rows, slots), lambda b: (b, 0, 0)),
        pl.BlockSpec((experts, 1, SLOTS, width), lambda b: (0, b, 0, 0)),
    ]


def put_cost(places, width):
    blocks, rows, slots = places.shape
    return cost(2 * blocks * slots * rows * width, 2 * blocks * width * (rows + slots))


def put(places, picked):
    blocks, rows, _ = places.shape
    width = picked.shape[3]
    return pl.pallas_call(
        put_kernel,
        name="put",
        grid=(blocks,),
        in_specs=put_specs(places, picked),
        out_specs=pl.BlockSpec((rows, width), lambda b: (b, 0)),
        out_shape=jax.ShapeDtypeStruct((blocks * rows, width), BF),
        compiler_params=params(),
        cost_estimate=put_cost(places, width),
    )(places, picked)


def put_route(first, places, picked, probs, probs_grad, router_rows):
    blocks, rows, _ = places.shape
    experts, width = picked.shape[0], picked.shape[3]
    lanes = probs.shape[1]
    return pl.pallas_call(
        put_route_kernel,
        name="put_route",
        grid=(blocks,),
        in_specs=[smem()]
        + put_specs(places, picked)
        + [
            pl.BlockSpec((rows, lanes), lambda b: (b, 0)),
            pl.BlockSpec((experts, 1, 1, rows), lambda b: (0, b, 0, 0)),
            fixed(router_rows.shape),
        ],
        out_specs=[
            pl.BlockSpec((rows, width), lambda b: (b, 0)),
            pl.BlockSpec((rows, lanes), lambda b: (b, 0)),
        ],
        out_shape=[
            jax.ShapeDtypeStruct((blocks * rows, width), BF),
            jax.ShapeDtypeStruct((blocks * rows, lanes), BF),
        ],
        compiler_params=params(),
        cost_estimate=put_cost(places, width),
    )(first, places, picked, probs, probs_grad, router_rows)


def down_back_kernel(x_ref, w_ref, o_ref):
    ff = w_ref.shape[1]
    wide = o_ref.shape[-1]
    back = mm(x_ref[...].reshape(-1, x_ref.shape[-1]), w_ref[0], 1, 1)
    o_ref[0, :, :ff] = back
    if wide > ff:
        o_ref[0, :, ff:] = jnp.zeros((o_ref.shape[1], wide - ff), F32)


def down_back(rows, down):
    experts, blocks, slots, width = rows.shape
    ff = down.shape[1]
    wide = -(-ff // 128) * 128
    count = blocks * slots
    return pl.pallas_call(
        down_back_kernel,
        name="down_back",
        grid=(experts,),
        in_specs=[
            pl.BlockSpec((1, blocks, slots, width), lambda e: (e, 0, 0, 0)),
            pl.BlockSpec((1, ff, width), lambda e: (e, 0, 0)),
        ],
        out_specs=pl.BlockSpec((1, count, wide), lambda e: (e, 0, 0)),
        out_shape=jax.ShapeDtypeStruct((experts, count, wide), F32),
        compiler_params=params(),
        cost_estimate=cost(
            2 * experts * count * width * ff,
            experts * (2 * count * width + 2 * ff * width + 4 * count * wide),
        ),
    )(rows, down)


def row_out_kernel(x_ref, w_ref, o_ref):
    ff = w_ref.shape[1]
    o_ref[...] = mm(x_ref[0, :, :ff], w_ref[0], 1, 0).astype(BF).reshape(o_ref.shape)


def row_out(active, down, blocks):
    experts, count, wide = active.shape
    ff, width = down.shape[1:]
    slots = count // blocks
    return pl.pallas_call(
        row_out_kernel,
        name="row_out",
        grid=(experts,),
        in_specs=[
            pl.BlockSpec((1, count, wide), lambda e: (e, 0, 0)),
            pl.BlockSpec((1, ff, width), lambda e: (e, 0, 0)),
        ],
        out_specs=pl.BlockSpec((1, blocks, slots, width), lambda e: (e, 0, 0, 0)),
        out_shape=jax.ShapeDtypeStruct((experts, blocks, slots, width), BF),
        compiler_params=params(),
        cost_estimate=cost(
            2 * experts * count * width * ff,
            2 * experts * (count * width + ff * width + count * wide),
        ),
    )(active, down)


def expert_kernel(
    x_ref, gate_ref, up_ref, back_ref, slot_ref, sg_ref,
    ga_ref, dg_ref, du_ref, dx_ref, pg_ref, w_ref, d_ref,
):
    ff = gate_ref.shape[1]
    wide = back_ref.shape[2]
    blocks, rows = slot_ref.shape[1], slot_ref.shape[3]

    @pl.when(pl.program_id(0) == 0)
    def _():
        w_ref[...] = jnp.zeros_like(w_ref)

    w_ref[:ff, :] = gate_ref[0]
    w_ref[wide : wide + ff, :] = up_ref[0]
    x = x_ref[...].reshape(-1, x_ref.shape[-1])
    both = mm(x, w_ref[...], 1, 1)
    a = both[:, :wide]
    b = both[:, wide:]
    place = lax.broadcasted_iota(jnp.int32, (SLOTS, rows), 0)
    slot_gate = sg_ref[...].reshape(-1, 1)
    back = back_ref[0]
    sig = jax.nn.sigmoid(a)
    swish = a * sig
    active = swish * b
    gate_grad = jnp.sum(active * back, axis=-1, keepdims=True)
    for i in range(blocks):
        part = gate_grad[i * SLOTS : (i + 1) * SLOTS, :]
        pg_ref[0, i] = jnp.sum(
            jnp.where(slot_ref[0, i] == place, part, 0.0), axis=0, keepdims=True
        )
    gated = back * slot_gate
    ga_ref[0] = (active * slot_gate).astype(BF)
    dg = (gated * b * (sig + swish * (1.0 - sig))).astype(BF)
    du = (gated * swish).astype(BF)
    dg_ref[0] = dg
    du_ref[0] = du
    d_ref[:, :wide] = dg
    d_ref[:, wide:] = du
    dx_ref[...] = mm(d_ref[...], w_ref[...], 1, 0).astype(BF).reshape(dx_ref.shape)


def expert_step(rows, gate_t, up_t, back, slot, slot_gates):
    experts, blocks, slots, width = rows.shape
    ff = gate_t.shape[1]
    wide = back.shape[2]
    count = blocks * slots
    whole = pl.BlockSpec((1, blocks, slots, width), lambda e: (e, 0, 0, 0))
    flat = lambda n: pl.BlockSpec((1, count, n), lambda e: (e, 0, 0))
    shape = lambda n, dtype: jax.ShapeDtypeStruct((experts, count, n), dtype)
    weight = pl.BlockSpec((1, ff, width), lambda e: (e, 0, 0))
    by_token = pl.BlockSpec((1,) + slot.shape[1:], lambda e: (e, 0, 0, 0))
    return pl.pallas_call(
        expert_kernel,
        name="expert_step",
        grid=(experts,),
        in_specs=[
            whole,
            weight,
            weight,
            flat(wide),
            by_token,
            pl.BlockSpec((1, blocks, slots, 1), lambda e: (e, 0, 0, 0)),
        ],
        out_specs=[flat(wide), flat(wide), flat(wide), whole, by_token],
        out_shape=[
            shape(wide, BF),
            shape(wide, BF),
            shape(wide, BF),
            jax.ShapeDtypeStruct(rows.shape, BF),
            jax.ShapeDtypeStruct(slot.shape, F32),
        ],
        scratch_shapes=[pltpu.VMEM((2 * wide, width), BF), pltpu.VMEM((count, 2 * wide), BF)],
        compiler_params=params(),
        cost_estimate=cost(
            8 * experts * count * width * wide,
            2 * experts * (2 * count * width + 2 * width * wide + 5 * count * wide),
            experts * count * wide,
        ),
    )(rows, gate_t, up_t, back, slot, slot_gates)


def dot(eq, a, b):
    return jnp.einsum(eq, a, b, preferred_element_type=F32)


def passed_along(shard, axis, by):
    peers = lax.axis_size(axis)
    pairs = [(i, i + by) for i in range(peers) if 0 <= i + by < peers]
    return lax.ppermute(shard, axis, pairs)


def normed(values, norm_gain):
    return (
        values * lax.rsqrt(jnp.mean(values * values, axis=-1, keepdims=True) + epsilon) * norm_gain
    )


def norm_backward(values, norm_gain, upstream):
    _, pullback = jax.vjp(normed, values, norm_gain)
    return pullback(upstream)


def rotate(values, cosine, sine):
    half = values.shape[-1] // 2
    front, back = values[..., :half], values[..., half:]
    return jnp.concatenate([front * cosine - back * sine, back * cosine + front * sine], axis=-1)


def rotate_back(upstream, cosine, sine):
    return rotate(upstream, cosine, -sine)


def silu_gate(gate_val, up_val):
    return gate_val * jax.nn.sigmoid(gate_val) * up_val


def silu_backward(gate_val, up_val, upstream):
    _, pullback = jax.vjp(silu_gate, gate_val, up_val)
    return pullback(upstream)


def rope_tables(seq_all, seq_here, index_here):
    starts = jnp.sum((seq_all[None, :] < seq_here[:, None]).astype(jnp.int32), axis=1)
    position = (index_here - starts).astype(F32)
    frequency = 10000.0 ** (-(jnp.arange(DR // 2, dtype=F32) * 2.0) / DR)
    angle = position[:, None] * frequency[None, :]
    return jnp.cos(angle), jnp.sin(angle)


def after(value, *others):
    return lax.optimization_barrier((value,) + others)[0]


def scatter_sum(parts):
    joined = parts if not isinstance(parts, list) else jnp.concatenate(parts, axis=1)
    return lax.psum_scatter(joined, "dp", scatter_dimension=0, tiled=True)


def tensor_sum(value):
    peers = lax.axis_size("tensor")
    rank = lax.axis_index("tensor")
    rows = value.shape[0] // peers
    piece = lambda at: lax.dynamic_slice_in_dim(value, at * rows, rows, 0)
    turn = lambda piece, by: lax.ppermute(
        piece, "tensor", [(i, (i + by) % peers) for i in range(peers)]
    )
    total = piece(rank).astype(F32)
    for by in range(1, peers):
        total = total + turn(piece((rank + by) % peers), by).astype(F32)
    mine = total.astype(BF)
    out = jnp.zeros(value.shape, F32)
    out = lax.dynamic_update_slice_in_dim(out, total, rank * rows, 0)
    for by in range(1, peers):
        other = turn(mine, by).astype(F32)
        out = lax.dynamic_update_slice_in_dim(out, other, (rank - by) % peers * rows, 0)
    return out


def shards(
    tokens,
    seq_ids,
    route_ids,
    cotangent,
    input_gain,
    w_query,
    w_latent,
    latent_gain,
    w_expand,
    w_out,
    middle_gain,
    w_router,
    expert_gate,
    expert_up,
    expert_down,
    shared_gate,
    shared_up,
    shared_down,
):
    devices = lax.axis_size("dp")
    rank_dp = lax.axis_index("dp")
    tok_rows, width = tokens.shape
    experts_local = expert_gate.shape[0]
    all_experts = w_router.shape[1]
    ff_local = expert_gate.shape[2]
    heads_local = w_query.shape[1] // (DN + DR)
    reach = min(REACH, devices - 1)
    window = (reach + 1) * tok_rows

    cot_all = lax.all_gather(cotangent, "dp", tiled=True)
    route_all = lax.all_gather(route_ids, "dp", tiled=True)

    index_here = rank_dp * tok_rows + jnp.arange(tok_rows, dtype=jnp.int32)
    seq_here = lax.dynamic_slice_in_dim(seq_ids, rank_dp * tok_rows, tok_rows, 0)
    cosine, sine = rope_tables(seq_ids, seq_here, index_here)
    key_index = (rank_dp - reach) * tok_rows + jnp.arange(window, dtype=jnp.int32)
    seq_padded = jnp.concatenate([jnp.full((reach * tok_rows,), -1, jnp.int32), seq_ids])
    seq_keys = lax.dynamic_slice_in_dim(seq_padded, rank_dp * tok_rows, window, 0)
    place_q = jnp.stack([seq_here, index_here], axis=1)
    place_k = jnp.stack([seq_keys, key_index], axis=0)

    token_features = tokens.astype(F32)
    grad_output = cotangent.astype(F32)
    hidden_in = normed(token_features, input_gain).astype(BF)
    latent_full = jnp.dot(hidden_in, w_latent, preferred_element_type=F32)
    latent_raw = latent_full[:, :KVR]
    latent = normed(latent_raw, latent_gain).astype(BF)
    rope_key = rotate(latent_full[:, KVR:], cosine, sine).astype(BF)
    fill = jnp.zeros((tok_rows, -(KVR + DR) % 128), BF)
    own_keys = jnp.concatenate([latent, rope_key, fill], axis=1)
    keys = [passed_along(own_keys, "dp", back) for back in range(reach, 0, -1)] + [own_keys]
    query_pre = jnp.dot(hidden_in, w_query, preferred_element_type=F32)
    attended, lse = attend(query_pre, cosine, sine, w_expand, place_q, place_k, keys)
    attention = lax.psum(
        jnp.dot(attended, w_out, preferred_element_type=F32).astype(BF), "tensor"
    )
    attention = after(attention, cot_all)
    middle = token_features + attention.astype(F32)
    hidden_mid = normed(middle, middle_gain).astype(BF)
    hidden_all = lax.all_gather(hidden_mid, "dp", tiled=True)

    local_ids = rank_dp * experts_local + jnp.arange(experts_local, dtype=jnp.int32)
    named = jnp.any(route_all[:, :, None] == local_ids[None, None, :], axis=1)
    named_block = named.reshape(devices, tok_rows, experts_local)
    before = jnp.tril(jnp.ones((tok_rows, tok_rows), BF), -1)
    rank_within = dot("ts,bse->bte", before, named_block.astype(BF))
    slot_of = jnp.where(named_block, rank_within, -1.0)
    slot = slot_of.astype(jnp.int32).transpose(2, 0, 1)[:, :, None, :]
    columns = jnp.arange(experts_local * SLOTS, dtype=jnp.int32)
    spread = (columns[None, :] // SLOTS == jnp.arange(experts_local, dtype=jnp.int32)[:, None]).astype(
        BF
    )
    places = (
        dot("bte,en->btn", slot_of.astype(BF), spread) == (columns % SLOTS).astype(F32)
    ).astype(BF)
    gate_t = expert_gate.swapaxes(1, 2)
    up_t = expert_up.swapaxes(1, 2)
    cot_rows = pick(slot, cot_all)
    back = down_back(cot_rows, expert_down)

    shared_gate_val = jnp.dot(hidden_mid, shared_gate, preferred_element_type=F32)
    shared_up_val = jnp.dot(hidden_mid, shared_up, preferred_element_type=F32)
    shared_active = silu_gate(shared_gate_val, shared_up_val).astype(BF)
    shared_result = jnp.dot(shared_active, shared_down, preferred_element_type=F32)
    shared_active_grad = dot("td,fd->tf", cotangent, shared_down)
    shared_gate_grad, shared_up_grad = silu_backward(
        shared_gate_val, shared_up_val, shared_active_grad
    )
    shared_gate_grad = shared_gate_grad.astype(BF)
    shared_up_grad = shared_up_grad.astype(BF)
    mid_from_shared = dot("tf,df->td", shared_gate_grad, shared_gate) + dot(
        "tf,df->td", shared_up_grad, shared_up
    )
    shared_grads = jnp.concatenate(
        [
            dot("td,tf->df", cotangent, shared_active).astype(BF),
            dot("td,tf->df", hidden_mid, shared_gate_grad).astype(BF),
            dot("td,tf->df", hidden_mid, shared_up_grad).astype(BF),
        ],
        axis=1,
    )

    hidden_all = after(hidden_all, back, shared_grads)
    first = (rank_dp * experts_local).astype(jnp.int32).reshape(1)
    router_rows = jnp.pad(w_router.T, ((0, -all_experts % 128), (0, 0)))
    rows, router_probs, slot_gates = pick_route(first, slot, hidden_all, router_rows, all_experts)
    shared_sums = scatter_sum(shared_grads)
    gated_active, gate_val_grad, up_val_grad, row_grad, probs_grad = expert_step(
        rows, gate_t, up_t, back, slot, slot_gates
    )
    mid_part, logit_grad = put_route(first, places, row_grad, router_probs, probs_grad, router_rows)
    mid_part = after(mid_part, shared_sums)
    mid_block = lax.psum_scatter(mid_part, "dp", scatter_dimension=0, tiled=True)
    grad_router = dot("td,te->de", hidden_all, logit_grad[:, :all_experts]).astype(BF)
    routed_part = put(places, row_out(gated_active, expert_down, devices))
    rows_flat = rows.reshape(experts_local, -1, width)
    grad_expert_down = dot(
        "ecf,ecd->efd",
        gated_active[..., :ff_local],
        cot_rows.reshape(experts_local, -1, width),
    )
    grad_expert_gate = dot("ecd,ecf->edf", rows_flat, gate_val_grad[..., :ff_local])
    grad_expert_up = dot("ecd,ecf->edf", rows_flat, up_val_grad[..., :ff_local])

    routed_block = scatter_sum(after(routed_part, mid_block))
    mid_block = after(
        mid_block, routed_part, grad_router, grad_expert_down, grad_expert_gate, grad_expert_up
    )
    mid_grad = lax.psum((mid_block.astype(F32) + mid_from_shared).astype(BF), "tensor")
    routed_block = after(routed_block, mid_grad)
    mid_grad = mid_grad.astype(F32)

    middle_from_norm, grad_middle_gain = norm_backward(middle, middle_gain, mid_grad)
    middle_grad = grad_output + middle_from_norm
    middle_low = middle_grad.astype(BF)
    attended_grad = dot("td,cd->tc", middle_low, w_out).astype(BF)
    query_grad, grad_expand, *window_grads = attend_back(
        query_pre, cosine, sine, w_expand, place_q, place_k, lse, attended_grad, keys
    )
    ff_part = (routed_block.astype(F32) + shared_result).astype(BF)
    window_grads = lax.optimization_barrier((*window_grads, ff_part))[:-1]
    keys_grad = window_grads[-1]
    for step in range(reach, 0, -1):
        keys_grad = keys_grad + passed_along(window_grads[reach - step], "dp", -step).astype(F32)
    latent_raw_grad, grad_latent_gain = norm_backward(latent_raw, latent_gain, keys_grad[:, :KVR])
    rope_raw_grad = rotate_back(keys_grad[:, KVR : KVR + DR], cosine, sine)
    latent_full_grad = jnp.concatenate([latent_raw_grad, rope_raw_grad], axis=-1).astype(BF)
    input_part = dot("tc,dc->td", query_grad, w_query) + dot(
        "tc,dc->td", latent_full_grad, w_latent
    )
    _, grad_input_gain = norm_backward(token_features, input_gain, input_part)

    feedforward = lax.psum(ff_part, "tensor")
    output = (middle + feedforward.astype(F32)).astype(BF)
    input_part, grad_input_gain = lax.optimization_barrier((input_part.astype(BF), grad_input_gain))
    input_part = after(input_part, feedforward)
    input_grad = lax.psum(input_part, "tensor").astype(F32)
    tensors = lax.axis_size("tensor")
    query_width = heads_local * (DN + DR)
    out_width = heads_local * DV
    expand_width = w_expand.shape[1] * KVR // width
    latent_width = KVR + DR
    late = scatter_sum(
        [
            dot("td,tc->dc", middle_low, attended).astype(BF),
            dot("td,tc->dc", hidden_in, query_grad).astype(BF),
            grad_expand.reshape(width, expand_width),
        ]
    )
    gains = jnp.concatenate(
        [
            grad_middle_gain[None, :] / tensors,
            grad_input_gain[None, :],
            jnp.repeat(grad_latent_gain, width // KVR)[None, :],
            jnp.zeros((61, width), F32),
        ],
        axis=0,
    )
    parts = scatter_sum(
        [dot("td,tc->dc", hidden_in, latent_full_grad).astype(BF), grad_router, gains.astype(BF).T]
    )
    parts = tensor_sum(parts)
    input_grad = after(input_grad, parts)
    token_from_norm, _ = norm_backward(token_features, input_gain, input_grad)
    token_grad = (middle_grad + token_from_norm).astype(BF)
    sw = shared_gate.shape[1]
    gain_at = latent_width + all_experts
    return (
        output,
        token_grad,
        parts[:, gain_at + 1],
        late[:, out_width : out_width + query_width].astype(F32),
        parts[:, :latent_width],
        parts[:: width // KVR, gain_at + 2],
        late[:, out_width + query_width :].astype(F32).reshape(KVR // devices, -1),
        late[:, :out_width].astype(F32).T,
        parts[:, gain_at],
        parts[:, latent_width:gain_at],
        grad_expert_gate,
        grad_expert_up,
        grad_expert_down,
        shared_sums[:, sw : 2 * sw].astype(F32),
        shared_sums[:, 2 * sw :].astype(F32),
        shared_sums[:, :sw].astype(F32).T,
    )


def solution(mesh):
    placed = (
        P("dp", None),
        P(),
        P("dp", None),
        P("dp", None),
        P(),
        P(None, "tensor"),
        P(),
        P(),
        P(None, "tensor"),
        P("tensor", None),
        P(),
        P(),
        P("dp", None, "tensor"),
        P("dp", None, "tensor"),
        P("dp", "tensor", None),
        P(None, "tensor"),
        P(None, "tensor"),
        P("tensor", None),
    )
    return jax.shard_map(
        shards,
        mesh=mesh,
        in_specs=placed,
        out_specs=(
            P("dp", None),
            P("dp", None),
            P("dp"),
            P("dp", "tensor"),
            P("dp", None),
            P("dp"),
            P("dp", "tensor"),
            P("tensor", "dp"),
            P("dp"),
            P("dp", None),
            P("dp", None, "tensor"),
            P("dp", None, "tensor"),
            P("dp", "tensor", None),
            P("dp", "tensor"),
            P("dp", "tensor"),
            P("tensor", "dp"),
        ),
        check_vma=False,
    )
```

```python
import functools

import jax
import jax.numpy as jnp
from jax import lax
from jax.experimental import pallas as pl
from jax.experimental.pallas import tpu as pltpu
from jax.sharding import PartitionSpec as P

DN = 128
DR = 64
DV = 128
KVR = 512
REACH = 4
SLOTS = 80
BF = jnp.bfloat16
F32 = jnp.float32
VMEM_BYTES = 60 * 1024 * 1024
epsilon = 1e-06


def mm(a, b, ca, cb):
    return lax.dot_general(a, b, (((ca,), (cb,)), ((), ())), preferred_element_type=F32)


def cost(flops, nbytes, trans=0):
    return pl.CostEstimate(flops=int(flops), bytes_accessed=int(nbytes), transcendentals=int(trans))


def smem():
    return pl.BlockSpec(memory_space=pltpu.SMEM)


def fixed(shape):
    return pl.BlockSpec(shape, lambda *at: (0,) * len(shape))


def params():
    return pltpu.CompilerParams(vmem_limit_bytes=VMEM_BYTES)


def attend_setup(
    head, heads, step, qp_ref, cos_ref, sin_ref, wx_ref, sq_ref, sk_ref, keys,
    q_ref, key_ref, v_ref, bias_ref,
):
    rows = qp_ref.shape[0]

    @pl.when(head == 0)
    def _():
        for at in range(0, rows, step):
            part = pl.ds(at, step)
            allowed = (sq_ref[part, 0:1] == sk_ref[0:1, :]) & (
                sk_ref[1:2, :] <= sq_ref[part, 1:2]
            )
            bias_ref[part, :] = jnp.where(allowed, 0.0, -1e30).astype(BF)
        for i, key in enumerate(keys):
            key_ref[i * rows : (i + 1) * rows, DN:] = key[:, KVR : KVR + DR]

    for k in range(heads):

        @pl.when(head == k)
        def _():
            at = k * (DN + DR)
            front = qp_ref[:, at + DN : at + DN + DR // 2]
            back = qp_ref[:, at + DN + DR // 2 : at + DN + DR]
            cosine, sine = cos_ref[...], sin_ref[...]
            q_ref[:, :DN] = qp_ref[:, at : at + DN].astype(BF)
            q_ref[:, DN : DN + DR // 2] = (front * cosine - back * sine).astype(BF)
            q_ref[:, DN + DR // 2 :] = (back * cosine + front * sine).astype(BF)

    for i, key in enumerate(keys):
        kv = mm(key[:, :KVR], wx_ref[...], 1, 0).astype(BF)
        key_ref[i * rows : (i + 1) * rows, :DN] = kv[:, :DN]
        v_ref[i * rows : (i + 1) * rows, :] = kv[:, DN:]


def attend_kernel(heads, step, qp_ref, cos_ref, sin_ref, wx_ref, sq_ref, sk_ref, *rest):
    keys, (o_ref, lse_ref, q_ref, key_ref, v_ref, bias_ref) = rest[:-6], rest[-6:]
    rows = qp_ref.shape[0]
    scale = (DN + DR) ** (-0.5)
    attend_setup(
        pl.program_id(0), heads, step, qp_ref, cos_ref, sin_ref, wx_ref, sq_ref, sk_ref, keys,
        q_ref, key_ref, v_ref, bias_ref,
    )
    for at in range(0, rows, step):
        part = pl.ds(at, step)
        s = mm(q_ref[part, :], key_ref[...], 1, 1) * scale + bias_ref[part, :].astype(F32)
        top = jnp.max(s, axis=-1, keepdims=True)
        p = jnp.exp(s - top)
        total = jnp.sum(p, axis=-1, keepdims=True)
        o_ref[part, :] = mm((p * (1.0 / total)).astype(BF), v_ref[...], 1, 0).astype(BF)
        lse_ref[0, part, :] = top + jnp.log(total)


def attend_specs(query_pre, cosine, w_expand, place_q, place_k, keys):
    return [
        fixed(query_pre.shape),
        fixed(cosine.shape),
        fixed(cosine.shape),
        pl.BlockSpec((KVR, DN + DV), lambda h: (0, h)),
        fixed(place_q.shape),
        fixed(place_k.shape),
    ], [fixed(keys[0].shape) for _ in keys]


def attend(query_pre, cosine, sine, w_expand, place_q, place_k, keys):
    rows = query_pre.shape[0]
    heads = query_pre.shape[1] // (DN + DR)
    window = rows * len(keys)
    specs, key_specs = attend_specs(query_pre, cosine, w_expand, place_q, place_k, keys)
    return pl.pallas_call(
        functools.partial(attend_kernel, heads, rows // 2),
        name="attend",
        grid=(heads,),
        in_specs=specs + key_specs,
        out_specs=[
            pl.BlockSpec((rows, DV), lambda h: (0, h)),
            pl.BlockSpec((1, rows, 1), lambda h: (h, 0, 0)),
        ],
        out_shape=[
            jax.ShapeDtypeStruct((rows, heads * DV), BF),
            jax.ShapeDtypeStruct((heads, rows, 1), F32),
        ],
        scratch_shapes=[
            pltpu.VMEM((rows, DN + DR), BF),
            pltpu.VMEM((window, DN + DR), BF),
            pltpu.VMEM((window, DV), BF),
            pltpu.VMEM((rows, window), BF),
        ],
        compiler_params=params(),
        cost_estimate=cost(
            2 * heads * window * (rows * 384 + KVR * 256), 2 * window * 640, heads * rows * window
        ),
    )(query_pre, cosine, sine, w_expand, place_q, place_k, *keys)


def attend_back_kernel(
    heads, step, count, qp_ref, cos_ref, sin_ref, wx_ref, sq_ref, sk_ref, lse_ref, do_ref, *rest
):
    keys, rest = rest[:count], rest[count:]
    dq_ref, gx_ref = rest[:2]
    grads = rest[2 : 2 + count]
    q_ref, key_ref, v_ref, bias_ref, dk_ref, dv_ref, dkv_ref, acc_ref, dqs_ref = rest[2 + count :]
    rows = qp_ref.shape[0]
    head = pl.program_id(0)
    scale = (DN + DR) ** (-0.5)
    attend_setup(
        head, heads, step, qp_ref, cos_ref, sin_ref, wx_ref, sq_ref, sk_ref, keys,
        q_ref, key_ref, v_ref, bias_ref,
    )

    @pl.when(head == 0)
    def _():
        acc_ref[...] = jnp.zeros_like(acc_ref)

    for at in range(0, rows, step):
        part = pl.ds(at, step)
        q = q_ref[part, :]
        do = do_ref[part, :]
        s = mm(q, key_ref[...], 1, 1) * scale + bias_ref[part, :].astype(F32)
        p = jnp.exp(s - lse_ref[0, part, :])
        dp = mm(do, v_ref[...], 1, 1)
        ds = (p * (dp - jnp.sum(p * dp, axis=-1, keepdims=True))).astype(BF)
        dqs_ref[part, :] = mm(ds, key_ref[...], 1, 0) * scale
        dk = mm(ds, q, 0, 0) * scale
        dv = mm(p.astype(BF), do, 0, 0)
        if at == 0:
            dk_ref[...] = dk
            dv_ref[...] = dv
        else:
            dk_ref[...] += dk
            dv_ref[...] += dv
    dkv_ref[:, :DN] = dk_ref[:, :DN].astype(BF)
    dkv_ref[:, DN:] = dv_ref[...].astype(BF)
    acc_ref[:, :KVR] += mm(dkv_ref[...], wx_ref[...], 1, 1)
    acc_ref[:, KVR : KVR + DR] += dk_ref[:, DN:]
    expand_grad = jnp.zeros((KVR, DN + DV), F32)
    for i, key in enumerate(keys):
        expand_grad += mm(key[:, :KVR], dkv_ref[i * rows : (i + 1) * rows, :], 0, 0)
    gx_ref[...] = expand_grad.astype(BF)
    for k in range(heads):

        @pl.when(head == k)
        def _():
            at = k * (DN + DR)
            front = dqs_ref[:, DN : DN + DR // 2]
            back = dqs_ref[:, DN + DR // 2 :]
            cosine, sine = cos_ref[...], sin_ref[...]
            dq_ref[:, at : at + DN] = dqs_ref[:, :DN].astype(BF)
            dq_ref[:, at + DN : at + DN + DR // 2] = (front * cosine + back * sine).astype(BF)
            dq_ref[:, at + DN + DR // 2 : at + DN + DR] = (back * cosine - front * sine).astype(BF)

    @pl.when(head == heads - 1)
    def _():
        for i, grad in enumerate(grads):
            grad[...] = acc_ref[i * rows : (i + 1) * rows, :].astype(grad.dtype)


def attend_back(query_pre, cosine, sine, w_expand, place_q, place_k, lse, attended_grad, keys):
    rows = query_pre.shape[0]
    heads = query_pre.shape[1] // (DN + DR)
    window = rows * len(keys)
    count = len(keys)
    specs, key_specs = attend_specs(query_pre, cosine, w_expand, place_q, place_k, keys)
    wide = keys[0].shape[1]
    return pl.pallas_call(
        functools.partial(attend_back_kernel, heads, rows // 2, count),
        name="attend_back",
        grid=(heads,),
        in_specs=specs
        + [
            pl.BlockSpec((1, rows, 1), lambda h: (h, 0, 0)),
            pl.BlockSpec((rows, DV), lambda h: (0, h)),
        ]
        + key_specs,
        out_specs=[fixed(query_pre.shape), pl.BlockSpec((KVR, DN + DV), lambda h: (0, h))]
        + [fixed((rows, wide)) for _ in keys],
        out_shape=[
            jax.ShapeDtypeStruct(query_pre.shape, BF),
            jax.ShapeDtypeStruct(w_expand.shape, BF),
        ]
        + [jax.ShapeDtypeStruct((rows, wide), BF) for _ in keys[1:]]
        + [jax.ShapeDtypeStruct((rows, wide), F32)],
        scratch_shapes=[
            pltpu.VMEM((rows, DN + DR), BF),
            pltpu.VMEM((window, DN + DR), BF),
            pltpu.VMEM((window, DV), BF),
            pltpu.VMEM((rows, window), BF),
            pltpu.VMEM((window, DN + DR), F32),
            pltpu.VMEM((window, DV), F32),
            pltpu.VMEM((window, DN + DV), BF),
            pltpu.VMEM((window, wide), F32),
            pltpu.VMEM((rows, DN + DR), F32),
        ],
        compiler_params=params(),
        cost_estimate=cost(
            2 * heads * window * (rows * 1024 + KVR * 768), 4 * window * 640, heads * rows * window
        ),
    )(query_pre, cosine, sine, w_expand, place_q, place_k, lse, attended_grad, *keys)


def one_hot(slot_ref):
    experts, rows = slot_ref.shape[0], slot_ref.shape[-1]
    place = lax.broadcasted_iota(jnp.int32, (SLOTS, rows), 0)
    return jnp.concatenate(
        [(slot_ref[e, 0] == place).astype(F32).astype(BF) for e in range(experts)], axis=0
    )


def pick_kernel(slot_ref, x_ref, o_ref):
    o_ref[...] = mm(one_hot(slot_ref), x_ref[...], 1, 0).astype(BF).reshape(o_ref.shape)


def pick_route_kernel(count, first_ref, slot_ref, x_ref, w_ref, o_ref, p_ref, g_ref):
    x = x_ref[...]
    logits = mm(x, w_ref[...], 1, 1)
    lane = lax.broadcasted_iota(jnp.int32, logits.shape, 1)
    logits = jnp.where(lane < count, logits, -1e30)
    e = jnp.exp(logits - jnp.max(logits, axis=-1, keepdims=True))
    probs = e / jnp.sum(e, axis=-1, keepdims=True)
    p_ref[...] = probs
    high = probs.astype(BF)
    low = (probs - high.astype(F32)).astype(BF)
    chosen = one_hot(slot_ref)
    o_ref[...] = mm(chosen, x, 1, 0).astype(BF).reshape(o_ref.shape)
    taken = mm(chosen, high, 1, 0) + mm(chosen, low, 1, 0)
    lane = lax.broadcasted_iota(jnp.int32, (SLOTS, taken.shape[1]), 1)
    for i in range(slot_ref.shape[0]):
        part = taken[i * SLOTS : (i + 1) * SLOTS, :]
        g_ref[i, 0] = jnp.sum(
            jnp.where(lane == first_ref[0] + i, part, 0.0), axis=-1, keepdims=True
        )


def pick(slot, values):
    experts, blocks, _, rows = slot.shape
    width = values.shape[1]
    return pl.pallas_call(
        pick_kernel,
        name="pick",
        grid=(blocks,),
        in_specs=[
            pl.BlockSpec((experts, 1, 1, rows), lambda b: (0, b, 0, 0)),
            pl.BlockSpec((rows, width), lambda b: (b, 0)),
        ],
        out_specs=pl.BlockSpec((experts, 1, SLOTS, width), lambda b: (0, b, 0, 0)),
        out_shape=jax.ShapeDtypeStruct((experts, blocks, SLOTS, width), BF),
        compiler_params=params(),
        cost_estimate=cost(
            2 * experts * blocks * SLOTS * rows * width,
            2 * blocks * width * (rows + experts * SLOTS),
        ),
    )(slot, values)


def pick_route(first, slot, values, router_rows, count):
    experts, blocks, _, rows = slot.shape
    width = values.shape[1]
    lanes = router_rows.shape[0]
    return pl.pallas_call(
        functools.partial(pick_route_kernel, count),
        name="pick_route",
        grid=(blocks,),
        in_specs=[
            smem(),
            pl.BlockSpec((experts, 1, 1, rows), lambda b: (0, b, 0, 0)),
            pl.BlockSpec((rows, width), lambda b: (b, 0)),
            fixed(router_rows.shape),
        ],
        out_specs=[
            pl.BlockSpec((experts, 1, SLOTS, width), lambda b: (0, b, 0, 0)),
            pl.BlockSpec((rows, lanes), lambda b: (b, 0)),
            pl.BlockSpec((experts, 1, SLOTS, 1), lambda b: (0, b, 0, 0)),
        ],
        out_shape=[
            jax.ShapeDtypeStruct((experts, blocks, SLOTS, width), BF),
            jax.ShapeDtypeStruct((blocks * rows, lanes), F32),
            jax.ShapeDtypeStruct((experts, blocks, SLOTS, 1), F32),
        ],
        compiler_params=params(),
        cost_estimate=cost(
            2 * experts * blocks * SLOTS * rows * width,
            2 * blocks * width * (rows + experts * SLOTS),
        ),
    )(first, slot, values, router_rows)


def put_kernel(place_ref, r_ref, o_ref):
    o_ref[...] = mm(place_ref[0], r_ref[...].reshape(-1, r_ref.shape[-1]), 1, 0).astype(BF)


def put_route_kernel(first_ref, place_ref, r_ref, p_ref, pg_ref, w_ref, o_ref, lg_ref):
    experts, rows = pg_ref.shape[0], pg_ref.shape[3]
    by_expert = jnp.concatenate(
        [pg_ref[i, 0] for i in range(experts)] + [jnp.zeros((1, rows), F32)] * (-experts % 8), axis=0
    )
    high = by_expert.astype(BF)
    low = (by_expert - high.astype(F32)).astype(BF)
    probs = p_ref[...]
    shape = (by_expert.shape[0], probs.shape[1])
    expert = lax.broadcasted_iota(jnp.int32, shape, 0)
    lane = lax.broadcasted_iota(jnp.int32, shape, 1)
    spread = (lane == first_ref[0] + expert) & (expert < experts)
    spread = spread.astype(F32).astype(BF)
    grad = mm(high, spread, 0, 0) + mm(low, spread, 0, 0)
    back = (probs * (grad - jnp.sum(probs * grad, axis=-1, keepdims=True))).astype(BF)
    lg_ref[...] = back
    total = mm(place_ref[0], r_ref[...].reshape(-1, r_ref.shape[-1]), 1, 0)
    o_ref[...] = (total + mm(back, w_ref[...], 1, 0)).astype(BF)


def put_specs(places, picked):
    blocks, rows, slots = places.shape
    experts, width = picked.shape[0], picked.shape[3]
    return [
        pl.BlockSpec((1, rows, slots), lambda b: (b, 0, 0)),
        pl.BlockSpec((experts, 1, SLOTS, width), lambda b: (0, b, 0, 0)),
    ]


def put_cost(places, width):
    blocks, rows, slots = places.shape
    return cost(2 * blocks * slots * rows * width, 2 * blocks * width * (rows + slots))


def put(places, picked):
    blocks, rows, _ = places.shape
    width = picked.shape[3]
    return pl.pallas_call(
        put_kernel,
        name="put",
        grid=(blocks,),
        in_specs=put_specs(places, picked),
        out_specs=pl.BlockSpec((rows, width), lambda b: (b, 0)),
        out_shape=jax.ShapeDtypeStruct((blocks * rows, width), BF),
        compiler_params=params(),
        cost_estimate=put_cost(places, width),
    )(places, picked)


def put_route(first, places, picked, probs, probs_grad, router_rows):
    blocks, rows, _ = places.shape
    experts, width = picked.shape[0], picked.shape[3]
    lanes = probs.shape[1]
    return pl.pallas_call(
        put_route_kernel,
        name="put_route",
        grid=(blocks,),
        in_specs=[smem()]
        + put_specs(places, picked)
        + [
            pl.BlockSpec((rows, lanes), lambda b: (b, 0)),
            pl.BlockSpec((experts, 1, 1, rows), lambda b: (0, b, 0, 0)),
            fixed(router_rows.shape),
        ],
        out_specs=[
            pl.BlockSpec((rows, width), lambda b: (b, 0)),
            pl.BlockSpec((rows, lanes), lambda b: (b, 0)),
        ],
        out_shape=[
            jax.ShapeDtypeStruct((blocks * rows, width), BF),
            jax.ShapeDtypeStruct((blocks * rows, lanes), BF),
        ],
        compiler_params=params(),
        cost_estimate=put_cost(places, width),
    )(first, places, picked, probs, probs_grad, router_rows)


def down_back_kernel(x_ref, w_ref, o_ref):
    ff = w_ref.shape[1]
    wide = o_ref.shape[-1]
    back = mm(x_ref[...].reshape(-1, x_ref.shape[-1]), w_ref[0], 1, 1)
    o_ref[0, :, :ff] = back
    if wide > ff:
        o_ref[0, :, ff:] = jnp.zeros((o_ref.shape[1], wide - ff), F32)


def down_back(rows, down):
    experts, blocks, slots, width = rows.shape
    ff = down.shape[1]
    wide = -(-ff // 128) * 128
    count = blocks * slots
    return pl.pallas_call(
        down_back_kernel,
        name="down_back",
        grid=(experts,),
        in_specs=[
            pl.BlockSpec((1, blocks, slots, width), lambda e: (e, 0, 0, 0)),
            pl.BlockSpec((1, ff, width), lambda e: (e, 0, 0)),
        ],
        out_specs=pl.BlockSpec((1, count, wide), lambda e: (e, 0, 0)),
        out_shape=jax.ShapeDtypeStruct((experts, count, wide), F32),
        compiler_params=params(),
        cost_estimate=cost(
            2 * experts * count * width * ff,
            experts * (2 * count * width + 2 * ff * width + 4 * count * wide),
        ),
    )(rows, down)


def row_out_kernel(x_ref, w_ref, o_ref):
    ff = w_ref.shape[1]
    o_ref[...] = mm(x_ref[0, :, :ff], w_ref[0], 1, 0).astype(BF).reshape(o_ref.shape)


def row_out(active, down, blocks):
    experts, count, wide = active.shape
    ff, width = down.shape[1:]
    slots = count // blocks
    return pl.pallas_call(
        row_out_kernel,
        name="row_out",
        grid=(experts,),
        in_specs=[
            pl.BlockSpec((1, count, wide), lambda e: (e, 0, 0)),
            pl.BlockSpec((1, ff, width), lambda e: (e, 0, 0)),
        ],
        out_specs=pl.BlockSpec((1, blocks, slots, width), lambda e: (e, 0, 0, 0)),
        out_shape=jax.ShapeDtypeStruct((experts, blocks, slots, width), BF),
        compiler_params=params(),
        cost_estimate=cost(
            2 * experts * count * width * ff,
            2 * experts * (count * width + ff * width + count * wide),
        ),
    )(active, down)


def expert_kernel(
    x_ref, gate_ref, up_ref, back_ref, slot_ref, sg_ref,
    ga_ref, dg_ref, du_ref, dx_ref, pg_ref, w_ref, d_ref,
):
    ff = gate_ref.shape[1]
    wide = back_ref.shape[2]
    blocks, rows = slot_ref.shape[1], slot_ref.shape[3]

    @pl.when(pl.program_id(0) == 0)
    def _():
        w_ref[...] = jnp.zeros_like(w_ref)

    w_ref[:ff, :] = gate_ref[0]
    w_ref[wide : wide + ff, :] = up_ref[0]
    x = x_ref[...].reshape(-1, x_ref.shape[-1])
    both = mm(x, w_ref[...], 1, 1)
    a = both[:, :wide]
    b = both[:, wide:]
    place = lax.broadcasted_iota(jnp.int32, (SLOTS, rows), 0)
    slot_gate = sg_ref[...].reshape(-1, 1)
    back = back_ref[0]
    sig = jax.nn.sigmoid(a)
    swish = a * sig
    active = swish * b
    gate_grad = jnp.sum(active * back, axis=-1, keepdims=True)
    for i in range(blocks):
        part = gate_grad[i * SLOTS : (i + 1) * SLOTS, :]
        pg_ref[0, i] = jnp.sum(
            jnp.where(slot_ref[0, i] == place, part, 0.0), axis=0, keepdims=True
        )
    gated = back * slot_gate
    ga_ref[0] = (active * slot_gate).astype(BF)
    dg = (gated * b * (sig + swish * (1.0 - sig))).astype(BF)
    du = (gated * swish).astype(BF)
    dg_ref[0] = dg
    du_ref[0] = du
    d_ref[:, :wide] = dg
    d_ref[:, wide:] = du
    dx_ref[...] = mm(d_ref[...], w_ref[...], 1, 0).astype(BF).reshape(dx_ref.shape)


def expert_step(rows, gate_t, up_t, back, slot, slot_gates):
    experts, blocks, slots, width = rows.shape
    ff = gate_t.shape[1]
    wide = back.shape[2]
    count = blocks * slots
    whole = pl.BlockSpec((1, blocks, slots, width), lambda e: (e, 0, 0, 0))
    flat = lambda n: pl.BlockSpec((1, count, n), lambda e: (e, 0, 0))
    shape = lambda n, dtype: jax.ShapeDtypeStruct((experts, count, n), dtype)
    weight = pl.BlockSpec((1, ff, width), lambda e: (e, 0, 0))
    by_token = pl.BlockSpec((1,) + slot.shape[1:], lambda e: (e, 0, 0, 0))
    return pl.pallas_call(
        expert_kernel,
        name="expert_step",
        grid=(experts,),
        in_specs=[
            whole,
            weight,
            weight,
            flat(wide),
            by_token,
            pl.BlockSpec((1, blocks, slots, 1), lambda e: (e, 0, 0, 0)),
        ],
        out_specs=[flat(wide), flat(wide), flat(wide), whole, by_token],
        out_shape=[
            shape(wide, BF),
            shape(wide, BF),
            shape(wide, BF),
            jax.ShapeDtypeStruct(rows.shape, BF),
            jax.ShapeDtypeStruct(slot.shape, F32),
        ],
        scratch_shapes=[pltpu.VMEM((2 * wide, width), BF), pltpu.VMEM((count, 2 * wide), BF)],
        compiler_params=params(),
        cost_estimate=cost(
            8 * experts * count * width * wide,
            2 * experts * (2 * count * width + 2 * width * wide + 5 * count * wide),
            experts * count * wide,
        ),
    )(rows, gate_t, up_t, back, slot, slot_gates)


def norm_kernel(x_ref, add_ref, gain_ref, sum_ref, o_ref):
    x = x_ref[...].astype(F32) + add_ref[...].astype(F32)
    sum_ref[...] = x
    scale = lax.rsqrt(jnp.mean(x * x, axis=-1, keepdims=True) + epsilon)
    o_ref[...] = (x * scale * gain_ref[...]).astype(BF)


def norm_sum(values, added, gain):
    rows, width = values.shape
    block = pl.BlockSpec((rows // 4, width), lambda i: (i, 0))
    return pl.pallas_call(
        norm_kernel,
        name="norm_sum",
        grid=(4,),
        in_specs=[block, block, fixed((1, width))],
        out_specs=[block, block],
        out_shape=[
            jax.ShapeDtypeStruct((rows, width), F32),
            jax.ShapeDtypeStruct((rows, width), BF),
        ],
        compiler_params=params(),
        cost_estimate=cost(8 * rows * width, 10 * rows * width),
    )(values, added, gain.reshape(1, width))


def norm_back_kernel(x_ref, up_ref, res_ref, gain_ref, *outs):
    x = x_ref[...].astype(F32)
    up = up_ref[...].astype(F32)
    scale = lax.rsqrt(jnp.mean(x * x, axis=-1, keepdims=True) + epsilon)
    scaled = x * scale
    if len(outs) > 1:

        @pl.when(pl.program_id(0) == 0)
        def _():
            outs[2][...] = jnp.zeros_like(outs[2])

        outs[2][...] += jnp.sum(up * scaled, axis=0, keepdims=True)
    up = up * gain_ref[...]
    back = scale * (up - scaled * jnp.mean(up * scaled, axis=-1, keepdims=True))
    total = res_ref[...].astype(F32) + back
    outs[0][...] = total.astype(BF)
    if len(outs) > 1:
        outs[1][...] = total


def norm_back(values, upstream, residual, gain, last):
    rows, width = values.shape
    block = pl.BlockSpec((rows // 4, width), lambda i: (i, 0))
    specs = [block] if last else [block, block, fixed((1, width))]
    shapes = [jax.ShapeDtypeStruct((rows, width), BF)]
    if not last:
        shapes += [
            jax.ShapeDtypeStruct((rows, width), F32),
            jax.ShapeDtypeStruct((1, width), F32),
        ]
    return pl.pallas_call(
        norm_back_kernel,
        name="norm_back",
        grid=(4,),
        in_specs=[block, block, block, fixed((1, width))],
        out_specs=specs,
        out_shape=shapes,
        compiler_params=params(),
        cost_estimate=cost(12 * rows * width, 12 * rows * width),
    )(values, upstream, residual, gain.reshape(1, width))


def dot(eq, a, b):
    return jnp.einsum(eq, a, b, preferred_element_type=F32)


def passed_along(shard, axis, by):
    peers = lax.axis_size(axis)
    pairs = [(i, i + by) for i in range(peers) if 0 <= i + by < peers]
    return lax.ppermute(shard, axis, pairs)


def normed(values, norm_gain):
    return (
        values * lax.rsqrt(jnp.mean(values * values, axis=-1, keepdims=True) + epsilon) * norm_gain
    )


def norm_backward(values, norm_gain, upstream):
    _, pullback = jax.vjp(normed, values, norm_gain)
    return pullback(upstream)


def rotate(values, cosine, sine):
    half = values.shape[-1] // 2
    front, back = values[..., :half], values[..., half:]
    return jnp.concatenate([front * cosine - back * sine, back * cosine + front * sine], axis=-1)


def rotate_back(upstream, cosine, sine):
    return rotate(upstream, cosine, -sine)


def silu_gate(gate_val, up_val):
    return gate_val * jax.nn.sigmoid(gate_val) * up_val


def silu_backward(gate_val, up_val, upstream):
    _, pullback = jax.vjp(silu_gate, gate_val, up_val)
    return pullback(upstream)


def rope_tables(seq_all, seq_here, index_here):
    starts = jnp.sum((seq_all[None, :] < seq_here[:, None]).astype(jnp.int32), axis=1)
    position = (index_here - starts).astype(F32)
    frequency = 10000.0 ** (-(jnp.arange(DR // 2, dtype=F32) * 2.0) / DR)
    angle = position[:, None] * frequency[None, :]
    return jnp.cos(angle), jnp.sin(angle)


def swapped(value):
    return lax.ppermute(value, "dp", [(i, i ^ 1) for i in range(lax.axis_size("dp"))])


def after(value, *others):
    return lax.optimization_barrier((value,) + others)[0]


def scatter_sum(parts):
    joined = parts if not isinstance(parts, list) else jnp.concatenate(parts, axis=1)
    return lax.psum_scatter(joined, "dp", scatter_dimension=0, tiled=True)


def tensor_sum(value):
    peers = lax.axis_size("tensor")
    rank = lax.axis_index("tensor")
    rows = value.shape[0] // peers
    piece = lambda at: lax.dynamic_slice_in_dim(value, at * rows, rows, 0)
    turn = lambda piece, by: lax.ppermute(
        piece, "tensor", [(i, (i + by) % peers) for i in range(peers)]
    )
    total = piece(rank).astype(F32)
    for by in range(1, peers):
        total = total + turn(piece((rank + by) % peers), by).astype(F32)
    mine = total.astype(BF)
    around = [turn(mine, by) for by in range(peers - 1, 0, -1)] + [mine]
    both = jnp.concatenate(around + around[:-1], axis=0)
    return lax.dynamic_slice_in_dim(both, (peers - 1 - rank) * rows, value.shape[0], 0)


def shards(
    tokens,
    seq_ids,
    route_ids,
    cotangent,
    input_gain,
    w_query,
    w_latent,
    latent_gain,
    w_expand,
    w_out,
    middle_gain,
    w_router,
    expert_gate,
    expert_up,
    expert_down,
    shared_gate,
    shared_up,
    shared_down,
):
    devices = lax.axis_size("dp")
    rank_dp = lax.axis_index("dp")
    tok_rows, width = tokens.shape
    experts_local = expert_gate.shape[0]
    all_experts = w_router.shape[1]
    ff_local = expert_gate.shape[2]
    heads_local = w_query.shape[1] // (DN + DR)

    cot_all = lax.all_gather(cotangent, "dp", tiled=True)
    route_all = lax.all_gather(route_ids, "dp", tiled=True)

    index_here = rank_dp * tok_rows + jnp.arange(tok_rows, dtype=jnp.int32)
    seq_here = lax.dynamic_slice_in_dim(seq_ids, rank_dp * tok_rows, tok_rows, 0)
    cosine, sine = rope_tables(seq_ids, seq_here, index_here)
    odd = rank_dp % 2
    blocks = [rank_dp - 4, rank_dp - 2, (rank_dp - 2) ^ 1, rank_dp - 3 + 2 * odd, rank_dp]
    seq_padded = jnp.concatenate([jnp.full((4 * tok_rows,), -1, jnp.int32), seq_ids])
    seq_keys = jnp.concatenate(
        [lax.dynamic_slice_in_dim(seq_padded, (at + 4) * tok_rows, tok_rows, 0) for at in blocks]
    )
    key_index = jnp.concatenate(
        [at * tok_rows + jnp.arange(tok_rows, dtype=jnp.int32) for at in blocks]
    )
    place_q = jnp.stack([seq_here, index_here], axis=1)
    place_k = jnp.stack([seq_keys, key_index], axis=0)

    token_features = tokens.astype(F32)
    hidden_in = normed(token_features, input_gain).astype(BF)
    latent_full = jnp.dot(hidden_in, w_latent, preferred_element_type=F32)
    latent_raw = latent_full[:, :KVR]
    latent = normed(latent_raw, latent_gain).astype(BF)
    rope_key = rotate(latent_full[:, KVR:], cosine, sine).astype(BF)
    fill = jnp.zeros((tok_rows, -(KVR + DR) % 128), BF)
    own_keys = jnp.concatenate([latent, rope_key, fill], axis=1)
    before_two = passed_along(own_keys, "dp", 2)
    before_four = passed_along(own_keys, "dp", 4)
    keys = [
        before_four,
        before_two,
        swapped(before_two),
        swapped(jnp.where(odd == 0, own_keys, before_four)),
        own_keys,
    ]
    query_pre = jnp.dot(hidden_in, w_query, preferred_element_type=F32)
    attended, lse = attend(query_pre, cosine, sine, w_expand, place_q, place_k, keys)
    attention = lax.psum(
        jnp.dot(attended, w_out, preferred_element_type=F32).astype(BF), "tensor"
    )
    attention = after(attention, cot_all)
    middle, hidden_mid = norm_sum(tokens, attention, middle_gain)
    hidden_all = lax.all_gather(hidden_mid, "dp", tiled=True)

    local_ids = rank_dp * experts_local + jnp.arange(experts_local, dtype=jnp.int32)
    named = jnp.any(route_all[:, :, None] == local_ids[None, None, :], axis=1)
    named_block = named.reshape(devices, tok_rows, experts_local)
    before = jnp.tril(jnp.ones((tok_rows, tok_rows), BF), -1)
    rank_within = dot("ts,bse->bte", before, named_block.astype(BF))
    slot_of = jnp.where(named_block, rank_within, -1.0)
    slot = slot_of.astype(jnp.int32).transpose(2, 0, 1)[:, :, None, :]
    columns = jnp.arange(experts_local * SLOTS, dtype=jnp.int32)
    spread = (columns[None, :] // SLOTS == jnp.arange(experts_local, dtype=jnp.int32)[:, None]).astype(
        BF
    )
    places = (
        dot("bte,en->btn", slot_of.astype(BF), spread) == (columns % SLOTS).astype(F32)
    ).astype(BF)
    gate_t = expert_gate.swapaxes(1, 2)
    up_t = expert_up.swapaxes(1, 2)
    cot_rows = pick(slot, cot_all)
    back = down_back(cot_rows, expert_down)

    shared_gate_val = jnp.dot(hidden_mid, shared_gate, preferred_element_type=F32)
    shared_up_val = jnp.dot(hidden_mid, shared_up, preferred_element_type=F32)
    shared_active = silu_gate(shared_gate_val, shared_up_val).astype(BF)
    shared_result = jnp.dot(shared_active, shared_down, preferred_element_type=F32)
    shared_active_grad = dot("td,fd->tf", cotangent, shared_down)
    shared_gate_grad, shared_up_grad = silu_backward(
        shared_gate_val, shared_up_val, shared_active_grad
    )
    shared_gate_grad = shared_gate_grad.astype(BF)
    shared_up_grad = shared_up_grad.astype(BF)
    mid_from_shared = dot("tf,df->td", shared_gate_grad, shared_gate) + dot(
        "tf,df->td", shared_up_grad, shared_up
    )
    shared_grads = jnp.concatenate(
        [
            dot("td,tf->df", cotangent, shared_active).astype(BF),
            dot("td,tf->df", hidden_mid, shared_gate_grad).astype(BF),
            dot("td,tf->df", hidden_mid, shared_up_grad).astype(BF),
        ],
        axis=1,
    )

    hidden_all = after(hidden_all, back, shared_grads)
    first = (rank_dp * experts_local).astype(jnp.int32).reshape(1)
    router_rows = jnp.pad(w_router.T, ((0, -all_experts % 128), (0, 0)))
    rows, router_probs, slot_gates = pick_route(first, slot, hidden_all, router_rows, all_experts)
    shared_sums = scatter_sum(shared_grads)
    gated_active, gate_val_grad, up_val_grad, row_grad, probs_grad = expert_step(
        rows, gate_t, up_t, back, slot, slot_gates
    )
    mid_part, logit_grad = put_route(first, places, row_grad, router_probs, probs_grad, router_rows)
    mid_part = after(mid_part, shared_sums)
    mid_block = lax.psum_scatter(mid_part, "dp", scatter_dimension=0, tiled=True)
    grad_router = dot("td,te->de", hidden_all, logit_grad[:, :all_experts]).astype(BF)
    routed_part = put(places, row_out(gated_active, expert_down, devices))
    rows_flat = rows.reshape(experts_local, -1, width)
    grad_expert_down = dot(
        "ecf,ecd->efd",
        gated_active[..., :ff_local],
        cot_rows.reshape(experts_local, -1, width),
    )
    grad_expert_gate = dot("ecd,ecf->edf", rows_flat, gate_val_grad[..., :ff_local])
    grad_expert_up = dot("ecd,ecf->edf", rows_flat, up_val_grad[..., :ff_local])

    routed_block = scatter_sum(routed_part)
    mid_block = after(mid_block, routed_part, grad_router, grad_expert_down)
    mid_grad = lax.psum((mid_block.astype(F32) + mid_from_shared).astype(BF), "tensor")
    mid_grad = after(mid_grad, grad_expert_gate, grad_expert_up)

    middle_low, middle_grad, grad_middle_gain = norm_back(
        middle, mid_grad, cotangent, middle_gain, False
    )
    attended_grad = dot("td,cd->tc", middle_low, w_out).astype(BF)
    query_grad, grad_expand, *window_grads = attend_back(
        query_pre, cosine, sine, w_expand, place_q, place_k, lse, attended_grad, keys
    )
    routed_block = after(routed_block, grad_expand)
    ff_part = (routed_block.astype(F32) + shared_result).astype(BF)
    window_grads = lax.optimization_barrier((*window_grads, ff_part))[:-1]
    four_grad, two_grad, pair_grad, last_grad, keys_grad = window_grads
    pair_grad = swapped(pair_grad)
    last_grad = swapped(last_grad).astype(F32)
    two_grad = (two_grad.astype(F32) + pair_grad.astype(F32)).astype(BF)
    four_grad = (four_grad.astype(F32) + jnp.where(odd == 1, last_grad, 0.0)).astype(BF)
    keys_grad = keys_grad + jnp.where(odd == 0, last_grad, 0.0)
    keys_grad = keys_grad + passed_along(two_grad, "dp", -2).astype(F32)
    keys_grad = keys_grad + passed_along(four_grad, "dp", -4).astype(F32)
    latent_raw_grad, grad_latent_gain = norm_backward(latent_raw, latent_gain, keys_grad[:, :KVR])
    rope_raw_grad = rotate_back(keys_grad[:, KVR : KVR + DR], cosine, sine)
    latent_full_grad = jnp.concatenate([latent_raw_grad, rope_raw_grad], axis=-1).astype(BF)
    input_part = dot("tc,dc->td", query_grad, w_query) + dot(
        "tc,dc->td", latent_full_grad, w_latent
    )
    _, grad_input_gain = norm_backward(token_features, input_gain, input_part)

    feedforward = lax.psum(ff_part, "tensor")
    output = (middle + feedforward.astype(F32)).astype(BF)
    input_part, grad_input_gain = lax.optimization_barrier((input_part.astype(BF), grad_input_gain))
    input_part = after(input_part, feedforward)
    input_grad = lax.psum(input_part, "tensor")
    tensors = lax.axis_size("tensor")
    query_width = heads_local * (DN + DR)
    out_width = heads_local * DV
    expand_width = w_expand.shape[1] * KVR // width
    latent_width = KVR + DR
    gains = jnp.concatenate(
        [
            grad_middle_gain / tensors,
            grad_input_gain[None, :],
            jnp.repeat(grad_latent_gain, width // KVR)[None, :],
            jnp.zeros((125, width), F32),
        ],
        axis=0,
    )
    parts = scatter_sum(
        [dot("td,tc->dc", hidden_in, latent_full_grad).astype(BF), grad_router, gains.astype(BF).T]
    )
    late = scatter_sum(
        [
            dot("td,tc->dc", middle_low, attended).astype(BF),
            dot("td,tc->dc", hidden_in, query_grad).astype(BF),
            after(grad_expand, keys_grad).reshape(width, expand_width),
        ]
    )
    parts = tensor_sum(parts).astype(F32)
    input_grad = after(input_grad, parts)
    (token_grad,) = norm_back(tokens, input_grad, middle_grad, input_gain, True)
    sw = shared_gate.shape[1]
    gain_at = latent_width + all_experts
    return (
        output,
        token_grad,
        parts[:, gain_at + 1],
        late[:, out_width : out_width + query_width].astype(F32),
        parts[:, :latent_width],
        parts[:: width // KVR, gain_at + 2],
        late[:, out_width + query_width :].astype(F32).reshape(KVR // devices, -1),
        late[:, :out_width].astype(F32).T,
        parts[:, gain_at],
        parts[:, latent_width:gain_at],
        grad_expert_gate,
        grad_expert_up,
        grad_expert_down,
        shared_sums[:, sw : 2 * sw].astype(F32),
        shared_sums[:, 2 * sw :].astype(F32),
        shared_sums[:, :sw].astype(F32).T,
    )


def solution(mesh):
    placed = (
        P("dp", None),
        P(),
        P("dp", None),
        P("dp", None),
        P(),
        P(None, "tensor"),
        P(),
        P(),
        P(None, "tensor"),
        P("tensor", None),
        P(),
        P(),
        P("dp", None, "tensor"),
        P("dp", None, "tensor"),
        P("dp", "tensor", None),
        P(None, "tensor"),
        P(None, "tensor"),
        P("tensor", None),
    )
    return jax.shard_map(
        shards,
        mesh=mesh,
        in_specs=placed,
        out_specs=(
            P("dp", None),
            P("dp", None),
            P("dp"),
            P("dp", "tensor"),
            P("dp", None),
            P("dp"),
            P("dp", "tensor"),
            P("tensor", "dp"),
            P("dp"),
            P("dp", None),
            P("dp", None, "tensor"),
            P("dp", None, "tensor"),
            P("dp", "tensor", None),
            P("dp", "tensor"),
            P("dp", "tensor"),
            P("tensor", "dp"),
        ),
        check_vma=False,
    )
```

```python
import functools

import jax
import jax.numpy as jnp
from jax import lax
from jax.experimental import pallas as pl
from jax.experimental.pallas import tpu as pltpu
from jax.sharding import PartitionSpec as P

DN = 128
DR = 64
DV = 128
KVR = 512
REACH = 4
SLOTS = 80
BF = jnp.bfloat16
F32 = jnp.float32
VMEM_BYTES = 60 * 1024 * 1024
epsilon = 1e-06


def mm(a, b, ca, cb):
    return lax.dot_general(a, b, (((ca,), (cb,)), ((), ())), preferred_element_type=F32)


def cost(flops, nbytes, trans=0):
    return pl.CostEstimate(flops=int(flops), bytes_accessed=int(nbytes), transcendentals=int(trans))


def smem():
    return pl.BlockSpec(memory_space=pltpu.SMEM)


def fixed(shape):
    return pl.BlockSpec(shape, lambda *at: (0,) * len(shape))


def params():
    return pltpu.CompilerParams(vmem_limit_bytes=VMEM_BYTES)


def attend_setup(
    head, heads, step, qp_ref, cos_ref, sin_ref, wx_ref, sq_ref, sk_ref, keys,
    q_ref, key_ref, v_ref, bias_ref,
):
    rows = qp_ref.shape[0]

    @pl.when(head == 0)
    def _():
        for at in range(0, rows, step):
            part = pl.ds(at, step)
            allowed = (sq_ref[part, 0:1] == sk_ref[0:1, :]) & (
                sk_ref[1:2, :] <= sq_ref[part, 1:2]
            )
            bias_ref[part, :] = jnp.where(allowed, 0.0, -1e30).astype(BF)
        for i, key in enumerate(keys):
            key_ref[i * rows : (i + 1) * rows, DN:] = key[:, KVR : KVR + DR]

    for k in range(heads):

        @pl.when(head == k)
        def _():
            at = k * (DN + DR)
            front = qp_ref[:, at + DN : at + DN + DR // 2]
            back = qp_ref[:, at + DN + DR // 2 : at + DN + DR]
            cosine, sine = cos_ref[...], sin_ref[...]
            q_ref[:, :DN] = qp_ref[:, at : at + DN].astype(BF)
            q_ref[:, DN : DN + DR // 2] = (front * cosine - back * sine).astype(BF)
            q_ref[:, DN + DR // 2 :] = (back * cosine + front * sine).astype(BF)

    for i, key in enumerate(keys):
        kv = mm(key[:, :KVR], wx_ref[...], 1, 0).astype(BF)
        key_ref[i * rows : (i + 1) * rows, :DN] = kv[:, :DN]
        v_ref[i * rows : (i + 1) * rows, :] = kv[:, DN:]


def attend_kernel(heads, step, qp_ref, cos_ref, sin_ref, wx_ref, sq_ref, sk_ref, *rest):
    keys, (o_ref, lse_ref, q_ref, key_ref, v_ref, bias_ref) = rest[:-6], rest[-6:]
    rows = qp_ref.shape[0]
    scale = (DN + DR) ** (-0.5)
    attend_setup(
        pl.program_id(0), heads, step, qp_ref, cos_ref, sin_ref, wx_ref, sq_ref, sk_ref, keys,
        q_ref, key_ref, v_ref, bias_ref,
    )
    for at in range(0, rows, step):
        part = pl.ds(at, step)
        s = mm(q_ref[part, :], key_ref[...], 1, 1) * scale + bias_ref[part, :].astype(F32)
        top = jnp.max(s, axis=-1, keepdims=True)
        p = jnp.exp(s - top)
        total = jnp.sum(p, axis=-1, keepdims=True)
        o_ref[part, :] = mm((p * (1.0 / total)).astype(BF), v_ref[...], 1, 0).astype(BF)
        lse_ref[0, part, :] = top + jnp.log(total)


def attend_specs(query_pre, cosine, w_expand, place_q, place_k, keys):
    return [
        fixed(query_pre.shape),
        fixed(cosine.shape),
        fixed(cosine.shape),
        pl.BlockSpec((KVR, DN + DV), lambda h: (0, h)),
        fixed(place_q.shape),
        fixed(place_k.shape),
    ], [fixed(keys[0].shape) for _ in keys]


def attend(query_pre, cosine, sine, w_expand, place_q, place_k, keys):
    rows = query_pre.shape[0]
    heads = query_pre.shape[1] // (DN + DR)
    window = rows * len(keys)
    specs, key_specs = attend_specs(query_pre, cosine, w_expand, place_q, place_k, keys)
    return pl.pallas_call(
        functools.partial(attend_kernel, heads, rows // 2),
        name="attend",
        grid=(heads,),
        in_specs=specs + key_specs,
        out_specs=[
            pl.BlockSpec((rows, DV), lambda h: (0, h)),
            pl.BlockSpec((1, rows, 1), lambda h: (h, 0, 0)),
        ],
        out_shape=[
            jax.ShapeDtypeStruct((rows, heads * DV), BF),
            jax.ShapeDtypeStruct((heads, rows, 1), F32),
        ],
        scratch_shapes=[
            pltpu.VMEM((rows, DN + DR), BF),
            pltpu.VMEM((window, DN + DR), BF),
            pltpu.VMEM((window, DV), BF),
            pltpu.VMEM((rows, window), BF),
        ],
        compiler_params=params(),
        cost_estimate=cost(
            2 * heads * window * (rows * 384 + KVR * 256), 2 * window * 640, heads * rows * window
        ),
    )(query_pre, cosine, sine, w_expand, place_q, place_k, *keys)


def attend_back_kernel(
    heads, step, count, qp_ref, cos_ref, sin_ref, wx_ref, sq_ref, sk_ref, lse_ref, do_ref, *rest
):
    keys, rest = rest[:count], rest[count:]
    dq_ref, gx_ref = rest[:2]
    grads = rest[2 : 2 + count]
    q_ref, key_ref, v_ref, bias_ref, dk_ref, dv_ref, dkv_ref, acc_ref, dqs_ref = rest[2 + count :]
    rows = qp_ref.shape[0]
    head = pl.program_id(0)
    scale = (DN + DR) ** (-0.5)
    attend_setup(
        head, heads, step, qp_ref, cos_ref, sin_ref, wx_ref, sq_ref, sk_ref, keys,
        q_ref, key_ref, v_ref, bias_ref,
    )

    @pl.when(head == 0)
    def _():
        acc_ref[...] = jnp.zeros_like(acc_ref)

    for at in range(0, rows, step):
        part = pl.ds(at, step)
        q = q_ref[part, :]
        do = do_ref[part, :]
        s = mm(q, key_ref[...], 1, 1) * scale + bias_ref[part, :].astype(F32)
        p = jnp.exp(s - lse_ref[0, part, :])
        dp = mm(do, v_ref[...], 1, 1)
        ds = (p * (dp - jnp.sum(p * dp, axis=-1, keepdims=True))).astype(BF)
        dqs_ref[part, :] = mm(ds, key_ref[...], 1, 0) * scale
        dk = mm(ds, q, 0, 0) * scale
        dv = mm(p.astype(BF), do, 0, 0)
        if at == 0:
            dk_ref[...] = dk
            dv_ref[...] = dv
        else:
            dk_ref[...] += dk
            dv_ref[...] += dv
    dkv_ref[:, :DN] = dk_ref[:, :DN].astype(BF)
    dkv_ref[:, DN:] = dv_ref[...].astype(BF)
    acc_ref[:, :KVR] += mm(dkv_ref[...], wx_ref[...], 1, 1)
    acc_ref[:, KVR : KVR + DR] += dk_ref[:, DN:]
    expand_grad = jnp.zeros((KVR, DN + DV), F32)
    for i, key in enumerate(keys):
        expand_grad += mm(key[:, :KVR], dkv_ref[i * rows : (i + 1) * rows, :], 0, 0)
    gx_ref[...] = expand_grad.astype(BF)
    for k in range(heads):

        @pl.when(head == k)
        def _():
            at = k * (DN + DR)
            front = dqs_ref[:, DN : DN + DR // 2]
            back = dqs_ref[:, DN + DR // 2 :]
            cosine, sine = cos_ref[...], sin_ref[...]
            dq_ref[:, at : at + DN] = dqs_ref[:, :DN].astype(BF)
            dq_ref[:, at + DN : at + DN + DR // 2] = (front * cosine + back * sine).astype(BF)
            dq_ref[:, at + DN + DR // 2 : at + DN + DR] = (back * cosine - front * sine).astype(BF)

    @pl.when(head == heads - 1)
    def _():
        for i, grad in enumerate(grads):
            grad[...] = acc_ref[i * rows : (i + 1) * rows, :].astype(grad.dtype)


def attend_back(query_pre, cosine, sine, w_expand, place_q, place_k, lse, attended_grad, keys):
    rows = query_pre.shape[0]
    heads = query_pre.shape[1] // (DN + DR)
    window = rows * len(keys)
    count = len(keys)
    specs, key_specs = attend_specs(query_pre, cosine, w_expand, place_q, place_k, keys)
    wide = keys[0].shape[1]
    return pl.pallas_call(
        functools.partial(attend_back_kernel, heads, rows // 2, count),
        name="attend_back",
        grid=(heads,),
        in_specs=specs
        + [
            pl.BlockSpec((1, rows, 1), lambda h: (h, 0, 0)),
            pl.BlockSpec((rows, DV), lambda h: (0, h)),
        ]
        + key_specs,
        out_specs=[fixed(query_pre.shape), pl.BlockSpec((KVR, DN + DV), lambda h: (0, h))]
        + [fixed((rows, wide)) for _ in keys],
        out_shape=[
            jax.ShapeDtypeStruct(query_pre.shape, BF),
            jax.ShapeDtypeStruct(w_expand.shape, BF),
        ]
        + [jax.ShapeDtypeStruct((rows, wide), BF) for _ in keys[1:]]
        + [jax.ShapeDtypeStruct((rows, wide), F32)],
        scratch_shapes=[
            pltpu.VMEM((rows, DN + DR), BF),
            pltpu.VMEM((window, DN + DR), BF),
            pltpu.VMEM((window, DV), BF),
            pltpu.VMEM((rows, window), BF),
            pltpu.VMEM((window, DN + DR), F32),
            pltpu.VMEM((window, DV), F32),
            pltpu.VMEM((window, DN + DV), BF),
            pltpu.VMEM((window, wide), F32),
            pltpu.VMEM((rows, DN + DR), F32),
        ],
        compiler_params=params(),
        cost_estimate=cost(
            2 * heads * window * (rows * 1024 + KVR * 768), 4 * window * 640, heads * rows * window
        ),
    )(query_pre, cosine, sine, w_expand, place_q, place_k, lse, attended_grad, *keys)


def one_hot(slot_ref):
    experts, rows = slot_ref.shape[0], slot_ref.shape[-1]
    place = lax.broadcasted_iota(jnp.int32, (SLOTS, rows), 0)
    return jnp.concatenate(
        [(slot_ref[e, 0] == place).astype(F32).astype(BF) for e in range(experts)], axis=0
    )


def pick_kernel(order_ref, slot_ref, x_ref, o_ref):
    o_ref[...] = mm(one_hot(slot_ref), x_ref[...], 1, 0).astype(BF).reshape(o_ref.shape)


def pick(order, slot, values):
    experts, blocks, _, rows = slot.shape
    width = values.shape[1]
    return pl.pallas_call(
        pick_kernel,
        name="pick",
        grid_spec=pltpu.PrefetchScalarGridSpec(
            num_scalar_prefetch=1,
            grid=(blocks,),
            in_specs=[
                pl.BlockSpec((experts, 1, 1, rows), lambda b, o: (0, b, 0, 0)),
                pl.BlockSpec((rows, width), lambda b, o: (o[b], 0)),
            ],
            out_specs=pl.BlockSpec((experts, 1, SLOTS, width), lambda b, o: (0, b, 0, 0)),
        ),
        out_shape=jax.ShapeDtypeStruct((experts, blocks, SLOTS, width), BF),
        compiler_params=params(),
        cost_estimate=cost(
            2 * experts * blocks * SLOTS * rows * width,
            2 * blocks * width * (rows + experts * SLOTS),
        ),
    )(order, slot, values)


def pick_route_kernel(count, pieces, first_ref, slot_ref, w_ref, *refs):
    o_ref, p_ref, g_ref = refs[-3:]
    experts, rows = slot_ref.shape[0], slot_ref.shape[3]
    for n in range(pieces):
        x = refs[n][...]
        logits = mm(x, w_ref[...], 1, 1)
        lane = lax.broadcasted_iota(jnp.int32, logits.shape, 1)
        logits = jnp.where(lane < count, logits, -1e30)
        e = jnp.exp(logits - jnp.max(logits, axis=-1, keepdims=True))
        probs = e / jnp.sum(e, axis=-1, keepdims=True)
        p_ref[n * rows : (n + 1) * rows, :] = probs
        high = probs.astype(BF)
        low = (probs - high.astype(F32)).astype(BF)
        place = lax.broadcasted_iota(jnp.int32, (SLOTS, rows), 0)
        chosen = jnp.concatenate(
            [(slot_ref[i, n] == place).astype(F32).astype(BF) for i in range(experts)], axis=0
        )
        picked = mm(chosen, x, 1, 0).astype(BF)
        o_ref[:, n] = picked.reshape(experts, SLOTS, -1)
        taken = mm(chosen, high, 1, 0) + mm(chosen, low, 1, 0)
        lane = lax.broadcasted_iota(jnp.int32, (SLOTS, taken.shape[1]), 1)
        for i in range(experts):
            part = taken[i * SLOTS : (i + 1) * SLOTS, :]
            g_ref[i, n] = jnp.sum(
                jnp.where(lane == first_ref[0] + i, part, 0.0), axis=-1, keepdims=True
            )


def pick_route(first, slot, values, router_rows, count, at, steps, earlier):
    experts, blocks, _, rows = slot.shape
    pieces = len(values)
    width = values[0].shape[1]
    lanes = router_rows.shape[0]
    at = at // pieces
    whole = pl.BlockSpec(memory_space=pl.ANY)
    return pl.pallas_call(
        functools.partial(pick_route_kernel, count, pieces),
        name="pick_route",
        grid=(steps,),
        in_specs=[
            smem(),
            pl.BlockSpec((experts, pieces, 1, rows), lambda b: (0, at + b, 0, 0)),
            fixed(router_rows.shape),
        ]
        + [pl.BlockSpec((rows, width), lambda b: (b, 0)) for _ in values]
        + [whole for _ in earlier],
        out_specs=[
            pl.BlockSpec((experts, pieces, SLOTS, width), lambda b: (0, at + b, 0, 0)),
            pl.BlockSpec((pieces * rows, lanes), lambda b: (at + b, 0)),
            pl.BlockSpec((experts, pieces, SLOTS, 1), lambda b: (0, at + b, 0, 0)),
        ],
        out_shape=[
            jax.ShapeDtypeStruct((experts, blocks, SLOTS, width), BF),
            jax.ShapeDtypeStruct((blocks * rows, lanes), F32),
            jax.ShapeDtypeStruct((experts, blocks, SLOTS, 1), F32),
        ],
        input_output_aliases={3 + pieces + i: i for i in range(len(earlier))},
        compiler_params=params(),
        cost_estimate=cost(
            pieces * steps * rows * width,
            pieces * steps * width * rows,
        ),
    )(first, slot, router_rows, *values, *earlier)


def put_kernel(order_ref, place_ref, r_ref, o_ref):
    o_ref[...] = mm(place_ref[0], r_ref[...].reshape(-1, r_ref.shape[-1]), 1, 0).astype(BF)


def put_route_kernel(order_ref, first_ref, place_ref, r_ref, p_ref, pg_ref, w_ref, o_ref, lg_ref):
    experts, rows = pg_ref.shape[0], pg_ref.shape[3]
    by_expert = jnp.concatenate(
        [pg_ref[i, 0] for i in range(experts)] + [jnp.zeros((1, rows), F32)] * (-experts % 8), axis=0
    )
    high = by_expert.astype(BF)
    low = (by_expert - high.astype(F32)).astype(BF)
    probs = p_ref[...]
    shape = (by_expert.shape[0], probs.shape[1])
    expert = lax.broadcasted_iota(jnp.int32, shape, 0)
    lane = lax.broadcasted_iota(jnp.int32, shape, 1)
    spread = (lane == first_ref[0] + expert) & (expert < experts)
    spread = spread.astype(F32).astype(BF)
    grad = mm(high, spread, 0, 0) + mm(low, spread, 0, 0)
    back = (probs * (grad - jnp.sum(probs * grad, axis=-1, keepdims=True))).astype(BF)
    lg_ref[...] = back
    total = mm(place_ref[0], r_ref[...].reshape(-1, r_ref.shape[-1]), 1, 0)
    o_ref[...] = (total + mm(back, w_ref[...], 1, 0)).astype(BF)


def put_specs(places, picked):
    blocks, rows, slots = places.shape
    experts, width = picked.shape[0], picked.shape[3]
    return [
        pl.BlockSpec((1, rows, slots), lambda b, o: (b, 0, 0)),
        pl.BlockSpec((experts, 1, SLOTS, width), lambda b, o: (0, b, 0, 0)),
    ]


def put_cost(places, width):
    blocks, rows, slots = places.shape
    return cost(2 * blocks * slots * rows * width, 2 * blocks * width * (rows + slots))


def put(order, places, picked):
    blocks, rows, _ = places.shape
    width = picked.shape[3]
    return pl.pallas_call(
        put_kernel,
        name="put",
        grid_spec=pltpu.PrefetchScalarGridSpec(
            num_scalar_prefetch=1,
            grid=(blocks,),
            in_specs=put_specs(places, picked),
            out_specs=pl.BlockSpec((rows, width), lambda b, o: (o[b], 0)),
        ),
        out_shape=jax.ShapeDtypeStruct((blocks * rows, width), BF),
        compiler_params=params(),
        cost_estimate=put_cost(places, width),
    )(order, places, picked)


def put_route(order, first, places, picked, probs, probs_grad, router_rows):
    blocks, rows, _ = places.shape
    experts, width = picked.shape[0], picked.shape[3]
    lanes = probs.shape[1]
    return pl.pallas_call(
        put_route_kernel,
        name="put_route",
        grid_spec=pltpu.PrefetchScalarGridSpec(
            num_scalar_prefetch=1,
            grid=(blocks,),
            in_specs=[smem()]
            + put_specs(places, picked)
            + [
                pl.BlockSpec((rows, lanes), lambda b, o: (b, 0)),
                pl.BlockSpec((experts, 1, 1, rows), lambda b, o: (0, b, 0, 0)),
                fixed(router_rows.shape),
            ],
            out_specs=[
                pl.BlockSpec((rows, width), lambda b, o: (o[b], 0)),
                pl.BlockSpec((rows, lanes), lambda b, o: (b, 0)),
            ],
        ),
        out_shape=[
            jax.ShapeDtypeStruct((blocks * rows, width), BF),
            jax.ShapeDtypeStruct((blocks * rows, lanes), BF),
        ],
        compiler_params=params(),
        cost_estimate=put_cost(places, width),
    )(order, first, places, picked, probs, probs_grad, router_rows)


def down_back_kernel(x_ref, w_ref, o_ref):
    ff = w_ref.shape[1]
    wide = o_ref.shape[-1]
    back = mm(x_ref[...].reshape(-1, x_ref.shape[-1]), w_ref[0], 1, 1)
    o_ref[0, :, :ff] = back
    if wide > ff:
        o_ref[0, :, ff:] = jnp.zeros((o_ref.shape[1], wide - ff), F32)


def down_back(rows, down):
    experts, blocks, slots, width = rows.shape
    ff = down.shape[1]
    wide = -(-ff // 128) * 128
    count = blocks * slots
    return pl.pallas_call(
        down_back_kernel,
        name="down_back",
        grid=(experts,),
        in_specs=[
            pl.BlockSpec((1, blocks, slots, width), lambda e: (e, 0, 0, 0)),
            pl.BlockSpec((1, ff, width), lambda e: (e, 0, 0)),
        ],
        out_specs=pl.BlockSpec((1, count, wide), lambda e: (e, 0, 0)),
        out_shape=jax.ShapeDtypeStruct((experts, count, wide), F32),
        compiler_params=params(),
        cost_estimate=cost(
            experts * count * width,
            experts * count * ff,
        ),
    )(rows, down)


def row_out_kernel(x_ref, w_ref, o_ref):
    ff = w_ref.shape[1]
    o_ref[...] = mm(x_ref[0, :, :ff], w_ref[0], 1, 0).astype(BF).reshape(o_ref.shape)


def row_out(active, down, blocks):
    experts, count, wide = active.shape
    ff, width = down.shape[1:]
    slots = count // blocks
    return pl.pallas_call(
        row_out_kernel,
        name="row_out",
        grid=(experts,),
        in_specs=[
            pl.BlockSpec((1, count, wide), lambda e: (e, 0, 0)),
            pl.BlockSpec((1, ff, width), lambda e: (e, 0, 0)),
        ],
        out_specs=pl.BlockSpec((1, blocks, slots, width), lambda e: (e, 0, 0, 0)),
        out_shape=jax.ShapeDtypeStruct((experts, blocks, slots, width), BF),
        compiler_params=params(),
        cost_estimate=cost(
            2 * experts * count * width * ff,
            2 * experts * (count * width + ff * width + count * wide),
        ),
    )(active, down)


def expert_kernel(
    x_ref, gate_ref, up_ref, back_ref, slot_ref, sg_ref,
    ga_ref, dg_ref, du_ref, dx_ref, pg_ref, w_ref, d_ref,
):
    ff = gate_ref.shape[1]
    wide = back_ref.shape[2]
    blocks, rows = slot_ref.shape[1], slot_ref.shape[3]

    @pl.when(pl.program_id(0) == 0)
    def _():
        w_ref[...] = jnp.zeros_like(w_ref)

    w_ref[:ff, :] = gate_ref[0]
    w_ref[wide : wide + ff, :] = up_ref[0]
    x = x_ref[...].reshape(-1, x_ref.shape[-1])
    both = mm(x, w_ref[...], 1, 1)
    a = both[:, :wide]
    b = both[:, wide:]
    place = lax.broadcasted_iota(jnp.int32, (SLOTS, rows), 0)
    slot_gate = sg_ref[...].reshape(-1, 1)
    back = back_ref[0]
    sig = jax.nn.sigmoid(a)
    swish = a * sig
    active = swish * b
    gate_grad = jnp.sum(active * back, axis=-1, keepdims=True)
    for i in range(blocks):
        part = gate_grad[i * SLOTS : (i + 1) * SLOTS, :]
        pg_ref[0, i] = jnp.sum(
            jnp.where(slot_ref[0, i] == place, part, 0.0), axis=0, keepdims=True
        )
    gated = back * slot_gate
    ga_ref[0] = (active * slot_gate).astype(BF)
    dg = (gated * b * (sig + swish * (1.0 - sig))).astype(BF)
    du = (gated * swish).astype(BF)
    dg_ref[0] = dg
    du_ref[0] = du
    d_ref[:, :wide] = dg
    d_ref[:, wide:] = du
    dx_ref[...] = mm(d_ref[...], w_ref[...], 1, 0).astype(BF).reshape(dx_ref.shape)


def expert_step(rows, gate_t, up_t, back, slot, slot_gates):
    experts, blocks, slots, width = rows.shape
    ff = gate_t.shape[1]
    wide = back.shape[2]
    count = blocks * slots
    whole = pl.BlockSpec((1, blocks, slots, width), lambda e: (e, 0, 0, 0))
    flat = lambda n: pl.BlockSpec((1, count, n), lambda e: (e, 0, 0))
    shape = lambda n, dtype: jax.ShapeDtypeStruct((experts, count, n), dtype)
    weight = pl.BlockSpec((1, ff, width), lambda e: (e, 0, 0))
    by_token = pl.BlockSpec((1,) + slot.shape[1:], lambda e: (e, 0, 0, 0))
    return pl.pallas_call(
        expert_kernel,
        name="expert_step",
        grid=(experts,),
        in_specs=[
            whole,
            weight,
            weight,
            flat(wide),
            by_token,
            pl.BlockSpec((1, blocks, slots, 1), lambda e: (e, 0, 0, 0)),
        ],
        out_specs=[flat(wide), flat(wide), flat(wide), whole, by_token],
        out_shape=[
            shape(wide, BF),
            shape(wide, BF),
            shape(wide, BF),
            jax.ShapeDtypeStruct(rows.shape, BF),
            jax.ShapeDtypeStruct(slot.shape, F32),
        ],
        scratch_shapes=[pltpu.VMEM((2 * wide, width), BF), pltpu.VMEM((count, 2 * wide), BF)],
        compiler_params=params(),
        cost_estimate=cost(
            8 * experts * count * width * wide,
            2 * experts * (2 * count * width + 2 * width * wide + 5 * count * wide),
            experts * count * wide,
        ),
    )(rows, gate_t, up_t, back, slot, slot_gates)


def norm_kernel(x_ref, add_ref, gain_ref, sum_ref, o_ref):
    x = x_ref[...].astype(F32) + add_ref[...].astype(F32)
    sum_ref[...] = x
    scale = lax.rsqrt(jnp.mean(x * x, axis=-1, keepdims=True) + epsilon)
    o_ref[...] = (x * scale * gain_ref[...]).astype(BF)


def norm_sum(values, added, gain):
    rows, width = values.shape
    block = pl.BlockSpec((rows // 4, width), lambda i: (i, 0))
    return pl.pallas_call(
        norm_kernel,
        name="norm_sum",
        grid=(4,),
        in_specs=[block, block, fixed((1, width))],
        out_specs=[block, block],
        out_shape=[
            jax.ShapeDtypeStruct((rows, width), F32),
            jax.ShapeDtypeStruct((rows, width), BF),
        ],
        compiler_params=params(),
        cost_estimate=cost(8 * rows * width, 10 * rows * width),
    )(values, added, gain.reshape(1, width))


def norm_back_kernel(x_ref, up_ref, res_ref, gain_ref, *outs):
    x = x_ref[...].astype(F32)
    up = up_ref[...].astype(F32)
    scale = lax.rsqrt(jnp.mean(x * x, axis=-1, keepdims=True) + epsilon)
    scaled = x * scale
    if len(outs) > 1:

        @pl.when(pl.program_id(0) == 0)
        def _():
            outs[2][...] = jnp.zeros_like(outs[2])

        outs[2][...] += jnp.sum(up * scaled, axis=0, keepdims=True)
    up = up * gain_ref[...]
    back = scale * (up - scaled * jnp.mean(up * scaled, axis=-1, keepdims=True))
    total = res_ref[...].astype(F32) + back
    outs[0][...] = total.astype(BF)
    if len(outs) > 1:
        outs[1][...] = total


def norm_back(values, upstream, residual, gain, last):
    rows, width = values.shape
    block = pl.BlockSpec((rows // 4, width), lambda i: (i, 0))
    specs = [block] if last else [block, block, fixed((1, width))]
    shapes = [jax.ShapeDtypeStruct((rows, width), BF)]
    if not last:
        shapes += [
            jax.ShapeDtypeStruct((rows, width), F32),
            jax.ShapeDtypeStruct((1, width), F32),
        ]
    return pl.pallas_call(
        norm_back_kernel,
        name="norm_back",
        grid=(4,),
        in_specs=[block, block, block, fixed((1, width))],
        out_specs=specs,
        out_shape=shapes,
        compiler_params=params(),
        cost_estimate=cost(12 * rows * width, 12 * rows * width),
    )(values, upstream, residual, gain.reshape(1, width))


def shared_kernel(x_ref, up_ref, wg_ref, wu_ref, wd_ref, act_ref, dg_ref, du_ref, grad_ref):
    ff = wd_ref.shape[0]
    x = x_ref[...]
    upstream = up_ref[...]
    a = mm(x, wg_ref[...], 1, 1)
    b = mm(x, wu_ref[...], 1, 1)
    back = mm(upstream, wd_ref[...], 1, 1)
    sig = jax.nn.sigmoid(a)
    swish = a * sig
    active = (swish * b).astype(BF)
    dg = (back * b * (sig + swish * (1.0 - sig))).astype(BF)
    du = (back * swish).astype(BF)
    act_ref[...] = active
    dg_ref[...] = dg
    du_ref[...] = du
    grad_ref[:ff, :] = mm(active, upstream, 0, 0).astype(BF)
    grad_ref[ff : 2 * ff, :] = mm(dg, x, 0, 0).astype(BF)
    grad_ref[2 * ff :, :] = mm(du, x, 0, 0).astype(BF)


def shared_step(values, upstream, gate_t, up_t, down):
    rows, width = values.shape
    ff = down.shape[0]
    inner = jax.ShapeDtypeStruct((rows, ff), BF)
    return pl.pallas_call(
        shared_kernel,
        name="shared_step",
        grid=(1,),
        in_specs=[fixed((rows, width))] * 2 + [fixed((ff, width))] * 3,
        out_specs=[fixed((rows, ff))] * 3 + [fixed((3 * ff, width))],
        out_shape=[inner, inner, inner, jax.ShapeDtypeStruct((3 * ff, width), BF)],
        compiler_params=params(),
        cost_estimate=cost(rows * width, rows * width),
    )(values, upstream, gate_t, up_t, down)


def dot(eq, a, b):
    return jnp.einsum(eq, a, b, preferred_element_type=F32)


def passed_along(shard, axis, by):
    peers = lax.axis_size(axis)
    pairs = [(i, i + by) for i in range(peers) if 0 <= i + by < peers]
    return lax.ppermute(shard, axis, pairs)


def normed(values, norm_gain):
    return (
        values * lax.rsqrt(jnp.mean(values * values, axis=-1, keepdims=True) + epsilon) * norm_gain
    )


def norm_backward(values, norm_gain, upstream):
    _, pullback = jax.vjp(normed, values, norm_gain)
    return pullback(upstream)


def rotate(values, cosine, sine):
    half = values.shape[-1] // 2
    front, back = values[..., :half], values[..., half:]
    return jnp.concatenate([front * cosine - back * sine, back * cosine + front * sine], axis=-1)


def rotate_back(upstream, cosine, sine):
    return rotate(upstream, cosine, -sine)


def silu_gate(gate_val, up_val):
    return gate_val * jax.nn.sigmoid(gate_val) * up_val


def silu_backward(gate_val, up_val, upstream):
    _, pullback = jax.vjp(silu_gate, gate_val, up_val)
    return pullback(upstream)


def rope_tables(seq_all, seq_here, index_here):
    starts = jnp.sum((seq_all[None, :] < seq_here[:, None]).astype(jnp.int32), axis=1)
    position = (index_here - starts).astype(F32)
    frequency = 10000.0 ** (-(jnp.arange(DR // 2, dtype=F32) * 2.0) / DR)
    angle = position[:, None] * frequency[None, :]
    return jnp.cos(angle), jnp.sin(angle)


def turned(value, by):
    return lax.ppermute(value, "dp", [(i, i ^ by) for i in range(lax.axis_size("dp"))])


def swapped(value):
    return turned(value, 1)


def after(value, *others):
    return lax.optimization_barrier((value,) + others)[0]


def scatter_sum(parts):
    joined = parts if not isinstance(parts, list) else jnp.concatenate(parts, axis=1)
    return lax.psum_scatter(joined, "dp", scatter_dimension=0, tiled=True)


def shards(
    tokens,
    seq_ids,
    route_ids,
    cotangent,
    input_gain,
    w_query,
    w_latent,
    latent_gain,
    w_expand,
    w_out,
    middle_gain,
    w_router,
    expert_gate,
    expert_up,
    expert_down,
    shared_gate,
    shared_up,
    shared_down,
):
    devices = lax.axis_size("dp")
    rank_dp = lax.axis_index("dp")
    tok_rows, width = tokens.shape
    experts_local = expert_gate.shape[0]
    all_experts = w_router.shape[1]
    ff_local = expert_gate.shape[2]
    heads_local = w_query.shape[1] // (DN + DR)

    direct = devices == 8
    apart = jnp.array([0, 1, 2, 4, 3, 5, 6, 7] if direct else list(range(devices)), jnp.int32)
    order = (rank_dp ^ apart) if direct else apart

    index_here = rank_dp * tok_rows + jnp.arange(tok_rows, dtype=jnp.int32)
    seq_here = lax.dynamic_slice_in_dim(seq_ids, rank_dp * tok_rows, tok_rows, 0)
    cosine, sine = rope_tables(seq_ids, seq_here, index_here)
    odd = rank_dp % 2
    blocks = [rank_dp - 4, rank_dp - 2, (rank_dp - 2) ^ 1, rank_dp - 3 + 2 * odd, rank_dp]
    seq_padded = jnp.concatenate([jnp.full((4 * tok_rows,), -1, jnp.int32), seq_ids])
    seq_keys = jnp.concatenate(
        [lax.dynamic_slice_in_dim(seq_padded, (at + 4) * tok_rows, tok_rows, 0) for at in blocks]
    )
    key_index = jnp.concatenate(
        [at * tok_rows + jnp.arange(tok_rows, dtype=jnp.int32) for at in blocks]
    )
    place_q = jnp.stack([seq_here, index_here], axis=1)
    place_k = jnp.stack([seq_keys, key_index], axis=0)

    token_features = tokens.astype(F32)
    hidden_in = normed(token_features, input_gain).astype(BF)
    latent_full = jnp.dot(hidden_in, w_latent, preferred_element_type=F32)
    latent_raw = latent_full[:, :KVR]
    latent = normed(latent_raw, latent_gain).astype(BF)
    rope_key = rotate(latent_full[:, KVR:], cosine, sine).astype(BF)
    fill = jnp.zeros((tok_rows, -(KVR + DR) % 128), BF)
    own_keys = jnp.concatenate([latent, rope_key, fill], axis=1)
    before_two = passed_along(own_keys, "dp", 2)
    before_four = passed_along(own_keys, "dp", 4)
    keys = [
        before_four,
        before_two,
        swapped(before_two),
        swapped(jnp.where(odd == 0, own_keys, before_four)),
        own_keys,
    ]
    cot_all = lax.all_gather(after(cotangent, before_two, before_four), "dp", tiled=True)
    query_pre = jnp.dot(hidden_in, w_query, preferred_element_type=F32)
    attended, lse = attend(query_pre, cosine, sine, w_expand, place_q, place_k, keys)
    attention_part = jnp.dot(attended, w_out, preferred_element_type=F32).astype(BF)
    attention = lax.psum(attention_part, "tensor")

    route_all = lax.all_gather(after(route_ids, attention_part), "dp", tiled=True)
    local_ids = rank_dp * experts_local + jnp.arange(experts_local, dtype=jnp.int32)
    routes = jnp.take(route_all.reshape(devices, tok_rows, -1), order, axis=0)
    named_block = jnp.any(routes[..., None] == local_ids, axis=2)
    before = jnp.tril(jnp.ones((tok_rows, tok_rows), BF), -1)
    rank_within = dot("ts,bse->bte", before, named_block.astype(BF))
    slot_of = jnp.where(named_block, rank_within, -1.0)
    slot = slot_of.astype(jnp.int32).transpose(2, 0, 1)[:, :, None, :]
    columns = jnp.arange(experts_local * SLOTS, dtype=jnp.int32)
    spread = (columns[None, :] // SLOTS == jnp.arange(experts_local, dtype=jnp.int32)[:, None]).astype(
        BF
    )
    places = (
        dot("bte,en->btn", slot_of.astype(BF), spread) == (columns % SLOTS).astype(F32)
    ).astype(BF)
    gate_t = expert_gate.swapaxes(1, 2)
    up_t = expert_up.swapaxes(1, 2)
    cot_rows = pick(order, slot, cot_all)
    back = down_back(cot_rows, expert_down)

    attention = after(attention, cot_rows, places)
    middle, hidden_mid = norm_sum(tokens, attention, middle_gain)
    first = (rank_dp * experts_local).astype(jnp.int32).reshape(1)
    router_rows = jnp.pad(w_router.T, ((0, -all_experts % 128), (0, 0)))
    if direct:
        half = tok_rows // 2
        pair = swapped(hidden_mid)
        by_x = turned(hidden_mid, 2)
        by_y = turned(hidden_mid, 4)
        held = pick_route(first, slot, [hidden_mid, pair], router_rows, all_experts, 0, 1, [])
    else:
        hidden_all = lax.all_gather(hidden_mid, "dp", tiled=True)

    hidden_shared = after(hidden_mid, pair) if direct else hidden_mid
    shared_active, shared_gate_grad, shared_up_grad, shared_grads = shared_step(
        hidden_shared, cotangent, shared_gate.T, shared_up.T, shared_down
    )
    shared_result = jnp.dot(shared_active, shared_down, preferred_element_type=F32)
    mid_from_shared = dot("tf,df->td", shared_gate_grad, shared_gate) + dot(
        "tf,df->td", shared_up_grad, shared_up
    )
    if direct:
        by_x, by_y = lax.optimization_barrier((by_x, by_y, held[0], back, shared_grads))[:2]
        pair_x, pair_y = swapped(by_x), swapped(by_y)
        top = turned(by_y[:half], 2)
        bottom = turned(by_x[half:], 4)
        held = pick_route(first, slot, [by_x, by_y], router_rows, all_experts, 2, 1, held)
        held = pick_route(first, slot, [pair_x, pair_y], router_rows, all_experts, 4, 1, held)
        corner = jnp.concatenate([after(top, held[0]), bottom], axis=0)
        pair_corner = swapped(corner)
        held = pick_route(first, slot, [corner], router_rows, all_experts, 6, 1, held)
        held = pick_route(first, slot, [pair_corner], router_rows, all_experts, 7, 1, held)
        rows, router_probs, slot_gates = held
        hidden_all = jnp.concatenate(
            [hidden_mid, pair, by_x, by_y, pair_x, pair_y, after(corner, rows), pair_corner], axis=0
        )
    else:
        rows, router_probs, slot_gates = pick_route(
            first, slot, [hidden_all], router_rows, all_experts, 0, devices, []
        )
    shared_sums = lax.psum_scatter(
        after(shared_grads, rows), "dp", scatter_dimension=1, tiled=True
    )
    gated_active, gate_val_grad, up_val_grad, row_grad, probs_grad = expert_step(
        rows, gate_t, up_t, back, slot, slot_gates
    )
    mid_part, logit_grad = put_route(
        order, first, places, row_grad, router_probs, probs_grad, router_rows
    )
    mid_part = after(mid_part, shared_sums)
    mid_block = lax.psum_scatter(mid_part, "dp", scatter_dimension=0, tiled=True)
    grad_router = dot("td,te->de", hidden_all, logit_grad[:, :all_experts]).astype(BF)
    routed_part = put(order, places, row_out(gated_active, expert_down, devices))
    rows_flat = rows.reshape(experts_local, -1, width)
    grad_expert_down = dot(
        "ecf,ecd->efd",
        gated_active[..., :ff_local],
        cot_rows.reshape(experts_local, -1, width),
    )
    grad_expert_gate = dot("ecd,ecf->edf", rows_flat, gate_val_grad[..., :ff_local])
    grad_expert_up = dot("ecd,ecf->edf", rows_flat, up_val_grad[..., :ff_local])

    routed_block = scatter_sum(routed_part)
    mid_block = after(mid_block, routed_part, grad_router, grad_expert_down)
    mid_grad = lax.psum((mid_block.astype(F32) + mid_from_shared).astype(BF), "tensor")
    mid_grad = after(mid_grad, grad_expert_gate, grad_expert_up)

    middle_low, middle_grad, grad_middle_gain = norm_back(
        middle, mid_grad, cotangent, middle_gain, False
    )
    attended_grad = dot("td,cd->tc", middle_low, w_out).astype(BF)
    query_grad, grad_expand, *window_grads = attend_back(
        query_pre, cosine, sine, w_expand, place_q, place_k, lse, attended_grad, keys
    )
    routed_block = after(routed_block, grad_expand)
    ff_part = (routed_block.astype(F32) + shared_result).astype(BF)
    window_grads = lax.optimization_barrier((*window_grads, ff_part))[:-1]
    four_grad, two_grad, pair_grad, last_grad, keys_grad = window_grads
    pair_grad = swapped(pair_grad)
    last_grad = swapped(last_grad).astype(F32)
    two_grad = (two_grad.astype(F32) + pair_grad.astype(F32)).astype(BF)
    four_grad = (four_grad.astype(F32) + jnp.where(odd == 1, last_grad, 0.0)).astype(BF)
    keys_grad = keys_grad + jnp.where(odd == 0, last_grad, 0.0)
    keys_grad = keys_grad + passed_along(two_grad, "dp", -2).astype(F32)
    keys_grad = keys_grad + passed_along(four_grad, "dp", -4).astype(F32)
    latent_raw_grad, grad_latent_gain = norm_backward(latent_raw, latent_gain, keys_grad[:, :KVR])
    rope_raw_grad = rotate_back(keys_grad[:, KVR : KVR + DR], cosine, sine)
    latent_full_grad = jnp.concatenate([latent_raw_grad, rope_raw_grad], axis=-1).astype(BF)
    input_part = dot("tc,dc->td", query_grad, w_query) + dot(
        "tc,dc->td", latent_full_grad, w_latent
    )
    _, grad_input_gain = norm_backward(token_features, input_gain, input_part)

    feedforward = lax.psum(ff_part, "tensor")
    output = (middle + feedforward.astype(F32)).astype(BF)
    input_part, grad_input_gain = lax.optimization_barrier((input_part.astype(BF), grad_input_gain))
    input_part = after(input_part, feedforward)
    tensors = lax.axis_size("tensor")
    query_width = heads_local * (DN + DR)
    out_width = heads_local * DV
    expand_width = w_expand.shape[1] * KVR // width
    latent_width = KVR + DR
    gains = jnp.concatenate(
        [
            grad_middle_gain / tensors,
            grad_input_gain[None, :],
            jnp.repeat(grad_latent_gain, width // KVR)[None, :],
            jnp.zeros((125, width), F32),
        ],
        axis=0,
    )
    parts = scatter_sum(
        [dot("td,tc->dc", hidden_in, latent_full_grad).astype(BF), grad_router, gains.astype(BF).T]
    )
    late = scatter_sum(
        [
            dot("td,tc->dc", middle_low, attended).astype(BF),
            dot("td,tc->dc", hidden_in, query_grad).astype(BF),
            after(grad_expand, keys_grad).reshape(width, expand_width),
        ]
    )
    input_grad, parts = lax.psum((input_part, parts), "tensor")
    parts = parts.astype(F32)
    (token_grad,) = norm_back(tokens, input_grad, middle_grad, input_gain, True)
    sw = shared_gate.shape[1]
    gain_at = latent_width + all_experts
    return (
        output,
        token_grad,
        parts[:, gain_at + 1],
        late[:, out_width : out_width + query_width].astype(F32),
        parts[:, :latent_width],
        parts[:: width // KVR, gain_at + 2],
        late[:, out_width + query_width :].astype(F32).reshape(KVR // devices, -1),
        late[:, :out_width].astype(F32).T,
        parts[:, gain_at],
        parts[:, latent_width:gain_at],
        grad_expert_gate,
        grad_expert_up,
        grad_expert_down,
        shared_sums[sw : 2 * sw].astype(F32).T,
        shared_sums[2 * sw :].astype(F32).T,
        shared_sums[:sw].astype(F32),
    )


def solution(mesh):
    placed = (
        P("dp", None),
        P(),
        P("dp", None),
        P("dp", None),
        P(),
        P(None, "tensor"),
        P(),
        P(),
        P(None, "tensor"),
        P("tensor", None),
        P(),
        P(),
        P("dp", None, "tensor"),
        P("dp", None, "tensor"),
        P("dp", "tensor", None),
        P(None, "tensor"),
        P(None, "tensor"),
        P("tensor", None),
    )
    return jax.shard_map(
        shards,
        mesh=mesh,
        in_specs=placed,
        out_specs=(
            P("dp", None),
            P("dp", None),
            P("dp"),
            P("dp", "tensor"),
            P("dp", None),
            P("dp"),
            P("dp", "tensor"),
            P("tensor", "dp"),
            P("dp"),
            P("dp", None),
            P("dp", None, "tensor"),
            P("dp", None, "tensor"),
            P("dp", "tensor", None),
            P("dp", "tensor"),
            P("dp", "tensor"),
            P("tensor", "dp"),
        ),
        check_vma=False,
    )
```

```python
import functools

import jax
import jax.numpy as jnp
from jax import lax
from jax.experimental import pallas as pl
from jax.experimental.pallas import tpu as pltpu
from jax.sharding import PartitionSpec as P

DN = 128
DR = 64
DV = 128
KVR = 512
REACH = 4
SLOTS = 80
BF = jnp.bfloat16
F32 = jnp.float32
VMEM_BYTES = 60 * 1024 * 1024
epsilon = 1e-06


def mm(a, b, ca, cb):
    return lax.dot_general(a, b, (((ca,), (cb,)), ((), ())), preferred_element_type=F32)


def cost(flops, nbytes, trans=0):
    return pl.CostEstimate(flops=int(flops), bytes_accessed=int(nbytes), transcendentals=int(trans))


def smem():
    return pl.BlockSpec(memory_space=pltpu.SMEM)


def fixed(shape):
    return pl.BlockSpec(shape, lambda *at: (0,) * len(shape))


def params():
    return pltpu.CompilerParams(vmem_limit_bytes=VMEM_BYTES)


def attend_setup(
    head, heads, step, qp_ref, cos_ref, sin_ref, at_ref, sq_ref, seq_ref, keys, q_ref, key_ref, bias_ref
):
    rows = qp_ref.shape[0]

    @pl.when(head == 0)
    def _():
        for at in range(0, rows, step):
            part = pl.ds(at, step)
            for i in range(len(keys)):
                block = at_ref[i]
                where = pl.multiple_of(jnp.maximum(block, 0) * rows, 128)
                sequence = jnp.where(block >= 0, seq_ref[0:1, pl.ds(where, rows)], -1)
                position = block * rows + lax.broadcasted_iota(jnp.int32, (1, rows), 1)
                allowed = (sq_ref[part, 0:1] == sequence) & (position <= sq_ref[part, 1:2])
                bias_ref[part, i * rows : (i + 1) * rows] = jnp.where(allowed, 0.0, -1e30).astype(BF)
        for i, key in enumerate(keys):
            key_ref[i * rows : (i + 1) * rows, DN:] = key[:, KVR : KVR + DR]

    for k in range(heads):

        @pl.when(head == k)
        def _():
            at = k * (DN + DR)
            front = qp_ref[:, at + DN : at + DN + DR // 2]
            back = qp_ref[:, at + DN + DR // 2 : at + DN + DR]
            cosine, sine = cos_ref[...], sin_ref[...]
            q_ref[:, :DN] = qp_ref[:, at : at + DN].astype(BF)
            q_ref[:, DN : DN + DR // 2] = (front * cosine - back * sine).astype(BF)
            q_ref[:, DN + DR // 2 :] = (back * cosine + front * sine).astype(BF)


def attend_kernel(heads, step, qp_ref, cos_ref, sin_ref, wx_ref, at_ref, sq_ref, seq_ref, *rest):
    keys, (o_ref, lse_ref, kv_ref, q_ref, key_ref, bias_ref) = rest[:-6], rest[-6:]
    rows = qp_ref.shape[0]
    scale = (DN + DR) ** (-0.5)
    attend_setup(
        pl.program_id(0), heads, step, qp_ref, cos_ref, sin_ref, at_ref, sq_ref, seq_ref, keys,
        q_ref, key_ref, bias_ref,
    )
    for i, key in enumerate(keys):
        part = pl.ds(i * rows, rows)
        kv = mm(key[:, :KVR], wx_ref[...], 1, 0).astype(BF)
        kv_ref[part, :] = kv
        key_ref[part, :DN] = kv[:, :DN]
    for at in range(0, rows, step):
        part = pl.ds(at, step)
        s = mm(q_ref[part, :], key_ref[...], 1, 1) * scale + bias_ref[part, :].astype(F32)
        top = jnp.max(s, axis=-1, keepdims=True)
        p = jnp.exp(s - top)
        total = jnp.sum(p, axis=-1, keepdims=True)
        o_ref[part, :] = mm((p * (1.0 / total)).astype(BF), kv_ref[:, DN:], 1, 0).astype(BF)
        lse_ref[0, part, :] = top + jnp.log(total)


def attend_specs(query_pre, cosine, w_expand, blocks, place_q, sequences, keys):
    return [
        fixed(query_pre.shape),
        fixed(cosine.shape),
        fixed(cosine.shape),
        pl.BlockSpec((KVR, DN + DV), lambda h: (0, h)),
        smem(),
        fixed(place_q.shape),
        fixed(sequences.shape),
    ], [fixed(keys[0].shape) for _ in keys]


def attend(query_pre, cosine, sine, w_expand, blocks, place_q, sequences, keys):
    rows = query_pre.shape[0]
    heads = query_pre.shape[1] // (DN + DR)
    window = rows * len(keys)
    specs, key_specs = attend_specs(query_pre, cosine, w_expand, blocks, place_q, sequences, keys)
    return pl.pallas_call(
        functools.partial(attend_kernel, heads, rows // 2),
        name="attend",
        grid=(heads,),
        in_specs=specs + key_specs,
        out_specs=[
            pl.BlockSpec((rows, DV), lambda h: (0, h)),
            pl.BlockSpec((1, rows, 1), lambda h: (h, 0, 0)),
            pl.BlockSpec((window, DN + DV), lambda h: (0, h)),
        ],
        out_shape=[
            jax.ShapeDtypeStruct((rows, heads * DV), BF),
            jax.ShapeDtypeStruct((heads, rows, 1), F32),
            jax.ShapeDtypeStruct((window, heads * (DN + DV)), BF),
        ],
        scratch_shapes=[
            pltpu.VMEM((rows, DN + DR), BF),
            pltpu.VMEM((window, DN + DR), BF),
            pltpu.VMEM((rows, window), BF),
        ],
        compiler_params=params(),
        cost_estimate=cost(
            2 * heads * window * (rows * 384 + KVR * 256), 2 * window * 640, heads * rows * window
        ),
    )(query_pre, cosine, sine, w_expand, blocks, place_q, sequences, *keys)


def attend_back_kernel(
    heads, step, count, qp_ref, cos_ref, sin_ref, wx_ref, at_ref, sq_ref, seq_ref, lse_ref, do_ref, kv_ref,
    *rest
):
    keys, rest = rest[:count], rest[count:]
    dq_ref, dkv_ref = rest[:2]
    grads = rest[2 : 2 + count]
    q_ref, key_ref, bias_ref, dk_ref, dv_ref, acc_ref, dqs_ref = rest[2 + count :]
    rows = qp_ref.shape[0]
    head = pl.program_id(0)
    scale = (DN + DR) ** (-0.5)
    attend_setup(
        head, heads, step, qp_ref, cos_ref, sin_ref, at_ref, sq_ref, seq_ref, keys, q_ref, key_ref, bias_ref
    )
    key_ref[:, :DN] = kv_ref[:, :DN]

    @pl.when(head == 0)
    def _():
        acc_ref[...] = jnp.zeros_like(acc_ref)

    for at in range(0, rows, step):
        part = pl.ds(at, step)
        q = q_ref[part, :]
        do = do_ref[part, :]
        s = mm(q, key_ref[...], 1, 1) * scale + bias_ref[part, :].astype(F32)
        p = jnp.exp(s - lse_ref[0, part, :])
        dp = mm(do, kv_ref[:, DN:], 1, 1)
        ds = (p * (dp - jnp.sum(p * dp, axis=-1, keepdims=True))).astype(BF)
        dqs_ref[part, :] = mm(ds, key_ref[...], 1, 0) * scale
        dk = mm(ds, q, 0, 0) * scale
        dv = mm(p.astype(BF), do, 0, 0)
        if at == 0:
            dk_ref[...] = dk
            dv_ref[...] = dv
        else:
            dk_ref[...] += dk
            dv_ref[...] += dv
    dkv_ref[:, :DN] = dk_ref[:, :DN].astype(BF)
    dkv_ref[:, DN:] = dv_ref[...].astype(BF)
    acc_ref[:, :KVR] += mm(dkv_ref[...], wx_ref[...], 1, 1)
    acc_ref[:, KVR : KVR + DR] += dk_ref[:, DN:]
    for k in range(heads):

        @pl.when(head == k)
        def _():
            at = k * (DN + DR)
            front = dqs_ref[:, DN : DN + DR // 2]
            back = dqs_ref[:, DN + DR // 2 :]
            cosine, sine = cos_ref[...], sin_ref[...]
            dq_ref[:, at : at + DN] = dqs_ref[:, :DN].astype(BF)
            dq_ref[:, at + DN : at + DN + DR // 2] = (front * cosine + back * sine).astype(BF)
            dq_ref[:, at + DN + DR // 2 : at + DN + DR] = (back * cosine - front * sine).astype(BF)

    @pl.when(head == heads - 1)
    def _():
        for i, grad in enumerate(grads):
            grad[...] = acc_ref[i * rows : (i + 1) * rows, :].astype(grad.dtype)


def attend_back(query_pre, cosine, sine, w_expand, blocks, place_q, sequences, lse, attended_grad, kv, keys):
    rows = query_pre.shape[0]
    heads = query_pre.shape[1] // (DN + DR)
    window = rows * len(keys)
    count = len(keys)
    specs, key_specs = attend_specs(query_pre, cosine, w_expand, blocks, place_q, sequences, keys)
    wide = keys[0].shape[1]
    return pl.pallas_call(
        functools.partial(attend_back_kernel, heads, rows // 2, count),
        name="attend_back",
        grid=(heads,),
        in_specs=specs
        + [
            pl.BlockSpec((1, rows, 1), lambda h: (h, 0, 0)),
            pl.BlockSpec((rows, DV), lambda h: (0, h)),
            pl.BlockSpec((window, DN + DV), lambda h: (0, h)),
        ]
        + key_specs,
        out_specs=[fixed(query_pre.shape), pl.BlockSpec((window, DN + DV), lambda h: (0, h))]
        + [fixed((rows, wide)) for _ in keys],
        out_shape=[
            jax.ShapeDtypeStruct(query_pre.shape, BF),
            jax.ShapeDtypeStruct((window, w_expand.shape[1]), BF),
        ]
        + [jax.ShapeDtypeStruct((rows, wide), BF) for _ in keys[1:]]
        + [jax.ShapeDtypeStruct((rows, wide), F32)],
        scratch_shapes=[
            pltpu.VMEM((rows, DN + DR), BF),
            pltpu.VMEM((window, DN + DR), BF),
            pltpu.VMEM((rows, window), BF),
            pltpu.VMEM((window, DN + DR), F32),
            pltpu.VMEM((window, DV), F32),
            pltpu.VMEM((window, wide), F32),
            pltpu.VMEM((rows, DN + DR), F32),
        ],
        compiler_params=params(),
        cost_estimate=cost(
            2 * heads * window * (rows * 1024 + KVR * 768), 4 * window * 640, heads * rows * window
        ),
    )(query_pre, cosine, sine, w_expand, blocks, place_q, sequences, lse, attended_grad, kv, *keys)


def one_hot(slot_ref):
    experts, rows = slot_ref.shape[0], slot_ref.shape[-1]
    place = lax.broadcasted_iota(jnp.int32, (SLOTS, rows), 0)
    return jnp.concatenate(
        [(slot_ref[e, 0] == place).astype(F32).astype(BF) for e in range(experts)], axis=0
    )


def pick_kernel(order_ref, slot_ref, x_ref, o_ref):
    o_ref[...] = mm(one_hot(slot_ref), x_ref[...], 1, 0).astype(BF).reshape(o_ref.shape)


def pick(order, slot, values):
    experts, blocks, _, rows = slot.shape
    width = values.shape[1]
    return pl.pallas_call(
        pick_kernel,
        name="pick",
        grid_spec=pltpu.PrefetchScalarGridSpec(
            num_scalar_prefetch=1,
            grid=(blocks,),
            in_specs=[
                pl.BlockSpec((experts, 1, 1, rows), lambda b, o: (0, b, 0, 0)),
                pl.BlockSpec((rows, width), lambda b, o: (o[b], 0)),
            ],
            out_specs=pl.BlockSpec((experts, 1, SLOTS, width), lambda b, o: (0, b, 0, 0)),
        ),
        out_shape=jax.ShapeDtypeStruct((experts, blocks, SLOTS, width), BF),
        compiler_params=params(),
        cost_estimate=cost(
            2 * experts * blocks * SLOTS * rows * width,
            2 * blocks * width * (rows + experts * SLOTS),
        ),
    )(order, slot, values)


def pick_route_kernel(count, pieces, parts, first_ref, slot_ref, w_ref, *refs):
    o_ref, p_ref, g_ref = refs[-3:]
    experts, rows = slot_ref.shape[0], slot_ref.shape[3]
    size = rows // parts
    for n in range(pieces):
        place = lax.broadcasted_iota(jnp.int32, (SLOTS, rows), 0)
        chosen = jnp.concatenate(
            [(slot_ref[i, n] == place).astype(F32).astype(BF) for i in range(experts)], axis=0
        )
        picked, taken = 0.0, 0.0
        for m in range(parts):
            x = refs[n * parts + m][...]
            logits = mm(x, w_ref[...], 1, 1)
            lane = lax.broadcasted_iota(jnp.int32, logits.shape, 1)
            logits = jnp.where(lane < count, logits, -1e30)
            e = jnp.exp(logits - jnp.max(logits, axis=-1, keepdims=True))
            probs = e / jnp.sum(e, axis=-1, keepdims=True)
            p_ref[n * rows + m * size : n * rows + (m + 1) * size, :] = probs
            high = probs.astype(BF)
            low = (probs - high.astype(F32)).astype(BF)
            part = chosen[:, m * size : (m + 1) * size]
            picked += mm(part, x, 1, 0)
            taken += mm(part, high, 1, 0) + mm(part, low, 1, 0)
        o_ref[:, n] = picked.astype(BF).reshape(experts, SLOTS, -1)
        lane = lax.broadcasted_iota(jnp.int32, (SLOTS, taken.shape[1]), 1)
        for i in range(experts):
            part = taken[i * SLOTS : (i + 1) * SLOTS, :]
            g_ref[i, n] = jnp.sum(
                jnp.where(lane == first_ref[0] + i, part, 0.0), axis=-1, keepdims=True
            )


def pick_route(first, slot, values, router_rows, count, at, steps, earlier):
    experts, blocks, _, rows = slot.shape
    parts = len(values[0])
    pieces = len(values)
    values = [part for value in values for part in value]
    width = values[0].shape[1]
    lanes = router_rows.shape[0]
    at = at // pieces
    whole = pl.BlockSpec(memory_space=pl.ANY)
    return pl.pallas_call(
        functools.partial(pick_route_kernel, count, pieces, parts),
        name="pick_route",
        grid=(steps,),
        in_specs=[
            smem(),
            pl.BlockSpec((experts, pieces, 1, rows), lambda b: (0, at + b, 0, 0)),
            fixed(router_rows.shape),
        ]
        + [pl.BlockSpec((rows // parts, width), lambda b: (b, 0)) for _ in values]
        + [whole for _ in earlier],
        out_specs=[
            pl.BlockSpec((experts, pieces, SLOTS, width), lambda b: (0, at + b, 0, 0)),
            pl.BlockSpec((pieces * rows, lanes), lambda b: (at + b, 0)),
            pl.BlockSpec((experts, pieces, SLOTS, 1), lambda b: (0, at + b, 0, 0)),
        ],
        out_shape=[
            jax.ShapeDtypeStruct((experts, blocks, SLOTS, width), BF),
            jax.ShapeDtypeStruct((blocks * rows, lanes), F32),
            jax.ShapeDtypeStruct((experts, blocks, SLOTS, 1), F32),
        ],
        input_output_aliases={3 + len(values) + i: i for i in range(len(earlier))},
        compiler_params=params(),
        cost_estimate=cost(pieces * steps * rows * width, pieces * steps * width * rows),
    )(first, slot, router_rows, *values, *earlier)


def route_grad_kernel(count, *refs):
    total = 0.0
    grads, values = refs[:count], refs[count:-1]
    which, at = 0, 0
    for ref in values:
        size = ref.shape[0]
        total += mm(grads[which][at : at + size, :], ref[...], 0, 0)
        at += size
        if at == grads[which].shape[0]:
            which, at = which + 1, 0
    refs[-1][...] = total.astype(BF)


def route_grad(grads, values):
    width = values[0].shape[1]
    lanes = grads[0].shape[1]
    return pl.pallas_call(
        functools.partial(route_grad_kernel, len(grads)),
        name="route_grad",
        grid=(1,),
        in_specs=[fixed(array.shape) for array in [*grads, *values]],
        out_specs=fixed((lanes, width)),
        out_shape=jax.ShapeDtypeStruct((lanes, width), BF),
        compiler_params=params(),
        cost_estimate=cost(lanes * width, lanes * width),
    )(*grads, *values)


def parts_kernel(lg_ref, x_ref, route_ref, gain_ref, o_ref):
    inner = lg_ref.shape[1]
    count = o_ref.shape[0] - inner - gain_ref.shape[0]
    o_ref[:inner, :] = mm(lg_ref[...], x_ref[...], 0, 0).astype(BF)
    o_ref[inner : inner + count, :] = route_ref[:count, :]
    o_ref[inner + count :, :] = gain_ref[...].astype(BF)


def parts_rows(latent_grad, values, route, gains, count):
    width = values.shape[1]
    shape = (latent_grad.shape[1] + count + gains.shape[0], width)
    return pl.pallas_call(
        parts_kernel,
        name="parts_rows",
        grid=(1,),
        in_specs=[fixed(array.shape) for array in (latent_grad, values, route, gains)],
        out_specs=fixed(shape),
        out_shape=jax.ShapeDtypeStruct(shape, BF),
        compiler_params=params(),
        cost_estimate=cost(width, width),
    )(latent_grad, values, route, gains)


def put_kernel(order_ref, place_ref, r_ref, o_ref):
    o_ref[...] = mm(place_ref[0], r_ref[...].reshape(-1, r_ref.shape[-1]), 1, 0).astype(BF)


def returned(first_ref, place_ref, r_ref, p_ref, pg_ref, w_ref):
    experts, rows = pg_ref.shape[0], pg_ref.shape[3]
    by_expert = jnp.concatenate(
        [pg_ref[i, 0] for i in range(experts)] + [jnp.zeros((1, rows), F32)] * (-experts % 8), axis=0
    )
    high = by_expert.astype(BF)
    low = (by_expert - high.astype(F32)).astype(BF)
    probs = p_ref[...]
    shape = (by_expert.shape[0], probs.shape[1])
    expert = lax.broadcasted_iota(jnp.int32, shape, 0)
    lane = lax.broadcasted_iota(jnp.int32, shape, 1)
    spread = (lane == first_ref[0] + expert) & (expert < experts)
    spread = spread.astype(F32).astype(BF)
    grad = mm(high, spread, 0, 0) + mm(low, spread, 0, 0)
    back = (probs * (grad - jnp.sum(probs * grad, axis=-1, keepdims=True))).astype(BF)
    total = mm(place_ref[0], r_ref[...].reshape(-1, r_ref.shape[-1]), 1, 0)
    return total + mm(back, w_ref[...], 1, 0), back


def put_route_kernel(
    order_ref, first_ref, place_ref, r_ref, p_ref, pg_ref, w_ref, *rest
):
    total, back = returned(first_ref, place_ref, r_ref, p_ref, pg_ref, w_ref)
    if len(rest) == 3:
        total += rest[0][...].astype(F32)
    rest[-2][...] = total.astype(BF)
    rest[-1][...] = back


def put_cross_kernel(
    order_ref, first_ref, place_ref, r_ref, p_ref, pg_ref, w_ref, add_ref,
    sx_ref, sy_ref, keep_ref, lg_ref,
):
    total, back = returned(first_ref, place_ref, r_ref, p_ref, pg_ref, w_ref)
    lg_ref[...] = back
    total = (total + add_ref[...].astype(F32)).astype(BF)
    half = total.shape[0] // 2
    top, bottom = total[:half], total[half:]
    step = pl.program_id(0)

    @pl.when(step == 0)
    def _():
        sx_ref[half:, :] = top
        keep_ref[half:, :] = bottom

    @pl.when(step == 1)
    def _():
        sy_ref[half:, :] = bottom
        keep_ref[:half, :] = top

    @pl.when(step == 2)
    def _():
        sx_ref[:half, :] = top
        sy_ref[:half, :] = bottom


def put_specs(places, picked):
    blocks, rows, slots = places.shape
    experts, width = picked.shape[0], picked.shape[3]
    return [
        pl.BlockSpec((1, rows, slots), lambda b, o: (b, 0, 0)),
        pl.BlockSpec((experts, 1, SLOTS, width), lambda b, o: (0, b, 0, 0)),
    ]


def put(order, places, picked):
    blocks, rows, _ = places.shape
    width = picked.shape[3]
    return pl.pallas_call(
        put_kernel,
        name="put",
        grid_spec=pltpu.PrefetchScalarGridSpec(
            num_scalar_prefetch=1,
            grid=(blocks,),
            in_specs=put_specs(places, picked),
            out_specs=pl.BlockSpec((rows, width), lambda b, o: (o[b], 0)),
        ),
        out_shape=jax.ShapeDtypeStruct((blocks * rows, width), BF),
        compiler_params=params(),
        cost_estimate=cost(blocks * rows * width, blocks * rows * width),
    )(order, places, picked)


def put_route(order, absolute, first, places, picked, probs, probs_grad, router_rows, added):
    _, rows, slots = places.shape
    blocks = order.shape[0]
    experts, width = picked.shape[0], picked.shape[3]
    lanes = probs.shape[1]
    come = (lambda b, o: b) if absolute else (lambda b, o: o[b])
    go = (lambda b, o: o[b]) if absolute else (lambda b, o: b)
    cross = added is not None and blocks == 3
    whole = pl.BlockSpec((rows, width), lambda b, o: (0, 0))
    out_specs = [whole] * 3 if cross else [pl.BlockSpec((rows, width), lambda b, o: (go(b, o), 0))]
    sizes = [rows] * 3 if cross else [blocks * rows]
    more = [] if added is None else [added]
    return pl.pallas_call(
        put_cross_kernel if cross else put_route_kernel,
        name="put_route",
        grid_spec=pltpu.PrefetchScalarGridSpec(
            num_scalar_prefetch=1,
            grid=(blocks,),
            in_specs=[
                smem(),
                pl.BlockSpec((1, rows, slots), lambda b, o: (come(b, o), 0, 0)),
                pl.BlockSpec((experts, 1, SLOTS, width), lambda b, o: (0, come(b, o), 0, 0)),
                pl.BlockSpec((rows, lanes), lambda b, o: (come(b, o), 0)),
                pl.BlockSpec((experts, 1, 1, rows), lambda b, o: (0, come(b, o), 0, 0)),
                fixed(router_rows.shape),
            ]
            + [pl.BlockSpec((rows, width), lambda b, o: (b, 0)) for _ in more],
            out_specs=out_specs + [pl.BlockSpec((rows, lanes), lambda b, o: (b, 0))],
        ),
        out_shape=[jax.ShapeDtypeStruct((size, width), BF) for size in sizes]
        + [jax.ShapeDtypeStruct((blocks * rows, lanes), BF)],
        compiler_params=params(),
        cost_estimate=cost(blocks * rows * width, blocks * rows * width),
    )(order, first, places, picked, probs, probs_grad, router_rows, *more)


def down_back_kernel(x_ref, w_ref, o_ref):
    ff = w_ref.shape[1]
    wide = o_ref.shape[-1]
    back = mm(x_ref[...].reshape(-1, x_ref.shape[-1]), w_ref[0], 1, 1)
    o_ref[0, :, :ff] = back
    if wide > ff:
        o_ref[0, :, ff:] = jnp.zeros((o_ref.shape[1], wide - ff), F32)


def down_back(rows, down):
    experts, blocks, slots, width = rows.shape
    ff = down.shape[1]
    wide = -(-ff // 128) * 128
    count = blocks * slots
    return pl.pallas_call(
        down_back_kernel,
        name="down_back",
        grid=(experts,),
        in_specs=[
            pl.BlockSpec((1, blocks, slots, width), lambda e: (e, 0, 0, 0)),
            pl.BlockSpec((1, ff, width), lambda e: (e, 0, 0)),
        ],
        out_specs=pl.BlockSpec((1, count, wide), lambda e: (e, 0, 0)),
        out_shape=jax.ShapeDtypeStruct((experts, count, wide), F32),
        compiler_params=params(),
        cost_estimate=cost(
            experts * count * width,
            experts * count * ff,
        ),
    )(rows, down)


def row_out_kernel(x_ref, w_ref, o_ref):
    ff = w_ref.shape[1]
    o_ref[...] = mm(x_ref[0, :, :ff], w_ref[0], 1, 0).astype(BF).reshape(o_ref.shape)


def row_out(active, down, blocks):
    experts, count, wide = active.shape
    ff, width = down.shape[1:]
    slots = count // blocks
    return pl.pallas_call(
        row_out_kernel,
        name="row_out",
        grid=(experts,),
        in_specs=[
            pl.BlockSpec((1, count, wide), lambda e: (e, 0, 0)),
            pl.BlockSpec((1, ff, width), lambda e: (e, 0, 0)),
        ],
        out_specs=pl.BlockSpec((1, blocks, slots, width), lambda e: (e, 0, 0, 0)),
        out_shape=jax.ShapeDtypeStruct((experts, blocks, slots, width), BF),
        compiler_params=params(),
        cost_estimate=cost(count * width, count * width),
    )(active, down)


def expert_kernel(
    x_ref, gate_ref, up_ref, back_ref, slot_ref, sg_ref,
    ga_ref, dg_ref, du_ref, dx_ref, pg_ref, w_ref, d_ref,
):
    ff = gate_ref.shape[1]
    wide = back_ref.shape[2]
    blocks, rows = slot_ref.shape[1], slot_ref.shape[3]

    @pl.when(pl.program_id(0) == 0)
    def _():
        w_ref[...] = jnp.zeros_like(w_ref)

    w_ref[:ff, :] = gate_ref[0]
    w_ref[wide : wide + ff, :] = up_ref[0]
    x = x_ref[...].reshape(-1, x_ref.shape[-1])
    both = mm(x, w_ref[...], 1, 1)
    a = both[:, :wide]
    b = both[:, wide:]
    place = lax.broadcasted_iota(jnp.int32, (SLOTS, rows), 0)
    slot_gate = sg_ref[...].reshape(-1, 1)
    back = back_ref[0]
    sig = jax.nn.sigmoid(a)
    swish = a * sig
    active = swish * b
    gate_grad = jnp.sum(active * back, axis=-1, keepdims=True)
    for i in range(blocks):
        part = gate_grad[i * SLOTS : (i + 1) * SLOTS, :]
        pg_ref[0, i] = jnp.sum(
            jnp.where(slot_ref[0, i] == place, part, 0.0), axis=0, keepdims=True
        )
    gated = back * slot_gate
    ga_ref[0] = (active * slot_gate).astype(BF)
    dg = (gated * b * (sig + swish * (1.0 - sig))).astype(BF)
    du = (gated * swish).astype(BF)
    dg_ref[0] = dg
    du_ref[0] = du
    d_ref[:, :wide] = dg
    d_ref[:, wide:] = du
    dx_ref[...] = mm(d_ref[...], w_ref[...], 1, 0).astype(BF).reshape(dx_ref.shape)


def expert_step(rows, gate_t, up_t, back, slot, slot_gates):
    experts, blocks, slots, width = rows.shape
    ff = gate_t.shape[1]
    wide = back.shape[2]
    count = blocks * slots
    whole = pl.BlockSpec((1, blocks, slots, width), lambda e: (e, 0, 0, 0))
    flat = lambda n: pl.BlockSpec((1, count, n), lambda e: (e, 0, 0))
    shape = lambda n, dtype: jax.ShapeDtypeStruct((experts, count, n), dtype)
    weight = pl.BlockSpec((1, ff, width), lambda e: (e, 0, 0))
    by_token = pl.BlockSpec((1,) + slot.shape[1:], lambda e: (e, 0, 0, 0))
    return pl.pallas_call(
        expert_kernel,
        name="expert_step",
        grid=(experts,),
        in_specs=[
            whole,
            weight,
            weight,
            flat(wide),
            by_token,
            pl.BlockSpec((1, blocks, slots, 1), lambda e: (e, 0, 0, 0)),
        ],
        out_specs=[flat(wide), flat(wide), flat(wide), whole, by_token],
        out_shape=[
            shape(wide, BF),
            shape(wide, BF),
            shape(wide, BF),
            jax.ShapeDtypeStruct(rows.shape, BF),
            jax.ShapeDtypeStruct(slot.shape, F32),
        ],
        scratch_shapes=[pltpu.VMEM((2 * wide, width), BF), pltpu.VMEM((count, 2 * wide), BF)],
        compiler_params=params(),
        cost_estimate=cost(
            8 * experts * count * width * wide,
            2 * experts * (2 * count * width + 2 * width * wide + 5 * count * wide),
            experts * count * wide,
        ),
    )(rows, gate_t, up_t, back, slot, slot_gates)


def norm_kernel(x_ref, add_ref, gain_ref, sum_ref, top_ref, bottom_ref):
    x = x_ref[...].astype(F32) + add_ref[...].astype(F32)
    sum_ref[...] = x
    scale = lax.rsqrt(jnp.mean(x * x, axis=-1, keepdims=True) + epsilon)
    out = (x * scale * gain_ref[...]).astype(BF)

    @pl.when(pl.program_id(0) < 2)
    def _():
        top_ref[...] = out

    @pl.when(pl.program_id(0) >= 2)
    def _():
        bottom_ref[...] = out


def norm_sum(values, added, gain):
    rows, width = values.shape
    block = pl.BlockSpec((rows // 4, width), lambda i: (i, 0))
    half = jax.ShapeDtypeStruct((rows // 2, width), BF)
    return pl.pallas_call(
        norm_kernel,
        name="norm_sum",
        grid=(4,),
        in_specs=[block, block, fixed((1, width))],
        out_specs=[
            block,
            pl.BlockSpec((rows // 4, width), lambda i: (jnp.minimum(i, 1), 0)),
            pl.BlockSpec((rows // 4, width), lambda i: (jnp.maximum(i - 2, 0), 0)),
        ],
        out_shape=[jax.ShapeDtypeStruct((rows, width), F32), half, half],
        compiler_params=params(),
        cost_estimate=cost(8 * rows * width, 10 * rows * width),
    )(values, added, gain.reshape(1, width))


def norm_back_kernel(x_ref, up_ref, res_ref, gain_ref, *rest):
    x = x_ref[...].astype(F32)
    up = up_ref[...].astype(F32)
    scale = lax.rsqrt(jnp.mean(x * x, axis=-1, keepdims=True) + epsilon)
    scaled = x * scale
    if len(rest) > 1:
        gain_grad_ref = rest[4]

        @pl.when(pl.program_id(0) == 0)
        def _():
            gain_grad_ref[...] = jnp.zeros_like(gain_grad_ref)

        gain_grad_ref[...] += jnp.sum(up * scaled, axis=0, keepdims=True)
    up = up * gain_ref[...]
    back = scale * (up - scaled * jnp.mean(up * scaled, axis=-1, keepdims=True))
    total = res_ref[...].astype(F32) + back
    if len(rest) == 1:
        rest[0][...] = total.astype(BF)
        return
    w_ref, low_ref, total_ref, out_ref = rest[:4]
    low = total.astype(BF)
    low_ref[...] = low
    total_ref[...] = total
    out_ref[...] = mm(low, w_ref[...], 1, 1).astype(BF)


def norm_back(values, upstream, residual, gain, weight):
    rows, width = values.shape
    block = pl.BlockSpec((rows // 4, width), lambda i: (i, 0))
    in_specs = [block, block, block, fixed((1, width))]
    out_specs = [block]
    shapes = [jax.ShapeDtypeStruct((rows, width), BF)]
    more = []
    if weight is not None:
        inner = weight.shape[0]
        more = [weight]
        in_specs += [fixed(weight.shape)]
        out_specs += [
            block,
            pl.BlockSpec((rows // 4, inner), lambda i: (i, 0)),
            fixed((1, width)),
        ]
        shapes += [
            jax.ShapeDtypeStruct((rows, width), F32),
            jax.ShapeDtypeStruct((rows, inner), BF),
            jax.ShapeDtypeStruct((1, width), F32),
        ]
    return pl.pallas_call(
        norm_back_kernel,
        name="norm_back",
        grid=(4,),
        in_specs=in_specs,
        out_specs=out_specs,
        out_shape=shapes,
        compiler_params=params(),
        cost_estimate=cost(12 * rows * width, 12 * rows * width),
    )(values, upstream, residual, gain.reshape(1, width), *more)


def shared_kernel(top_ref, bottom_ref, up_ref, wg_ref, wu_ref, wd_ref, act_ref, dg_ref, du_ref, grad_ref):
    ff = wd_ref.shape[0]
    x = jnp.concatenate([top_ref[...], bottom_ref[...]], axis=0)
    upstream = up_ref[...]
    a = mm(x, wg_ref[...], 1, 1)
    b = mm(x, wu_ref[...], 1, 1)
    back = mm(upstream, wd_ref[...], 1, 1)
    sig = jax.nn.sigmoid(a)
    swish = a * sig
    active = (swish * b).astype(BF)
    dg = (back * b * (sig + swish * (1.0 - sig))).astype(BF)
    du = (back * swish).astype(BF)
    act_ref[...] = active
    dg_ref[...] = dg
    du_ref[...] = du
    grad_ref[:ff, :] = mm(active, upstream, 0, 0).astype(BF)
    grad_ref[ff : 2 * ff, :] = mm(dg, x, 0, 0).astype(BF)
    grad_ref[2 * ff :, :] = mm(du, x, 0, 0).astype(BF)


def shared_step(top, bottom, upstream, gate_t, up_t, down):
    rows, width = upstream.shape
    ff = down.shape[0]
    inner = jax.ShapeDtypeStruct((rows, ff), BF)
    return pl.pallas_call(
        shared_kernel,
        name="shared_step",
        grid=(1,),
        in_specs=[fixed(top.shape)] * 2 + [fixed((rows, width))] + [fixed((ff, width))] * 3,
        out_specs=[fixed((rows, ff))] * 3 + [fixed((3 * ff, width))],
        out_shape=[inner, inner, inner, jax.ShapeDtypeStruct((3 * ff, width), BF)],
        compiler_params=params(),
        cost_estimate=cost(rows * width, rows * width),
    )(top, bottom, upstream, gate_t, up_t, down)


def finals_kernel(x_ref, proj_ref, query_ref, expand_ref):
    inner, rows = proj_ref.shape
    wide = query_ref.shape[1]
    part = x_ref.shape[1] - inner - wide
    count = expand_ref.shape[0]
    proj_ref[...] = x_ref[:, :inner].astype(F32).T
    query_ref[...] = x_ref[:, inner : inner + wide].astype(F32)
    for i in range(rows // count):
        expand_ref[:, i * part : (i + 1) * part] = x_ref[
            i * count : (i + 1) * count, inner + wide :
        ].astype(F32)


def finals(joined, inner, wide, count):
    rows = joined.shape[0]
    part = joined.shape[1] - inner - wide
    shapes = [(inner, rows), (rows, wide), (count, rows // count * part)]
    return pl.pallas_call(
        finals_kernel,
        name="finals",
        grid=(1,),
        in_specs=[fixed(joined.shape)],
        out_specs=[fixed(shape) for shape in shapes],
        out_shape=[jax.ShapeDtypeStruct(shape, F32) for shape in shapes],
        compiler_params=params(),
        cost_estimate=cost(rows, rows),
    )(joined)


def dot(eq, a, b):
    return jnp.einsum(eq, a, b, preferred_element_type=F32)


def passed_along(shard, axis, by):
    peers = lax.axis_size(axis)
    pairs = [(i, i + by) for i in range(peers) if 0 <= i + by < peers]
    return lax.ppermute(shard, axis, pairs)


def normed(values, norm_gain):
    return (
        values * lax.rsqrt(jnp.mean(values * values, axis=-1, keepdims=True) + epsilon) * norm_gain
    )


def norm_backward(values, norm_gain, upstream):
    _, pullback = jax.vjp(normed, values, norm_gain)
    return pullback(upstream)


def rotate(values, cosine, sine):
    half = values.shape[-1] // 2
    front, back = values[..., :half], values[..., half:]
    return jnp.concatenate([front * cosine - back * sine, back * cosine + front * sine], axis=-1)


def rotate_back(upstream, cosine, sine):
    return rotate(upstream, cosine, -sine)


def silu_gate(gate_val, up_val):
    return gate_val * jax.nn.sigmoid(gate_val) * up_val


def silu_backward(gate_val, up_val, upstream):
    _, pullback = jax.vjp(silu_gate, gate_val, up_val)
    return pullback(upstream)


def rope_tables(seq_all, seq_here, index_here):
    starts = jnp.sum((seq_all[None, :] < seq_here[:, None]).astype(jnp.int32), axis=1)
    position = (index_here - starts).astype(F32)
    frequency = 10000.0 ** (-(jnp.arange(DR // 2, dtype=F32) * 2.0) / DR)
    angle = position[:, None] * frequency[None, :]
    return jnp.cos(angle), jnp.sin(angle)


def turned(value, by):
    return lax.ppermute(value, "dp", [(i, i ^ by) for i in range(lax.axis_size("dp"))])


def swapped(value):
    return turned(value, 1)


def after(value, *others):
    return lax.optimization_barrier((value,) + others)[0]


def scatter_sum(parts):
    joined = parts if not isinstance(parts, list) else jnp.concatenate(parts, axis=1)
    return lax.psum_scatter(joined, "dp", scatter_dimension=0, tiled=True)


def shards(
    tokens,
    seq_ids,
    route_ids,
    cotangent,
    input_gain,
    w_query,
    w_latent,
    latent_gain,
    w_expand,
    w_out,
    middle_gain,
    w_router,
    expert_gate,
    expert_up,
    expert_down,
    shared_gate,
    shared_up,
    shared_down,
):
    devices = lax.axis_size("dp")
    rank_dp = lax.axis_index("dp")
    tok_rows, width = tokens.shape
    experts_local = expert_gate.shape[0]
    all_experts = w_router.shape[1]
    ff_local = expert_gate.shape[2]
    heads_local = w_query.shape[1] // (DN + DR)

    direct = devices == 8
    apart = jnp.array([0, 1, 2, 4, 3, 5, 6, 7] if direct else list(range(devices)), jnp.int32)
    order = (rank_dp ^ apart) if direct else apart

    index_here = rank_dp * tok_rows + jnp.arange(tok_rows, dtype=jnp.int32)
    seq_here = lax.dynamic_slice_in_dim(seq_ids, rank_dp * tok_rows, tok_rows, 0)
    cosine, sine = rope_tables(seq_ids, seq_here, index_here)
    token_features = tokens.astype(F32)
    hidden_in = normed(token_features, input_gain).astype(BF)
    latent_full = jnp.dot(hidden_in, w_latent, preferred_element_type=F32)
    latent_raw = latent_full[:, :KVR]
    latent = normed(latent_raw, latent_gain).astype(BF)
    rope_key = rotate(latent_full[:, KVR:], cosine, sine).astype(BF)
    fill = jnp.zeros((tok_rows, -(KVR + DR) % 128), BF)
    own_keys = jnp.concatenate([latent, rope_key, fill], axis=1)
    odd = rank_dp % 2
    blocks = jnp.stack(
        [rank_dp - 4, rank_dp - 2, (rank_dp - 2) ^ 1, rank_dp - 3 + 2 * odd, rank_dp]
    ).astype(jnp.int32)
    place_q = jnp.stack([seq_here, index_here], axis=1)
    sequences = seq_ids.reshape(1, -1)
    before_two = passed_along(own_keys, "dp", 2)
    before_four = passed_along(own_keys, "dp", 4)
    query_pre = jnp.dot(hidden_in, w_query, preferred_element_type=F32)
    from_pair = swapped(jnp.where(odd == 0, own_keys, before_four))
    before_two = after(before_two, query_pre, from_pair, place_q)
    keys = [before_four, before_two, swapped(before_two), from_pair, own_keys]
    cot_all = lax.all_gather(after(cotangent, before_two, before_four), "dp", tiled=True)
    attended, lse, kv = attend(query_pre, cosine, sine, w_expand, blocks, place_q, sequences, keys)
    attention_part = jnp.dot(attended, w_out, preferred_element_type=F32).astype(BF)
    attention = lax.psum(attention_part, "tensor")

    route_all = lax.all_gather(after(route_ids, attention_part), "dp", tiled=True)
    local_ids = rank_dp * experts_local + jnp.arange(experts_local, dtype=jnp.int32)
    routes = jnp.take(route_all.reshape(devices, tok_rows, -1), order, axis=0)
    named_block = jnp.any(routes[..., None] == local_ids, axis=2)
    before = jnp.tril(jnp.ones((tok_rows, tok_rows), BF), -1)
    rank_within = dot("ts,bse->bte", before, named_block.astype(BF))
    slot_of = jnp.where(named_block, rank_within, -1.0)
    slot = slot_of.astype(jnp.int32).transpose(2, 0, 1)[:, :, None, :]
    columns = jnp.arange(experts_local * SLOTS, dtype=jnp.int32)
    spread = (columns[None, :] // SLOTS == jnp.arange(experts_local, dtype=jnp.int32)[:, None]).astype(
        BF
    )
    places = (
        dot("bte,en->btn", slot_of.astype(BF), spread) == (columns % SLOTS).astype(F32)
    ).astype(BF)
    gate_t = expert_gate.swapaxes(1, 2)
    up_t = expert_up.swapaxes(1, 2)
    cot_rows = pick(order, slot, cot_all)
    back = down_back(cot_rows, expert_down)

    attention = after(attention, cot_rows, places)
    middle, *hidden_mid = norm_sum(tokens, attention, middle_gain)
    first = (rank_dp * experts_local).astype(jnp.int32).reshape(1)
    router_rows = jnp.pad(w_router.T, ((0, -all_experts % 128), (0, 0)))
    if direct:
        pair = [swapped(part) for part in hidden_mid]
        by_x = [turned(part, 2) for part in hidden_mid]
        by_y = [turned(part, 4) for part in hidden_mid]
        held = pick_route(first, slot, [hidden_mid, pair], router_rows, all_experts, 0, 1, [])
    else:
        hidden_all = lax.all_gather(jnp.concatenate(hidden_mid, axis=0), "dp", tiled=True)

    top, bottom = hidden_mid
    if direct:
        top = after(top, pair[0])
    shared_active, shared_gate_grad, shared_up_grad, shared_grads = shared_step(
        top, bottom, cotangent, shared_gate.T, shared_up.T, shared_down
    )
    shared_result = jnp.dot(shared_active, shared_down, preferred_element_type=F32)
    mid_from_shared = dot("tf,df->td", shared_gate_grad, shared_gate) + dot(
        "tf,df->td", shared_up_grad, shared_up
    )
    if direct:
        x_top, x_bottom, y_top, y_bottom = lax.optimization_barrier(
            (*by_x, *by_y, held[0], back, shared_grads)
        )[:4]
        by_x, by_y = [x_top, x_bottom], [y_top, y_bottom]
        corner = [turned(y_top, 2), turned(x_bottom, 4)]
        pair_x = [swapped(part) for part in by_x]
        pair_y = [swapped(part) for part in by_y]
        held = pick_route(first, slot, [by_x, by_y], router_rows, all_experts, 2, 1, held)
        held = pick_route(first, slot, [pair_x, pair_y], router_rows, all_experts, 4, 1, held)
        corner[0] = after(corner[0], held[0])
        pair_corner = [swapped(part) for part in corner]
        held = pick_route(first, slot, [corner], router_rows, all_experts, 6, 1, held)
        held = pick_route(first, slot, [pair_corner], router_rows, all_experts, 7, 1, held)
        rows, router_probs, slot_gates = held
        hidden_parts = [*hidden_mid, *pair, *by_x, *by_y, *corner, *pair_x, *pair_y, *pair_corner]
    else:
        rows, router_probs, slot_gates = pick_route(
            first, slot, [[hidden_all]], router_rows, all_experts, 0, devices, []
        )
        hidden_parts = [hidden_all]
    shared_sums = lax.psum_scatter(
        after(shared_grads, rows), "dp", scatter_dimension=1, tiled=True
    )
    gated_active, gate_val_grad, up_val_grad, row_grad, probs_grad = expert_step(
        rows, gate_t, up_t, back, slot, slot_gates
    )
    grad_expert_down = dot(
        "ecf,ecd->efd",
        gated_active[..., :ff_local],
        cot_rows.reshape(experts_local, -1, width),
    )
    if direct:
        put_args = (first, places, row_grad, router_probs, probs_grad, router_rows)
        some = lambda *at: jnp.array(at, jnp.int32)
        to_pair, logits_pair = put_route(some(4, 5, 7), False, *put_args, None)
        from_pair = swapped(to_pair)
        to_sibling, logits_sibling = put_route(some(1), False, *put_args, None)
        from_sibling = swapped(to_sibling)
        send_x, send_y, kept, logits_cross = put_route(some(2, 3, 6), False, *put_args, from_pair)
        send_x, shared_sums = lax.optimization_barrier((send_x, shared_sums))
        got_x = turned(send_x, 2)
        got_y = turned(send_y, 4)
        own, logits_own = put_route(some(0), False, *put_args, from_sibling)
        routed_part = put(order, places, row_out(gated_active, expert_down, devices))
        got_x, got_y, own, routed_part, mid_from_shared = lax.optimization_barrier(
            (got_x, got_y, own, routed_part, mid_from_shared)
        )
        half = tok_rows // 2
        plus = lambda *terms: sum(term.astype(F32) for term in terms)
        last_y = turned(plus(kept[:half], got_x[:half]).astype(BF), 4)
        last_x = turned(plus(kept[half:], got_y[:half]).astype(BF), 2)
        last_y, last_x = lax.optimization_barrier((last_y, last_x, grad_expert_down))[:2]
        mid_block = jnp.concatenate(
            [plus(own[:half], got_x[half:], last_y), plus(own[half:], got_y[half:], last_x)], axis=0
        )
        logit_grads = [logits_own, logits_sibling, logits_cross, logits_pair]
    else:
        mid_part, logit_grad = put_route(
            order, True, first, places, row_grad, router_probs, probs_grad, router_rows, None
        )
        mid_block = scatter_sum(after(mid_part, shared_sums)).astype(F32)
        routed_part = put(order, places, row_out(gated_active, expert_down, devices))
        mid_block = after(mid_block, routed_part, grad_expert_down)
        logit_grads = [logit_grad]
    mid_sum = (mid_block + mid_from_shared).astype(BF)
    routed_block = scatter_sum(after(routed_part, mid_sum))
    mid_grad = lax.psum(mid_sum, "tensor")
    rows_flat = rows.reshape(experts_local, -1, width)
    grad_expert_gate = dot("ecd,ecf->edf", rows_flat, gate_val_grad[..., :ff_local])
    grad_expert_up = dot("ecd,ecf->edf", rows_flat, up_val_grad[..., :ff_local])
    grad_router = route_grad(logit_grads, hidden_parts)
    mid_grad = after(mid_grad, grad_expert_gate, grad_expert_up, grad_router)

    middle_low, middle_grad, attended_grad, grad_middle_gain = norm_back(
        middle, mid_grad, cotangent, middle_gain, w_out
    )
    query_grad, expanded_grad, *window_grads = attend_back(
        query_pre, cosine, sine, w_expand, blocks, place_q, sequences, lse, attended_grad, kv, keys
    )
    routed_block = after(routed_block, expanded_grad)
    ff_part = (routed_block.astype(F32) + shared_result).astype(BF)
    window_grads = lax.optimization_barrier((*window_grads, ff_part))[:-1]
    four_grad, two_grad, pair_grad, last_grad, keys_grad = window_grads
    pair_grad = swapped(pair_grad)
    last_grad = swapped(last_grad).astype(F32)
    two_grad = (two_grad.astype(F32) + pair_grad.astype(F32)).astype(BF)
    four_grad = (four_grad.astype(F32) + jnp.where(odd == 1, last_grad, 0.0)).astype(BF)
    keys_grad = keys_grad + jnp.where(odd == 0, last_grad, 0.0)
    keys_grad = keys_grad + passed_along(two_grad, "dp", -2).astype(F32)
    keys_grad = keys_grad + passed_along(four_grad, "dp", -4).astype(F32)
    latent_raw_grad, grad_latent_gain = norm_backward(latent_raw, latent_gain, keys_grad[:, :KVR])
    rope_raw_grad = rotate_back(keys_grad[:, KVR : KVR + DR], cosine, sine)
    latent_full_grad = jnp.concatenate([latent_raw_grad, rope_raw_grad], axis=-1).astype(BF)
    input_part = dot("tc,dc->td", query_grad, w_query) + dot(
        "tc,dc->td", latent_full_grad, w_latent
    )
    _, grad_input_gain = norm_backward(token_features, input_gain, input_part)

    feedforward = lax.psum(ff_part, "tensor")
    output = (middle + feedforward.astype(F32)).astype(BF)
    input_part, grad_input_gain = lax.optimization_barrier((input_part.astype(BF), grad_input_gain))
    input_part = after(input_part, feedforward)
    tensors = lax.axis_size("tensor")
    query_width = heads_local * (DN + DR)
    out_width = heads_local * DV
    expand_width = w_expand.shape[1] * KVR // width
    latent_width = KVR + DR
    gains = jnp.concatenate(
        [
            grad_middle_gain / tensors,
            grad_input_gain[None, :],
            jnp.repeat(grad_latent_gain, width // KVR)[None, :],
            jnp.zeros((13, width), F32),
        ],
        axis=0,
    )
    parts = parts_rows(latent_full_grad, hidden_in, grad_router, gains, all_experts)
    parts = lax.psum_scatter(parts, "dp", scatter_dimension=1, tiled=True)
    latents = jnp.concatenate([key[:, :KVR] for key in keys], axis=0)
    grad_expand = dot("wk,wc->kc", latents, after(expanded_grad, keys_grad)).astype(BF)
    share = KVR // devices
    grad_expand = (
        grad_expand.reshape(devices, share, -1, expand_width)
        .transpose(0, 2, 1, 3)
        .reshape(width, expand_width)
    )
    late = scatter_sum(
        [
            dot("td,tc->dc", middle_low, attended).astype(BF),
            dot("td,tc->dc", hidden_in, query_grad).astype(BF),
            grad_expand,
        ]
    )
    grad_out_proj, grad_query, grad_expand = finals(late, out_width, query_width, share)
    input_grad, parts = lax.psum((input_part, parts), "tensor")
    parts = parts.astype(F32)
    (token_grad,) = norm_back(tokens, input_grad, middle_grad, input_gain, None)
    sw = shared_gate.shape[1]
    gain_at = latent_width + all_experts
    return (
        output,
        token_grad,
        parts[gain_at + 1],
        grad_query,
        parts[:latent_width].T,
        parts[gain_at + 2, :: width // KVR],
        grad_expand,
        grad_out_proj,
        parts[gain_at],
        parts[latent_width:gain_at].T,
        grad_expert_gate,
        grad_expert_up,
        grad_expert_down,
        shared_sums[sw : 2 * sw].astype(F32).T,
        shared_sums[2 * sw :].astype(F32).T,
        shared_sums[:sw].astype(F32),
    )


def solution(mesh):
    placed = (
        P("dp", None),
        P(),
        P("dp", None),
        P("dp", None),
        P(),
        P(None, "tensor"),
        P(),
        P(),
        P(None, "tensor"),
        P("tensor", None),
        P(),
        P(),
        P("dp", None, "tensor"),
        P("dp", None, "tensor"),
        P("dp", "tensor", None),
        P(None, "tensor"),
        P(None, "tensor"),
        P("tensor", None),
    )
    return jax.shard_map(
        shards,
        mesh=mesh,
        in_specs=placed,
        out_specs=(
            P("dp", None),
            P("dp", None),
            P("dp"),
            P("dp", "tensor"),
            P("dp", None),
            P("dp"),
            P("dp", "tensor"),
            P("tensor", "dp"),
            P("dp"),
            P("dp", None),
            P("dp", None, "tensor"),
            P("dp", None, "tensor"),
            P("dp", "tensor", None),
            P("dp", "tensor"),
            P("dp", "tensor"),
            P("tensor", "dp"),
        ),
        check_vma=False,
    )
```

```python
import functools

import jax
import jax.numpy as jnp
from jax import lax
from jax.experimental import pallas as pl
from jax.experimental.pallas import tpu as pltpu
from jax.sharding import PartitionSpec as P

DN = 128
DR = 64
DV = 128
KVR = 512
REACH = 4
SLOTS = 80
BF = jnp.bfloat16
F32 = jnp.float32
VMEM_BYTES = 60 * 1024 * 1024
epsilon = 1e-06


def mm(a, b, ca, cb):
    return lax.dot_general(a, b, (((ca,), (cb,)), ((), ())), preferred_element_type=F32)


def cost(flops, nbytes, trans=0):
    return pl.CostEstimate(flops=int(flops), bytes_accessed=int(nbytes), transcendentals=int(trans))


def smem():
    return pl.BlockSpec(memory_space=pltpu.SMEM)


def fixed(shape):
    return pl.BlockSpec(shape, lambda *at: (0,) * len(shape))


def params():
    return pltpu.CompilerParams(vmem_limit_bytes=VMEM_BYTES)


def attend_setup(
    head, heads, step, qp_ref, cos_ref, sin_ref, at_ref, sq_ref, seq_ref, keys, q_ref, key_ref, bias_ref
):
    rows = qp_ref.shape[0]

    @pl.when(head == 0)
    def _():
        for at in range(0, rows, step):
            part = pl.ds(at, step)
            for i in range(len(keys)):
                block = at_ref[i]
                where = pl.multiple_of(jnp.maximum(block, 0) * rows, 128)
                sequence = jnp.where(block >= 0, seq_ref[0:1, pl.ds(where, rows)], -1)
                position = block * rows + lax.broadcasted_iota(jnp.int32, (1, rows), 1)
                allowed = (sq_ref[part, 0:1] == sequence) & (position <= sq_ref[part, 1:2])
                bias_ref[part, i * rows : (i + 1) * rows] = jnp.where(allowed, 0.0, -1e30).astype(BF)
        for i, key in enumerate(keys):
            key_ref[i * rows : (i + 1) * rows, DN:] = key[:, KVR : KVR + DR]

    for k in range(heads):

        @pl.when(head == k)
        def _():
            at = k * (DN + DR)
            front = qp_ref[:, at + DN : at + DN + DR // 2]
            back = qp_ref[:, at + DN + DR // 2 : at + DN + DR]
            cosine, sine = cos_ref[...], sin_ref[...]
            q_ref[:, :DN] = qp_ref[:, at : at + DN].astype(BF)
            q_ref[:, DN : DN + DR // 2] = (front * cosine - back * sine).astype(BF)
            q_ref[:, DN + DR // 2 :] = (back * cosine + front * sine).astype(BF)


def attend_kernel(heads, step, qp_ref, cos_ref, sin_ref, wx_ref, at_ref, sq_ref, seq_ref, *rest):
    keys, (o_ref, lse_ref, kv_ref, q_ref, key_ref, bias_ref) = rest[:-6], rest[-6:]
    rows = qp_ref.shape[0]
    scale = (DN + DR) ** (-0.5)
    attend_setup(
        pl.program_id(0), heads, step, qp_ref, cos_ref, sin_ref, at_ref, sq_ref, seq_ref, keys,
        q_ref, key_ref, bias_ref,
    )
    for i, key in enumerate(keys):
        part = pl.ds(i * rows, rows)
        kv = mm(key[:, :KVR], wx_ref[...], 1, 0).astype(BF)
        kv_ref[part, :] = kv
        key_ref[part, :DN] = kv[:, :DN]
    for at in range(0, rows, step):
        part = pl.ds(at, step)
        s = mm(q_ref[part, :], key_ref[...], 1, 1) * scale + bias_ref[part, :].astype(F32)
        top = jnp.max(s, axis=-1, keepdims=True)
        p = jnp.exp(s - top)
        total = jnp.sum(p, axis=-1, keepdims=True)
        o_ref[part, :] = mm((p * (1.0 / total)).astype(BF), kv_ref[:, DN:], 1, 0).astype(BF)
        lse_ref[0, part, :] = top + jnp.log(total)


def attend_specs(query_pre, cosine, w_expand, blocks, place_q, sequences, keys):
    return [
        fixed(query_pre.shape),
        fixed(cosine.shape),
        fixed(cosine.shape),
        pl.BlockSpec((KVR, DN + DV), lambda h: (0, h)),
        smem(),
        fixed(place_q.shape),
        fixed(sequences.shape),
    ], [fixed(keys[0].shape) for _ in keys]


def attend(query_pre, cosine, sine, w_expand, blocks, place_q, sequences, keys):
    rows = query_pre.shape[0]
    heads = query_pre.shape[1] // (DN + DR)
    window = rows * len(keys)
    specs, key_specs = attend_specs(query_pre, cosine, w_expand, blocks, place_q, sequences, keys)
    return pl.pallas_call(
        functools.partial(attend_kernel, heads, rows // 2),
        name="attend",
        grid=(heads,),
        in_specs=specs + key_specs,
        out_specs=[
            pl.BlockSpec((rows, DV), lambda h: (0, h)),
            pl.BlockSpec((1, rows, 1), lambda h: (h, 0, 0)),
            pl.BlockSpec((window, DN + DV), lambda h: (0, h)),
        ],
        out_shape=[
            jax.ShapeDtypeStruct((rows, heads * DV), BF),
            jax.ShapeDtypeStruct((heads, rows, 1), F32),
            jax.ShapeDtypeStruct((window, heads * (DN + DV)), BF),
        ],
        scratch_shapes=[
            pltpu.VMEM((rows, DN + DR), BF),
            pltpu.VMEM((window, DN + DR), BF),
            pltpu.VMEM((rows, window), BF),
        ],
        compiler_params=params(),
        cost_estimate=cost(
            2 * heads * window * (rows * 384 + KVR * 256), 2 * window * 640, heads * rows * window
        ),
    )(query_pre, cosine, sine, w_expand, blocks, place_q, sequences, *keys)


def attend_back_kernel(
    heads, step, count, qp_ref, cos_ref, sin_ref, wx_ref, at_ref, sq_ref, seq_ref, lse_ref, do_ref, kv_ref,
    *rest
):
    keys, rest = rest[:count], rest[count:]
    dq_ref, dkv_ref = rest[:2]
    grads = rest[2 : 2 + count]
    q_ref, key_ref, bias_ref, dk_ref, dv_ref, acc_ref, dqs_ref = rest[2 + count :]
    rows = qp_ref.shape[0]
    head = pl.program_id(0)
    scale = (DN + DR) ** (-0.5)
    attend_setup(
        head, heads, step, qp_ref, cos_ref, sin_ref, at_ref, sq_ref, seq_ref, keys, q_ref, key_ref, bias_ref
    )
    key_ref[:, :DN] = kv_ref[:, :DN]

    @pl.when(head == 0)
    def _():
        acc_ref[...] = jnp.zeros_like(acc_ref)

    for at in range(0, rows, step):
        part = pl.ds(at, step)
        q = q_ref[part, :]
        do = do_ref[part, :]
        s = mm(q, key_ref[...], 1, 1) * scale + bias_ref[part, :].astype(F32)
        p = jnp.exp(s - lse_ref[0, part, :])
        dp = mm(do, kv_ref[:, DN:], 1, 1)
        ds = (p * (dp - jnp.sum(p * dp, axis=-1, keepdims=True))).astype(BF)
        dqs_ref[part, :] = mm(ds, key_ref[...], 1, 0) * scale
        dk = mm(ds, q, 0, 0) * scale
        dv = mm(p.astype(BF), do, 0, 0)
        if at == 0:
            dk_ref[...] = dk
            dv_ref[...] = dv
        else:
            dk_ref[...] += dk
            dv_ref[...] += dv
    dkv_ref[:, :DN] = dk_ref[:, :DN].astype(BF)
    dkv_ref[:, DN:] = dv_ref[...].astype(BF)
    acc_ref[:, :KVR] += mm(dkv_ref[...], wx_ref[...], 1, 1)
    acc_ref[:, KVR : KVR + DR] += dk_ref[:, DN:]
    for k in range(heads):

        @pl.when(head == k)
        def _():
            at = k * (DN + DR)
            front = dqs_ref[:, DN : DN + DR // 2]
            back = dqs_ref[:, DN + DR // 2 :]
            cosine, sine = cos_ref[...], sin_ref[...]
            dq_ref[:, at : at + DN] = dqs_ref[:, :DN].astype(BF)
            dq_ref[:, at + DN : at + DN + DR // 2] = (front * cosine + back * sine).astype(BF)
            dq_ref[:, at + DN + DR // 2 : at + DN + DR] = (back * cosine - front * sine).astype(BF)

    @pl.when(head == heads - 1)
    def _():
        for i, grad in enumerate(grads):
            grad[...] = acc_ref[i * rows : (i + 1) * rows, :].astype(grad.dtype)


def attend_back(query_pre, cosine, sine, w_expand, blocks, place_q, sequences, lse, attended_grad, kv, keys):
    rows = query_pre.shape[0]
    heads = query_pre.shape[1] // (DN + DR)
    window = rows * len(keys)
    count = len(keys)
    specs, key_specs = attend_specs(query_pre, cosine, w_expand, blocks, place_q, sequences, keys)
    wide = keys[0].shape[1]
    return pl.pallas_call(
        functools.partial(attend_back_kernel, heads, rows // 2, count),
        name="attend_back",
        grid=(heads,),
        in_specs=specs
        + [
            pl.BlockSpec((1, rows, 1), lambda h: (h, 0, 0)),
            pl.BlockSpec((rows, DV), lambda h: (0, h)),
            pl.BlockSpec((window, DN + DV), lambda h: (0, h)),
        ]
        + key_specs,
        out_specs=[fixed(query_pre.shape), pl.BlockSpec((window, DN + DV), lambda h: (0, h))]
        + [fixed((rows, wide)) for _ in keys],
        out_shape=[
            jax.ShapeDtypeStruct(query_pre.shape, BF),
            jax.ShapeDtypeStruct((window, w_expand.shape[1]), BF),
        ]
        + [jax.ShapeDtypeStruct((rows, wide), BF) for _ in keys[1:]]
        + [jax.ShapeDtypeStruct((rows, wide), F32)],
        scratch_shapes=[
            pltpu.VMEM((rows, DN + DR), BF),
            pltpu.VMEM((window, DN + DR), BF),
            pltpu.VMEM((rows, window), BF),
            pltpu.VMEM((window, DN + DR), F32),
            pltpu.VMEM((window, DV), F32),
            pltpu.VMEM((window, wide), F32),
            pltpu.VMEM((rows, DN + DR), F32),
        ],
        compiler_params=params(),
        cost_estimate=cost(window * rows, window * rows),
    )(query_pre, cosine, sine, w_expand, blocks, place_q, sequences, lse, attended_grad, kv, *keys)


def one_hot(slot_ref):
    experts, rows = slot_ref.shape[0], slot_ref.shape[-1]
    place = lax.broadcasted_iota(jnp.int32, (SLOTS, rows), 0)
    return jnp.concatenate(
        [(slot_ref[e, 0] == place).astype(F32).astype(BF) for e in range(experts)], axis=0
    )


def pick_kernel(order_ref, slot_ref, x_ref, o_ref):
    o_ref[...] = mm(one_hot(slot_ref), x_ref[...], 1, 0).astype(BF).reshape(o_ref.shape)


def pick(order, slot, values):
    experts, blocks, _, rows = slot.shape
    width = values.shape[1]
    return pl.pallas_call(
        pick_kernel,
        name="pick",
        grid_spec=pltpu.PrefetchScalarGridSpec(
            num_scalar_prefetch=1,
            grid=(blocks,),
            in_specs=[
                pl.BlockSpec((experts, 1, 1, rows), lambda b, o: (0, b, 0, 0)),
                pl.BlockSpec((rows, width), lambda b, o: (o[b], 0)),
            ],
            out_specs=pl.BlockSpec((experts, 1, SLOTS, width), lambda b, o: (0, b, 0, 0)),
        ),
        out_shape=jax.ShapeDtypeStruct((experts, blocks, SLOTS, width), BF),
        compiler_params=params(),
        cost_estimate=cost(
            2 * experts * blocks * SLOTS * rows * width,
            2 * blocks * width * (rows + experts * SLOTS),
        ),
    )(order, slot, values)


def pick_route_kernel(count, pieces, parts, first_ref, slot_ref, w_ref, *refs):
    o_ref, p_ref, g_ref = refs[-3:]
    experts, rows = slot_ref.shape[0], slot_ref.shape[3]
    size = rows // parts
    for n in range(pieces):
        place = lax.broadcasted_iota(jnp.int32, (SLOTS, rows), 0)
        chosen = jnp.concatenate(
            [(slot_ref[i, n] == place).astype(F32).astype(BF) for i in range(experts)], axis=0
        )
        picked, taken = 0.0, 0.0
        for m in range(parts):
            x = refs[n * parts + m][...]
            logits = mm(x, w_ref[...], 1, 1)
            lane = lax.broadcasted_iota(jnp.int32, logits.shape, 1)
            logits = jnp.where(lane < count, logits, -1e30)
            e = jnp.exp(logits - jnp.max(logits, axis=-1, keepdims=True))
            probs = e / jnp.sum(e, axis=-1, keepdims=True)
            p_ref[n * rows + m * size : n * rows + (m + 1) * size, :] = probs
            high = probs.astype(BF)
            low = (probs - high.astype(F32)).astype(BF)
            part = chosen[:, m * size : (m + 1) * size]
            picked += mm(part, x, 1, 0)
            taken += mm(part, high, 1, 0) + mm(part, low, 1, 0)
        o_ref[:, n] = picked.astype(BF).reshape(experts, SLOTS, -1)
        lane = lax.broadcasted_iota(jnp.int32, (SLOTS, taken.shape[1]), 1)
        for i in range(experts):
            part = taken[i * SLOTS : (i + 1) * SLOTS, :]
            g_ref[i, n] = jnp.sum(
                jnp.where(lane == first_ref[0] + i, part, 0.0), axis=-1, keepdims=True
            )


def pick_route(first, slot, values, router_rows, count, at, steps, earlier):
    experts, blocks, _, rows = slot.shape
    parts = len(values[0])
    pieces = len(values)
    values = [part for value in values for part in value]
    width = values[0].shape[1]
    lanes = router_rows.shape[0]
    at = at // pieces
    whole = pl.BlockSpec(memory_space=pl.ANY)
    return pl.pallas_call(
        functools.partial(pick_route_kernel, count, pieces, parts),
        name="pick_route",
        grid=(steps,),
        in_specs=[
            smem(),
            pl.BlockSpec((experts, pieces, 1, rows), lambda b: (0, at + b, 0, 0)),
            fixed(router_rows.shape),
        ]
        + [pl.BlockSpec((rows // parts, width), lambda b: (b, 0)) for _ in values]
        + [whole for _ in earlier],
        out_specs=[
            pl.BlockSpec((experts, pieces, SLOTS, width), lambda b: (0, at + b, 0, 0)),
            pl.BlockSpec((pieces * rows, lanes), lambda b: (at + b, 0)),
            pl.BlockSpec((experts, pieces, SLOTS, 1), lambda b: (0, at + b, 0, 0)),
        ],
        out_shape=[
            jax.ShapeDtypeStruct((experts, blocks, SLOTS, width), BF),
            jax.ShapeDtypeStruct((blocks * rows, lanes), F32),
            jax.ShapeDtypeStruct((experts, blocks, SLOTS, 1), F32),
        ],
        input_output_aliases={3 + len(values) + i: i for i in range(len(earlier))},
        compiler_params=params(),
        cost_estimate=cost(pieces * steps * rows * width, pieces * steps * width * rows),
    )(first, slot, router_rows, *values, *earlier)


def route_grad_kernel(count, *refs):
    total = 0.0
    grads, values = refs[:count], refs[count:-1]
    which, at = 0, 0
    for ref in values:
        size = ref.shape[0]
        total += mm(grads[which][at : at + size, :], ref[...], 0, 0)
        at += size
        if at == grads[which].shape[0]:
            which, at = which + 1, 0
    refs[-1][...] = total.astype(BF)


def route_grad(grads, values):
    width = values[0].shape[1]
    lanes = grads[0].shape[1]
    return pl.pallas_call(
        functools.partial(route_grad_kernel, len(grads)),
        name="route_grad",
        grid=(1,),
        in_specs=[fixed(array.shape) for array in [*grads, *values]],
        out_specs=fixed((lanes, width)),
        out_shape=jax.ShapeDtypeStruct((lanes, width), BF),
        compiler_params=params(),
        cost_estimate=cost(lanes * width, lanes * width),
    )(*grads, *values)


def parts_kernel(lg_ref, x_ref, route_ref, gain_ref, o_ref):
    inner = lg_ref.shape[1]
    count = o_ref.shape[0] - inner - gain_ref.shape[0]
    o_ref[:inner, :] = mm(lg_ref[...], x_ref[...], 0, 0).astype(BF)
    o_ref[inner : inner + count, :] = route_ref[:count, :]
    o_ref[inner + count :, :] = gain_ref[...].astype(BF)


def parts_rows(latent_grad, values, route, gains, count):
    width = values.shape[1]
    shape = (latent_grad.shape[1] + count + gains.shape[0], width)
    return pl.pallas_call(
        parts_kernel,
        name="parts_rows",
        grid=(1,),
        in_specs=[fixed(array.shape) for array in (latent_grad, values, route, gains)],
        out_specs=fixed(shape),
        out_shape=jax.ShapeDtypeStruct(shape, BF),
        compiler_params=params(),
        cost_estimate=cost(width, width),
    )(latent_grad, values, route, gains)


def put_kernel(order_ref, place_ref, r_ref, o_ref):
    o_ref[...] = mm(place_ref[0], r_ref[...].reshape(-1, r_ref.shape[-1]), 1, 0).astype(BF)


def returned(first_ref, place_ref, r_ref, p_ref, pg_ref, w_ref):
    experts, rows = pg_ref.shape[0], pg_ref.shape[3]
    by_expert = jnp.concatenate(
        [pg_ref[i, 0] for i in range(experts)] + [jnp.zeros((1, rows), F32)] * (-experts % 8), axis=0
    )
    high = by_expert.astype(BF)
    low = (by_expert - high.astype(F32)).astype(BF)
    probs = p_ref[...]
    shape = (by_expert.shape[0], probs.shape[1])
    expert = lax.broadcasted_iota(jnp.int32, shape, 0)
    lane = lax.broadcasted_iota(jnp.int32, shape, 1)
    spread = (lane == first_ref[0] + expert) & (expert < experts)
    spread = spread.astype(F32).astype(BF)
    grad = mm(high, spread, 0, 0) + mm(low, spread, 0, 0)
    back = (probs * (grad - jnp.sum(probs * grad, axis=-1, keepdims=True))).astype(BF)
    total = mm(place_ref[0], r_ref[...].reshape(-1, r_ref.shape[-1]), 1, 0)
    return total + mm(back, w_ref[...], 1, 0), back


def put_route_kernel(
    order_ref, first_ref, place_ref, r_ref, p_ref, pg_ref, w_ref, *rest
):
    total, back = returned(first_ref, place_ref, r_ref, p_ref, pg_ref, w_ref)
    if len(rest) == 3:
        total += rest[0][...].astype(F32)
    rest[-2][...] = total.astype(BF)
    rest[-1][...] = back


def put_cross_kernel(
    order_ref, first_ref, place_ref, r_ref, p_ref, pg_ref, w_ref, add_ref,
    sx_ref, sy_ref, keep_ref, lg_ref,
):
    total, back = returned(first_ref, place_ref, r_ref, p_ref, pg_ref, w_ref)
    lg_ref[...] = back
    total = (total + add_ref[...].astype(F32)).astype(BF)
    half = total.shape[0] // 2
    top, bottom = total[:half], total[half:]
    step = pl.program_id(0)

    @pl.when(step == 0)
    def _():
        sx_ref[half:, :] = top
        keep_ref[half:, :] = bottom

    @pl.when(step == 1)
    def _():
        sy_ref[half:, :] = bottom
        keep_ref[:half, :] = top

    @pl.when(step == 2)
    def _():
        sx_ref[:half, :] = top
        sy_ref[:half, :] = bottom


def put_specs(places, picked):
    blocks, rows, slots = places.shape
    experts, width = picked.shape[0], picked.shape[3]
    return [
        pl.BlockSpec((1, rows, slots), lambda b, o: (b, 0, 0)),
        pl.BlockSpec((experts, 1, SLOTS, width), lambda b, o: (0, b, 0, 0)),
    ]


def put(order, places, picked):
    blocks, rows, _ = places.shape
    width = picked.shape[3]
    return pl.pallas_call(
        put_kernel,
        name="put",
        grid_spec=pltpu.PrefetchScalarGridSpec(
            num_scalar_prefetch=1,
            grid=(blocks,),
            in_specs=put_specs(places, picked),
            out_specs=pl.BlockSpec((rows, width), lambda b, o: (o[b], 0)),
        ),
        out_shape=jax.ShapeDtypeStruct((blocks * rows, width), BF),
        compiler_params=params(),
        cost_estimate=cost(blocks * rows * width, blocks * rows * width),
    )(order, places, picked)


def put_route(order, absolute, first, places, picked, probs, probs_grad, router_rows, added):
    _, rows, slots = places.shape
    blocks = order.shape[0]
    experts, width = picked.shape[0], picked.shape[3]
    lanes = probs.shape[1]
    come = (lambda b, o: b) if absolute else (lambda b, o: o[b])
    go = (lambda b, o: o[b]) if absolute else (lambda b, o: b)
    cross = added is not None and blocks == 3
    whole = pl.BlockSpec((rows, width), lambda b, o: (0, 0))
    out_specs = [whole] * 3 if cross else [pl.BlockSpec((rows, width), lambda b, o: (go(b, o), 0))]
    sizes = [rows] * 3 if cross else [blocks * rows]
    more = [] if added is None else [added]
    return pl.pallas_call(
        put_cross_kernel if cross else put_route_kernel,
        name="put_route",
        grid_spec=pltpu.PrefetchScalarGridSpec(
            num_scalar_prefetch=1,
            grid=(blocks,),
            in_specs=[
                smem(),
                pl.BlockSpec((1, rows, slots), lambda b, o: (come(b, o), 0, 0)),
                pl.BlockSpec((experts, 1, SLOTS, width), lambda b, o: (0, come(b, o), 0, 0)),
                pl.BlockSpec((rows, lanes), lambda b, o: (come(b, o), 0)),
                pl.BlockSpec((experts, 1, 1, rows), lambda b, o: (0, come(b, o), 0, 0)),
                fixed(router_rows.shape),
            ]
            + [pl.BlockSpec((rows, width), lambda b, o: (b, 0)) for _ in more],
            out_specs=out_specs + [pl.BlockSpec((rows, lanes), lambda b, o: (b, 0))],
        ),
        out_shape=[jax.ShapeDtypeStruct((size, width), BF) for size in sizes]
        + [jax.ShapeDtypeStruct((blocks * rows, lanes), BF)],
        compiler_params=params(),
        cost_estimate=cost(blocks * rows * width, blocks * rows * width),
    )(order, first, places, picked, probs, probs_grad, router_rows, *more)


def down_back_kernel(x_ref, w_ref, o_ref):
    ff = w_ref.shape[1]
    wide = o_ref.shape[-1]
    back = mm(x_ref[...].reshape(-1, x_ref.shape[-1]), w_ref[0], 1, 1)
    o_ref[0, :, :ff] = back
    if wide > ff:
        o_ref[0, :, ff:] = jnp.zeros((o_ref.shape[1], wide - ff), F32)


def down_back(rows, down):
    experts, blocks, slots, width = rows.shape
    ff = down.shape[1]
    wide = -(-ff // 128) * 128
    count = blocks * slots
    return pl.pallas_call(
        down_back_kernel,
        name="down_back",
        grid=(experts,),
        in_specs=[
            pl.BlockSpec((1, blocks, slots, width), lambda e: (e, 0, 0, 0)),
            pl.BlockSpec((1, ff, width), lambda e: (e, 0, 0)),
        ],
        out_specs=pl.BlockSpec((1, count, wide), lambda e: (e, 0, 0)),
        out_shape=jax.ShapeDtypeStruct((experts, count, wide), F32),
        compiler_params=params(),
        cost_estimate=cost(
            experts * count * width,
            experts * count * ff,
        ),
    )(rows, down)


def row_out_kernel(x_ref, w_ref, o_ref):
    ff = w_ref.shape[1]
    o_ref[...] = mm(x_ref[0, :, :ff], w_ref[0], 1, 0).astype(BF).reshape(o_ref.shape)


def row_out(active, down, blocks):
    experts, count, wide = active.shape
    ff, width = down.shape[1:]
    slots = count // blocks
    return pl.pallas_call(
        row_out_kernel,
        name="row_out",
        grid=(experts,),
        in_specs=[
            pl.BlockSpec((1, count, wide), lambda e: (e, 0, 0)),
            pl.BlockSpec((1, ff, width), lambda e: (e, 0, 0)),
        ],
        out_specs=pl.BlockSpec((1, blocks, slots, width), lambda e: (e, 0, 0, 0)),
        out_shape=jax.ShapeDtypeStruct((experts, blocks, slots, width), BF),
        compiler_params=params(),
        cost_estimate=cost(count * width, count * width),
    )(active, down)


def expert_kernel(
    x_ref, gate_ref, up_ref, back_ref, slot_ref, sg_ref,
    ga_ref, dg_ref, du_ref, dx_ref, pg_ref, w_ref, d_ref,
):
    ff = gate_ref.shape[1]
    wide = back_ref.shape[2]
    blocks, rows = slot_ref.shape[1], slot_ref.shape[3]

    @pl.when(pl.program_id(0) == 0)
    def _():
        w_ref[...] = jnp.zeros_like(w_ref)

    w_ref[:ff, :] = gate_ref[0]
    w_ref[wide : wide + ff, :] = up_ref[0]
    x = x_ref[...].reshape(-1, x_ref.shape[-1])
    both = mm(x, w_ref[...], 1, 1)
    a = both[:, :wide]
    b = both[:, wide:]
    place = lax.broadcasted_iota(jnp.int32, (SLOTS, rows), 0)
    slot_gate = sg_ref[...].reshape(-1, 1)
    back = back_ref[0]
    sig = jax.nn.sigmoid(a)
    swish = a * sig
    active = swish * b
    gate_grad = jnp.sum(active * back, axis=-1, keepdims=True)
    for i in range(blocks):
        part = gate_grad[i * SLOTS : (i + 1) * SLOTS, :]
        pg_ref[0, i] = jnp.sum(
            jnp.where(slot_ref[0, i] == place, part, 0.0), axis=0, keepdims=True
        )
    gated = back * slot_gate
    ga_ref[0] = (active * slot_gate).astype(BF)
    dg = (gated * b * (sig + swish * (1.0 - sig))).astype(BF)
    du = (gated * swish).astype(BF)
    dg_ref[0] = dg
    du_ref[0] = du
    d_ref[:, :wide] = dg
    d_ref[:, wide:] = du
    dx_ref[...] = mm(d_ref[...], w_ref[...], 1, 0).astype(BF).reshape(dx_ref.shape)


def expert_step(rows, gate_t, up_t, back, slot, slot_gates):
    experts, blocks, slots, width = rows.shape
    ff = gate_t.shape[1]
    wide = back.shape[2]
    count = blocks * slots
    whole = pl.BlockSpec((1, blocks, slots, width), lambda e: (e, 0, 0, 0))
    flat = lambda n: pl.BlockSpec((1, count, n), lambda e: (e, 0, 0))
    shape = lambda n, dtype: jax.ShapeDtypeStruct((experts, count, n), dtype)
    weight = pl.BlockSpec((1, ff, width), lambda e: (e, 0, 0))
    by_token = pl.BlockSpec((1,) + slot.shape[1:], lambda e: (e, 0, 0, 0))
    return pl.pallas_call(
        expert_kernel,
        name="expert_step",
        grid=(experts,),
        in_specs=[
            whole,
            weight,
            weight,
            flat(wide),
            by_token,
            pl.BlockSpec((1, blocks, slots, 1), lambda e: (e, 0, 0, 0)),
        ],
        out_specs=[flat(wide), flat(wide), flat(wide), whole, by_token],
        out_shape=[
            shape(wide, BF),
            shape(wide, BF),
            shape(wide, BF),
            jax.ShapeDtypeStruct(rows.shape, BF),
            jax.ShapeDtypeStruct(slot.shape, F32),
        ],
        scratch_shapes=[pltpu.VMEM((2 * wide, width), BF), pltpu.VMEM((count, 2 * wide), BF)],
        compiler_params=params(),
        cost_estimate=cost(
            8 * experts * count * width * wide,
            2 * experts * (2 * count * width + 2 * width * wide + 5 * count * wide),
            experts * count * wide,
        ),
    )(rows, gate_t, up_t, back, slot, slot_gates)


def norm_kernel(x_ref, add_ref, gain_ref, sum_ref, top_ref, bottom_ref):
    x = x_ref[...].astype(F32) + add_ref[...].astype(F32)
    sum_ref[...] = x
    scale = lax.rsqrt(jnp.mean(x * x, axis=-1, keepdims=True) + epsilon)
    out = (x * scale * gain_ref[...]).astype(BF)

    @pl.when(pl.program_id(0) < 2)
    def _():
        top_ref[...] = out

    @pl.when(pl.program_id(0) >= 2)
    def _():
        bottom_ref[...] = out


def norm_sum(values, added, gain):
    rows, width = values.shape
    block = pl.BlockSpec((rows // 4, width), lambda i: (i, 0))
    half = jax.ShapeDtypeStruct((rows // 2, width), BF)
    return pl.pallas_call(
        norm_kernel,
        name="norm_sum",
        grid=(4,),
        in_specs=[block, block, fixed((1, width))],
        out_specs=[
            block,
            pl.BlockSpec((rows // 4, width), lambda i: (jnp.minimum(i, 1), 0)),
            pl.BlockSpec((rows // 4, width), lambda i: (jnp.maximum(i - 2, 0), 0)),
        ],
        out_shape=[jax.ShapeDtypeStruct((rows, width), F32), half, half],
        compiler_params=params(),
        cost_estimate=cost(8 * rows * width, 10 * rows * width),
    )(values, added, gain.reshape(1, width))


def norm_back_kernel(x_ref, up_ref, res_ref, gain_ref, *rest):
    x = x_ref[...].astype(F32)
    up = up_ref[...].astype(F32)
    scale = lax.rsqrt(jnp.mean(x * x, axis=-1, keepdims=True) + epsilon)
    scaled = x * scale
    if len(rest) > 1:
        gain_grad_ref = rest[4]

        @pl.when(pl.program_id(0) == 0)
        def _():
            gain_grad_ref[...] = jnp.zeros_like(gain_grad_ref)

        gain_grad_ref[...] += jnp.sum(up * scaled, axis=0, keepdims=True)
    up = up * gain_ref[...]
    back = scale * (up - scaled * jnp.mean(up * scaled, axis=-1, keepdims=True))
    total = res_ref[...].astype(F32) + back
    if len(rest) == 1:
        rest[0][...] = total.astype(BF)
        return
    w_ref, low_ref, total_ref, out_ref = rest[:4]
    low = total.astype(BF)
    low_ref[...] = low
    total_ref[...] = total
    out_ref[...] = mm(low, w_ref[...], 1, 1).astype(BF)


def norm_back(values, upstream, residual, gain, weight):
    rows, width = values.shape
    block = pl.BlockSpec((rows // 4, width), lambda i: (i, 0))
    in_specs = [block, block, block, fixed((1, width))]
    out_specs = [block]
    shapes = [jax.ShapeDtypeStruct((rows, width), BF)]
    more = []
    if weight is not None:
        inner = weight.shape[0]
        more = [weight]
        in_specs += [fixed(weight.shape)]
        out_specs += [
            block,
            pl.BlockSpec((rows // 4, inner), lambda i: (i, 0)),
            fixed((1, width)),
        ]
        shapes += [
            jax.ShapeDtypeStruct((rows, width), F32),
            jax.ShapeDtypeStruct((rows, inner), BF),
            jax.ShapeDtypeStruct((1, width), F32),
        ]
    return pl.pallas_call(
        norm_back_kernel,
        name="norm_back",
        grid=(4,),
        in_specs=in_specs,
        out_specs=out_specs,
        out_shape=shapes,
        compiler_params=params(),
        cost_estimate=cost(12 * rows * width, 12 * rows * width),
    )(values, upstream, residual, gain.reshape(1, width), *more)


def shared_kernel(top_ref, bottom_ref, up_ref, wg_ref, wu_ref, wd_ref, act_ref, dg_ref, du_ref, grad_ref):
    ff = wd_ref.shape[0]
    x = jnp.concatenate([top_ref[...], bottom_ref[...]], axis=0)
    upstream = up_ref[...]
    a = mm(x, wg_ref[...], 1, 1)
    b = mm(x, wu_ref[...], 1, 1)
    back = mm(upstream, wd_ref[...], 1, 1)
    sig = jax.nn.sigmoid(a)
    swish = a * sig
    active = (swish * b).astype(BF)
    dg = (back * b * (sig + swish * (1.0 - sig))).astype(BF)
    du = (back * swish).astype(BF)
    act_ref[...] = active
    dg_ref[...] = dg
    du_ref[...] = du
    grad_ref[:ff, :] = mm(active, upstream, 0, 0).astype(BF)
    grad_ref[ff : 2 * ff, :] = mm(dg, x, 0, 0).astype(BF)
    grad_ref[2 * ff :, :] = mm(du, x, 0, 0).astype(BF)


def shared_step(top, bottom, upstream, gate_t, up_t, down):
    rows, width = upstream.shape
    ff = down.shape[0]
    inner = jax.ShapeDtypeStruct((rows, ff), BF)
    return pl.pallas_call(
        shared_kernel,
        name="shared_step",
        grid=(1,),
        in_specs=[fixed(top.shape)] * 2 + [fixed((rows, width))] + [fixed((ff, width))] * 3,
        out_specs=[fixed((rows, ff))] * 3 + [fixed((3 * ff, width))],
        out_shape=[inner, inner, inner, jax.ShapeDtypeStruct((3 * ff, width), BF)],
        compiler_params=params(),
        cost_estimate=cost(rows * width, rows * width),
    )(top, bottom, upstream, gate_t, up_t, down)


def finals_kernel(x_ref, proj_ref, query_ref, expand_ref):
    inner, rows = proj_ref.shape
    wide = query_ref.shape[1]
    part = x_ref.shape[1] - inner - wide
    count = expand_ref.shape[0]
    proj_ref[...] = x_ref[:, :inner].astype(F32).T
    query_ref[...] = x_ref[:, inner : inner + wide].astype(F32)
    for i in range(rows // count):
        expand_ref[:, i * part : (i + 1) * part] = x_ref[
            i * count : (i + 1) * count, inner + wide :
        ].astype(F32)


def finals(joined, inner, wide, count):
    rows = joined.shape[0]
    part = joined.shape[1] - inner - wide
    shapes = [(inner, rows), (rows, wide), (count, rows // count * part)]
    return pl.pallas_call(
        finals_kernel,
        name="finals",
        grid=(1,),
        in_specs=[fixed(joined.shape)],
        out_specs=[fixed(shape) for shape in shapes],
        out_shape=[jax.ShapeDtypeStruct(shape, F32) for shape in shapes],
        compiler_params=params(),
        cost_estimate=cost(rows, rows),
    )(joined)


def dot(eq, a, b):
    return jnp.einsum(eq, a, b, preferred_element_type=F32)


def passed_along(shard, axis, by):
    peers = lax.axis_size(axis)
    pairs = [(i, i + by) for i in range(peers) if 0 <= i + by < peers]
    return lax.ppermute(shard, axis, pairs)


def normed(values, norm_gain):
    return (
        values * lax.rsqrt(jnp.mean(values * values, axis=-1, keepdims=True) + epsilon) * norm_gain
    )


def norm_backward(values, norm_gain, upstream):
    _, pullback = jax.vjp(normed, values, norm_gain)
    return pullback(upstream)


def rotate(values, cosine, sine):
    half = values.shape[-1] // 2
    front, back = values[..., :half], values[..., half:]
    return jnp.concatenate([front * cosine - back * sine, back * cosine + front * sine], axis=-1)


def rotate_back(upstream, cosine, sine):
    return rotate(upstream, cosine, -sine)


def silu_gate(gate_val, up_val):
    return gate_val * jax.nn.sigmoid(gate_val) * up_val


def silu_backward(gate_val, up_val, upstream):
    _, pullback = jax.vjp(silu_gate, gate_val, up_val)
    return pullback(upstream)


def rope_tables(seq_all, seq_here, index_here):
    starts = jnp.sum((seq_all[None, :] < seq_here[:, None]).astype(jnp.int32), axis=1)
    position = (index_here - starts).astype(F32)
    frequency = 10000.0 ** (-(jnp.arange(DR // 2, dtype=F32) * 2.0) / DR)
    angle = position[:, None] * frequency[None, :]
    return jnp.cos(angle), jnp.sin(angle)


def turned(value, by):
    return lax.ppermute(value, "dp", [(i, i ^ by) for i in range(lax.axis_size("dp"))])


def swapped(value):
    return turned(value, 1)


def after(value, *others):
    return lax.optimization_barrier((value,) + others)[0]


def scatter_sum(parts):
    joined = parts if not isinstance(parts, list) else jnp.concatenate(parts, axis=1)
    return lax.psum_scatter(joined, "dp", scatter_dimension=0, tiled=True)


def tensor_sum(value):
    peers = lax.axis_size("tensor")
    rank = lax.axis_index("tensor")
    size = value.shape[0] // peers
    piece = lambda at: lax.dynamic_slice_in_dim(value, at * size, size, 0)
    turn = lambda piece, by: lax.ppermute(
        piece, "tensor", [(i, (i + by) % peers) for i in range(peers)]
    )
    total = piece(rank).astype(F32)
    for by in range(1, peers):
        total = total + turn(piece((rank + by) % peers), by).astype(F32)
    mine = total.astype(BF)
    around = [turn(mine, by) for by in range(peers - 1, 0, -1)] + [mine]
    both = jnp.concatenate(around + around[:-1], axis=0)
    return lax.dynamic_slice_in_dim(both, (peers - 1 - rank) * size, value.shape[0], 0)


def shards(
    tokens,
    seq_ids,
    route_ids,
    cotangent,
    input_gain,
    w_query,
    w_latent,
    latent_gain,
    w_expand,
    w_out,
    middle_gain,
    w_router,
    expert_gate,
    expert_up,
    expert_down,
    shared_gate,
    shared_up,
    shared_down,
):
    devices = lax.axis_size("dp")
    rank_dp = lax.axis_index("dp")
    tok_rows, width = tokens.shape
    experts_local = expert_gate.shape[0]
    all_experts = w_router.shape[1]
    ff_local = expert_gate.shape[2]
    heads_local = w_query.shape[1] // (DN + DR)

    direct = devices == 8
    apart = jnp.array([0, 1, 2, 4, 3, 5, 6, 7] if direct else list(range(devices)), jnp.int32)
    order = (rank_dp ^ apart) if direct else apart

    index_here = rank_dp * tok_rows + jnp.arange(tok_rows, dtype=jnp.int32)
    seq_here = lax.dynamic_slice_in_dim(seq_ids, rank_dp * tok_rows, tok_rows, 0)
    cosine, sine = rope_tables(seq_ids, seq_here, index_here)
    token_features = tokens.astype(F32)
    hidden_in = normed(token_features, input_gain).astype(BF)
    latent_full = jnp.dot(hidden_in, w_latent, preferred_element_type=F32)
    latent_raw = latent_full[:, :KVR]
    latent = normed(latent_raw, latent_gain).astype(BF)
    rope_key = rotate(latent_full[:, KVR:], cosine, sine).astype(BF)
    fill = jnp.zeros((tok_rows, -(KVR + DR) % 128), BF)
    own_keys = jnp.concatenate([latent, rope_key, fill], axis=1)
    odd = rank_dp % 2
    blocks = jnp.stack(
        [rank_dp - 4, rank_dp - 2, (rank_dp - 2) ^ 1, rank_dp - 3 + 2 * odd, rank_dp]
    ).astype(jnp.int32)
    place_q = jnp.stack([seq_here, index_here], axis=1)
    sequences = seq_ids.reshape(1, -1)
    before_two = passed_along(own_keys, "dp", 2)
    before_four = passed_along(own_keys, "dp", 4)
    query_pre = jnp.dot(hidden_in, w_query, preferred_element_type=F32)
    route_all = lax.all_gather(after(route_ids, own_keys), "dp", tiled=True)
    before_four = after(before_four, query_pre, place_q, route_all)
    from_pair = swapped(jnp.where(odd == 0, own_keys, before_four))
    keys = [before_four, before_two, swapped(before_two), from_pair, own_keys]
    cot_all = lax.all_gather(after(cotangent, before_two, before_four), "dp", tiled=True)
    attended, lse, kv = attend(query_pre, cosine, sine, w_expand, blocks, place_q, sequences, keys)
    attention_part = jnp.dot(attended, w_out, preferred_element_type=F32).astype(BF)
    attention = lax.psum(attention_part, "tensor")

    local_ids = rank_dp * experts_local + jnp.arange(experts_local, dtype=jnp.int32)
    routes = jnp.take(route_all.reshape(devices, tok_rows, -1), order, axis=0)
    named_block = jnp.any(routes[..., None] == local_ids, axis=2)
    before = jnp.tril(jnp.ones((tok_rows, tok_rows), BF), -1)
    rank_within = dot("ts,bse->bte", before, named_block.astype(BF))
    slot_of = jnp.where(named_block, rank_within, -1.0)
    slot = slot_of.astype(jnp.int32).transpose(2, 0, 1)[:, :, None, :]
    columns = jnp.arange(experts_local * SLOTS, dtype=jnp.int32)
    spread = (columns[None, :] // SLOTS == jnp.arange(experts_local, dtype=jnp.int32)[:, None]).astype(
        BF
    )
    places = (
        dot("bte,en->btn", slot_of.astype(BF), spread) == (columns % SLOTS).astype(F32)
    ).astype(BF)
    gate_t = expert_gate.swapaxes(1, 2)
    up_t = expert_up.swapaxes(1, 2)
    cot_rows = pick(order, slot, cot_all)
    back = down_back(cot_rows, expert_down)

    attention = after(attention, cot_rows, places)
    middle, *hidden_mid = norm_sum(tokens, attention, middle_gain)
    first = (rank_dp * experts_local).astype(jnp.int32).reshape(1)
    router_rows = jnp.pad(w_router.T, ((0, -all_experts % 128), (0, 0)))
    if direct:
        pair = [swapped(part) for part in hidden_mid]
        by_x = [turned(part, 2) for part in hidden_mid]
        by_y = [turned(part, 4) for part in hidden_mid]
        held = pick_route(first, slot, [hidden_mid, pair], router_rows, all_experts, 0, 1, [])
    else:
        hidden_all = lax.all_gather(jnp.concatenate(hidden_mid, axis=0), "dp", tiled=True)

    top, bottom = hidden_mid
    if direct:
        top = after(top, pair[0])
    shared_active, shared_gate_grad, shared_up_grad, shared_grads = shared_step(
        top, bottom, cotangent, shared_gate.T, shared_up.T, shared_down
    )
    shared_result = jnp.dot(shared_active, shared_down, preferred_element_type=F32)
    mid_from_shared = dot("tf,df->td", shared_gate_grad, shared_gate) + dot(
        "tf,df->td", shared_up_grad, shared_up
    )
    if direct:
        x_top, x_bottom, y_top, y_bottom = lax.optimization_barrier(
            (*by_x, *by_y, held[0], back, shared_grads)
        )[:4]
        by_x, by_y = [x_top, x_bottom], [y_top, y_bottom]
        corner = [turned(y_top, 2), turned(x_bottom, 4)]
        pair_x = [swapped(part) for part in by_x]
        pair_y = [swapped(part) for part in by_y]
        held = pick_route(first, slot, [by_x, by_y], router_rows, all_experts, 2, 1, held)
        held = pick_route(first, slot, [pair_x, pair_y], router_rows, all_experts, 4, 1, held)
        corner[0] = after(corner[0], held[0])
        pair_corner = [swapped(part) for part in corner]
        held = pick_route(first, slot, [corner], router_rows, all_experts, 6, 1, held)
        held = pick_route(first, slot, [pair_corner], router_rows, all_experts, 7, 1, held)
        rows, router_probs, slot_gates = held
        hidden_parts = [*hidden_mid, *pair, *by_x, *by_y, *corner, *pair_x, *pair_y, *pair_corner]
    else:
        rows, router_probs, slot_gates = pick_route(
            first, slot, [[hidden_all]], router_rows, all_experts, 0, devices, []
        )
        hidden_parts = [hidden_all]
    shared_sums = lax.psum_scatter(
        after(shared_grads, rows), "dp", scatter_dimension=1, tiled=True
    )
    gated_active, gate_val_grad, up_val_grad, row_grad, probs_grad = expert_step(
        rows, gate_t, up_t, back, slot, slot_gates
    )
    grad_expert_down = dot(
        "ecf,ecd->efd",
        gated_active[..., :ff_local],
        cot_rows.reshape(experts_local, -1, width),
    )
    if direct:
        put_args = (first, places, row_grad, router_probs, probs_grad, router_rows)
        some = lambda *at: jnp.array(at, jnp.int32)
        to_pair, logits_pair = put_route(some(4, 5, 7), False, *put_args, None)
        from_pair = swapped(to_pair)
        to_sibling, logits_sibling = put_route(some(1), False, *put_args, None)
        from_sibling = swapped(to_sibling)
        send_x, send_y, kept, logits_cross = put_route(some(2, 3, 6), False, *put_args, from_pair)
        send_x, shared_sums = lax.optimization_barrier((send_x, shared_sums))
        got_x = turned(send_x, 2)
        got_y = turned(send_y, 4)
        own, logits_own = put_route(some(0), False, *put_args, from_sibling)
        routed_part = put(order, places, row_out(gated_active, expert_down, devices))
        got_x, got_y, own, routed_part, mid_from_shared = lax.optimization_barrier(
            (got_x, got_y, own, routed_part, mid_from_shared)
        )
        half = tok_rows // 2
        plus = lambda *terms: sum(term.astype(F32) for term in terms)
        last_y = turned(plus(kept[:half], got_x[:half]).astype(BF), 4)
        last_x = turned(plus(kept[half:], got_y[:half]).astype(BF), 2)
        last_y, last_x = lax.optimization_barrier((last_y, last_x, grad_expert_down))[:2]
        mid_block = jnp.concatenate(
            [plus(own[:half], got_x[half:], last_y), plus(own[half:], got_y[half:], last_x)], axis=0
        )
        logit_grads = [logits_own, logits_sibling, logits_cross, logits_pair]
    else:
        mid_part, logit_grad = put_route(
            order, True, first, places, row_grad, router_probs, probs_grad, router_rows, None
        )
        mid_block = scatter_sum(after(mid_part, shared_sums)).astype(F32)
        routed_part = put(order, places, row_out(gated_active, expert_down, devices))
        mid_block = after(mid_block, routed_part, grad_expert_down)
        logit_grads = [logit_grad]
    mid_sum = (mid_block + mid_from_shared).astype(BF)
    routed_block = scatter_sum(routed_part)
    mid_grad = lax.psum(mid_sum, "tensor")
    grad_router = route_grad(logit_grads, hidden_parts)
    ff_part = (routed_block.astype(F32) + shared_result).astype(BF)
    feedforward = lax.psum(after(ff_part, mid_grad), "tensor")
    mid_grad = after(mid_grad, grad_router, ff_part)

    middle_low, middle_grad, attended_grad, grad_middle_gain = norm_back(
        middle, mid_grad, cotangent, middle_gain, w_out
    )
    attended_grad = after(attended_grad, ff_part)
    query_grad, expanded_grad, *window_grads = attend_back(
        query_pre, cosine, sine, w_expand, blocks, place_q, sequences, lse, attended_grad, kv, keys
    )
    four_grad, two_grad, pair_grad, last_grad, keys_grad = window_grads
    pair_grad = swapped(pair_grad)
    last_grad = swapped(last_grad).astype(F32)
    two_grad = (two_grad.astype(F32) + pair_grad.astype(F32)).astype(BF)
    four_grad = (four_grad.astype(F32) + jnp.where(odd == 1, last_grad, 0.0)).astype(BF)
    keys_grad = after(keys_grad, feedforward) + jnp.where(odd == 0, last_grad, 0.0)
    keys_grad = keys_grad + passed_along(two_grad, "dp", -2).astype(F32)
    keys_grad = keys_grad + passed_along(four_grad, "dp", -4).astype(F32)
    latent_raw_grad, grad_latent_gain = norm_backward(latent_raw, latent_gain, keys_grad[:, :KVR])
    rope_raw_grad = rotate_back(keys_grad[:, KVR : KVR + DR], cosine, sine)
    latent_full_grad = jnp.concatenate([latent_raw_grad, rope_raw_grad], axis=-1).astype(BF)
    input_part = dot("tc,dc->td", query_grad, w_query) + dot(
        "tc,dc->td", latent_full_grad, w_latent
    )
    _, grad_input_gain = norm_backward(token_features, input_gain, input_part)

    output = (middle + feedforward.astype(F32)).astype(BF)
    input_part, grad_input_gain = lax.optimization_barrier((input_part.astype(BF), grad_input_gain))
    input_part = after(input_part, feedforward)
    tensors = lax.axis_size("tensor")
    query_width = heads_local * (DN + DR)
    out_width = heads_local * DV
    expand_width = w_expand.shape[1] * KVR // width
    latent_width = KVR + DR
    gains = jnp.concatenate(
        [
            grad_middle_gain / tensors,
            grad_input_gain[None, :],
            jnp.repeat(grad_latent_gain, width // KVR)[None, :],
            jnp.zeros((61, width), F32),
        ],
        axis=0,
    )
    parts = parts_rows(latent_full_grad, hidden_in, grad_router, gains, all_experts)
    parts = lax.psum_scatter(parts, "dp", scatter_dimension=1, tiled=True)
    latents = jnp.concatenate([key[:, :KVR] for key in keys], axis=0)
    grad_expand = dot("wk,wc->kc", latents, after(expanded_grad, keys_grad)).astype(BF)
    share = KVR // devices
    grad_expand = (
        grad_expand.reshape(devices, share, -1, expand_width)
        .transpose(0, 2, 1, 3)
        .reshape(width, expand_width)
    )
    late = jnp.concatenate(
        [
            dot("td,tc->dc", middle_low, attended).astype(BF),
            dot("td,tc->dc", hidden_in, query_grad).astype(BF),
            grad_expand,
        ],
        axis=1,
    )
    rows_late = after(rows, late).reshape(experts_local, -1, width)
    grad_expert_gate = dot("ecd,ecf->edf", rows_late, gate_val_grad[..., :ff_local])
    grad_expert_up = dot("ecd,ecf->edf", rows_late, up_val_grad[..., :ff_local])
    late = scatter_sum(late)
    grad_out_proj, grad_query, grad_expand = finals(late, out_width, query_width, share)
    input_grad = lax.psum(input_part, "tensor")
    input_grad = after(input_grad, grad_expert_gate, grad_expert_up)
    parts = tensor_sum(after(parts, input_grad)).astype(F32)
    (token_grad,) = norm_back(tokens, input_grad, middle_grad, input_gain, None)
    sw = shared_gate.shape[1]
    gain_at = latent_width + all_experts
    return (
        output,
        token_grad,
        parts[gain_at + 1],
        grad_query,
        parts[:latent_width].T,
        parts[gain_at + 2, :: width // KVR],
        grad_expand,
        grad_out_proj,
        parts[gain_at],
        parts[latent_width:gain_at].T,
        grad_expert_gate,
        grad_expert_up,
        grad_expert_down,
        shared_sums[sw : 2 * sw].astype(F32).T,
        shared_sums[2 * sw :].astype(F32).T,
        shared_sums[:sw].astype(F32),
    )


def solution(mesh):
    placed = (
        P("dp", None),
        P(),
        P("dp", None),
        P("dp", None),
        P(),
        P(None, "tensor"),
        P(),
        P(),
        P(None, "tensor"),
        P("tensor", None),
        P(),
        P(),
        P("dp", None, "tensor"),
        P("dp", None, "tensor"),
        P("dp", "tensor", None),
        P(None, "tensor"),
        P(None, "tensor"),
        P("tensor", None),
    )
    return jax.shard_map(
        shards,
        mesh=mesh,
        in_specs=placed,
        out_specs=(
            P("dp", None),
            P("dp", None),
            P("dp"),
            P("dp", "tensor"),
            P("dp", None),
            P("dp"),
            P("dp", "tensor"),
            P("tensor", "dp"),
            P("dp"),
            P("dp", None),
            P("dp", None, "tensor"),
            P("dp", None, "tensor"),
            P("dp", "tensor", None),
            P("dp", "tensor"),
            P("dp", "tensor"),
            P("tensor", "dp"),
        ),
        check_vma=False,
    )
```

```python
import functools

import jax
import jax.numpy as jnp
from jax import lax
from jax.experimental import pallas as pl
from jax.experimental.pallas import tpu as pltpu
from jax.sharding import PartitionSpec as P

DN = 128
DR = 64
DV = 128
KVR = 512
REACH = 4
SLOTS = 80
BF = jnp.bfloat16
F32 = jnp.float32
VMEM_BYTES = 60 * 1024 * 1024
epsilon = 1e-06


def mm(a, b, ca, cb):
    return lax.dot_general(a, b, (((ca,), (cb,)), ((), ())), preferred_element_type=F32)


def cost(flops, nbytes, trans=0):
    return pl.CostEstimate(flops=int(flops), bytes_accessed=int(nbytes), transcendentals=int(trans))


def smem():
    return pl.BlockSpec(memory_space=pltpu.SMEM)


def fixed(shape):
    return pl.BlockSpec(shape, lambda *at: (0,) * len(shape))


def params():
    return pltpu.CompilerParams(vmem_limit_bytes=VMEM_BYTES)


def attend_setup(
    head, heads, step, qp_ref, cos_ref, sin_ref, at_ref, sq_ref, seq_ref, keys, q_ref, key_ref, bias_ref
):
    rows = qp_ref.shape[0]

    @pl.when(head == 0)
    def _():
        for at in range(0, rows, step):
            part = pl.ds(at, step)
            for i in range(len(keys)):
                block = at_ref[i]
                where = pl.multiple_of(jnp.maximum(block, 0) * rows, 128)
                sequence = jnp.where(block >= 0, seq_ref[0:1, pl.ds(where, rows)], -1)
                position = block * rows + lax.broadcasted_iota(jnp.int32, (1, rows), 1)
                allowed = (sq_ref[part, 0:1] == sequence) & (position <= sq_ref[part, 1:2])
                bias_ref[part, i * rows : (i + 1) * rows] = jnp.where(allowed, 0.0, -1e30).astype(BF)
        for i, key in enumerate(keys):
            key_ref[i * rows : (i + 1) * rows, DN:] = key[:, KVR : KVR + DR]

    for k in range(heads):

        @pl.when(head == k)
        def _():
            at = k * (DN + DR)
            front = qp_ref[:, at + DN : at + DN + DR // 2]
            back = qp_ref[:, at + DN + DR // 2 : at + DN + DR]
            cosine, sine = cos_ref[...], sin_ref[...]
            q_ref[:, :DN] = qp_ref[:, at : at + DN].astype(BF)
            q_ref[:, DN : DN + DR // 2] = (front * cosine - back * sine).astype(BF)
            q_ref[:, DN + DR // 2 :] = (back * cosine + front * sine).astype(BF)


def attend_kernel(heads, step, qp_ref, cos_ref, sin_ref, wx_ref, at_ref, sq_ref, seq_ref, *rest):
    keys, (o_ref, lse_ref, kv_ref, q_ref, key_ref, bias_ref) = rest[:-6], rest[-6:]
    rows = qp_ref.shape[0]
    scale = (DN + DR) ** (-0.5)
    attend_setup(
        pl.program_id(0), heads, step, qp_ref, cos_ref, sin_ref, at_ref, sq_ref, seq_ref, keys,
        q_ref, key_ref, bias_ref,
    )
    for i, key in enumerate(keys):
        part = pl.ds(i * rows, rows)
        kv = mm(key[:, :KVR], wx_ref[...], 1, 0).astype(BF)
        kv_ref[part, :] = kv
        key_ref[part, :DN] = kv[:, :DN]
    for at in range(0, rows, step):
        part = pl.ds(at, step)
        s = mm(q_ref[part, :], key_ref[...], 1, 1) * scale + bias_ref[part, :].astype(F32)
        top = jnp.max(s, axis=-1, keepdims=True)
        p = jnp.exp(s - top)
        total = jnp.sum(p, axis=-1, keepdims=True)
        o_ref[part, :] = mm((p * (1.0 / total)).astype(BF), kv_ref[:, DN:], 1, 0).astype(BF)
        lse_ref[0, part, :] = top + jnp.log(total)


def attend_specs(query_pre, cosine, w_expand, blocks, place_q, sequences, keys):
    return [
        fixed(query_pre.shape),
        fixed(cosine.shape),
        fixed(cosine.shape),
        pl.BlockSpec((KVR, DN + DV), lambda h: (0, h)),
        smem(),
        fixed(place_q.shape),
        fixed(sequences.shape),
    ], [fixed(keys[0].shape) for _ in keys]


def attend(query_pre, cosine, sine, w_expand, blocks, place_q, sequences, keys):
    rows = query_pre.shape[0]
    heads = query_pre.shape[1] // (DN + DR)
    window = rows * len(keys)
    specs, key_specs = attend_specs(query_pre, cosine, w_expand, blocks, place_q, sequences, keys)
    return pl.pallas_call(
        functools.partial(attend_kernel, heads, rows // 2),
        name="attend",
        grid=(heads,),
        in_specs=specs + key_specs,
        out_specs=[
            pl.BlockSpec((rows, DV), lambda h: (0, h)),
            pl.BlockSpec((1, rows, 1), lambda h: (h, 0, 0)),
            pl.BlockSpec((window, DN + DV), lambda h: (0, h)),
        ],
        out_shape=[
            jax.ShapeDtypeStruct((rows, heads * DV), BF),
            jax.ShapeDtypeStruct((heads, rows, 1), F32),
            jax.ShapeDtypeStruct((window, heads * (DN + DV)), BF),
        ],
        scratch_shapes=[
            pltpu.VMEM((rows, DN + DR), BF),
            pltpu.VMEM((window, DN + DR), BF),
            pltpu.VMEM((rows, window), BF),
        ],
        compiler_params=params(),
        cost_estimate=cost(
            2 * heads * window * (rows * 384 + KVR * 256), 2 * window * 640, heads * rows * window
        ),
    )(query_pre, cosine, sine, w_expand, blocks, place_q, sequences, *keys)


def attend_back_kernel(
    heads, step, count, qp_ref, cos_ref, sin_ref, wx_ref, at_ref, sq_ref, seq_ref, lse_ref, do_ref, kv_ref,
    *rest
):
    keys, rest = rest[:count], rest[count:]
    dq_ref, dkv_ref = rest[:2]
    grads = rest[2 : 2 + count]
    q_ref, key_ref, bias_ref, dk_ref, dv_ref, acc_ref, dqs_ref = rest[2 + count :]
    rows = qp_ref.shape[0]
    head = pl.program_id(0)
    scale = (DN + DR) ** (-0.5)
    attend_setup(
        head, heads, step, qp_ref, cos_ref, sin_ref, at_ref, sq_ref, seq_ref, keys, q_ref, key_ref, bias_ref
    )
    key_ref[:, :DN] = kv_ref[:, :DN]

    @pl.when(head == 0)
    def _():
        acc_ref[...] = jnp.zeros_like(acc_ref)

    for at in range(0, rows, step):
        part = pl.ds(at, step)
        q = q_ref[part, :]
        do = do_ref[part, :]
        s = mm(q, key_ref[...], 1, 1) * scale + bias_ref[part, :].astype(F32)
        p = jnp.exp(s - lse_ref[0, part, :])
        dp = mm(do, kv_ref[:, DN:], 1, 1)
        ds = (p * (dp - jnp.sum(p * dp, axis=-1, keepdims=True))).astype(BF)
        dqs_ref[part, :] = mm(ds, key_ref[...], 1, 0) * scale
        dk = mm(ds, q, 0, 0) * scale
        dv = mm(p.astype(BF), do, 0, 0)
        if at == 0:
            dk_ref[...] = dk
            dv_ref[...] = dv
        else:
            dk_ref[...] += dk
            dv_ref[...] += dv
    dkv_ref[:, :DN] = dk_ref[:, :DN].astype(BF)
    dkv_ref[:, DN:] = dv_ref[...].astype(BF)
    acc_ref[:, :KVR] += mm(dkv_ref[...], wx_ref[...], 1, 1)
    acc_ref[:, KVR : KVR + DR] += dk_ref[:, DN:]
    for k in range(heads):

        @pl.when(head == k)
        def _():
            at = k * (DN + DR)
            front = dqs_ref[:, DN : DN + DR // 2]
            back = dqs_ref[:, DN + DR // 2 :]
            cosine, sine = cos_ref[...], sin_ref[...]
            dq_ref[:, at : at + DN] = dqs_ref[:, :DN].astype(BF)
            dq_ref[:, at + DN : at + DN + DR // 2] = (front * cosine + back * sine).astype(BF)
            dq_ref[:, at + DN + DR // 2 : at + DN + DR] = (back * cosine - front * sine).astype(BF)

    @pl.when(head == heads - 1)
    def _():
        for i, grad in enumerate(grads):
            grad[...] = acc_ref[i * rows : (i + 1) * rows, :].astype(grad.dtype)


def attend_back(query_pre, cosine, sine, w_expand, blocks, place_q, sequences, lse, attended_grad, kv, keys):
    rows = query_pre.shape[0]
    heads = query_pre.shape[1] // (DN + DR)
    window = rows * len(keys)
    count = len(keys)
    specs, key_specs = attend_specs(query_pre, cosine, w_expand, blocks, place_q, sequences, keys)
    wide = keys[0].shape[1]
    return pl.pallas_call(
        functools.partial(attend_back_kernel, heads, rows // 2, count),
        name="attend_back",
        grid=(heads,),
        in_specs=specs
        + [
            pl.BlockSpec((1, rows, 1), lambda h: (h, 0, 0)),
            pl.BlockSpec((rows, DV), lambda h: (0, h)),
            pl.BlockSpec((window, DN + DV), lambda h: (0, h)),
        ]
        + key_specs,
        out_specs=[fixed(query_pre.shape), pl.BlockSpec((window, DN + DV), lambda h: (0, h))]
        + [fixed((rows, wide)) for _ in keys],
        out_shape=[
            jax.ShapeDtypeStruct(query_pre.shape, BF),
            jax.ShapeDtypeStruct((window, w_expand.shape[1]), BF),
        ]
        + [jax.ShapeDtypeStruct((rows, wide), BF) for _ in keys[1:]]
        + [jax.ShapeDtypeStruct((rows, wide), F32)],
        scratch_shapes=[
            pltpu.VMEM((rows, DN + DR), BF),
            pltpu.VMEM((window, DN + DR), BF),
            pltpu.VMEM((rows, window), BF),
            pltpu.VMEM((window, DN + DR), F32),
            pltpu.VMEM((window, DV), F32),
            pltpu.VMEM((window, wide), F32),
            pltpu.VMEM((rows, DN + DR), F32),
        ],
        compiler_params=params(),
        cost_estimate=cost(window * rows, window * rows),
    )(query_pre, cosine, sine, w_expand, blocks, place_q, sequences, lse, attended_grad, kv, *keys)


def one_hot(slot_ref):
    experts, rows = slot_ref.shape[0], slot_ref.shape[-1]
    place = lax.broadcasted_iota(jnp.int32, (SLOTS, rows), 0)
    return jnp.concatenate(
        [(slot_ref[e, 0] == place).astype(F32).astype(BF) for e in range(experts)], axis=0
    )


def pick_kernel(order_ref, slot_ref, x_ref, o_ref):
    o_ref[...] = mm(one_hot(slot_ref), x_ref[...], 1, 0).astype(BF).reshape(o_ref.shape)


def pick(order, slot, values):
    experts, blocks, _, rows = slot.shape
    width = values.shape[1]
    return pl.pallas_call(
        pick_kernel,
        name="pick",
        grid_spec=pltpu.PrefetchScalarGridSpec(
            num_scalar_prefetch=1,
            grid=(blocks,),
            in_specs=[
                pl.BlockSpec((experts, 1, 1, rows), lambda b, o: (0, b, 0, 0)),
                pl.BlockSpec((rows, width), lambda b, o: (o[b], 0)),
            ],
            out_specs=pl.BlockSpec((experts, 1, SLOTS, width), lambda b, o: (0, b, 0, 0)),
        ),
        out_shape=jax.ShapeDtypeStruct((experts, blocks, SLOTS, width), BF),
        compiler_params=params(),
        cost_estimate=cost(
            2 * experts * blocks * SLOTS * rows * width,
            2 * blocks * width * (rows + experts * SLOTS),
        ),
    )(order, slot, values)


def pick_route_kernel(count, pieces, parts, first_ref, slot_ref, w_ref, *refs):
    o_ref, p_ref, g_ref = refs[-3:]
    experts, rows = slot_ref.shape[0], slot_ref.shape[3]
    size = rows // parts
    for n in range(pieces):
        place = lax.broadcasted_iota(jnp.int32, (SLOTS, rows), 0)
        chosen = jnp.concatenate(
            [(slot_ref[i, n] == place).astype(F32).astype(BF) for i in range(experts)], axis=0
        )
        picked, taken = 0.0, 0.0
        for m in range(parts):
            x = refs[n * parts + m][...]
            logits = mm(x, w_ref[...], 1, 1)
            lane = lax.broadcasted_iota(jnp.int32, logits.shape, 1)
            logits = jnp.where(lane < count, logits, -1e30)
            e = jnp.exp(logits - jnp.max(logits, axis=-1, keepdims=True))
            probs = e / jnp.sum(e, axis=-1, keepdims=True)
            p_ref[n * rows + m * size : n * rows + (m + 1) * size, :] = probs
            high = probs.astype(BF)
            low = (probs - high.astype(F32)).astype(BF)
            part = chosen[:, m * size : (m + 1) * size]
            picked += mm(part, x, 1, 0)
            taken += mm(part, high, 1, 0) + mm(part, low, 1, 0)
        o_ref[:, n] = picked.astype(BF).reshape(experts, SLOTS, -1)
        lane = lax.broadcasted_iota(jnp.int32, (SLOTS, taken.shape[1]), 1)
        for i in range(experts):
            part = taken[i * SLOTS : (i + 1) * SLOTS, :]
            g_ref[i, n] = jnp.sum(
                jnp.where(lane == first_ref[0] + i, part, 0.0), axis=-1, keepdims=True
            )


def pick_route(first, slot, values, router_rows, count, at, steps, earlier):
    experts, blocks, _, rows = slot.shape
    parts = len(values[0])
    pieces = len(values)
    values = [part for value in values for part in value]
    width = values[0].shape[1]
    lanes = router_rows.shape[0]
    at = at // pieces
    whole = pl.BlockSpec(memory_space=pl.ANY)
    return pl.pallas_call(
        functools.partial(pick_route_kernel, count, pieces, parts),
        name="pick_route",
        grid=(steps,),
        in_specs=[
            smem(),
            pl.BlockSpec((experts, pieces, 1, rows), lambda b: (0, at + b, 0, 0)),
            fixed(router_rows.shape),
        ]
        + [pl.BlockSpec((rows // parts, width), lambda b: (b, 0)) for _ in values]
        + [whole for _ in earlier],
        out_specs=[
            pl.BlockSpec((experts, pieces, SLOTS, width), lambda b: (0, at + b, 0, 0)),
            pl.BlockSpec((pieces * rows, lanes), lambda b: (at + b, 0)),
            pl.BlockSpec((experts, pieces, SLOTS, 1), lambda b: (0, at + b, 0, 0)),
        ],
        out_shape=[
            jax.ShapeDtypeStruct((experts, blocks, SLOTS, width), BF),
            jax.ShapeDtypeStruct((blocks * rows, lanes), F32),
            jax.ShapeDtypeStruct((experts, blocks, SLOTS, 1), F32),
        ],
        input_output_aliases={3 + len(values) + i: i for i in range(len(earlier))},
        compiler_params=params(),
        cost_estimate=cost(pieces * steps * rows * width, pieces * steps * width * rows),
    )(first, slot, router_rows, *values, *earlier)


def route_grad_kernel(count, *refs):
    total = 0.0
    grads, values = refs[:count], refs[count:-1]
    which, at = 0, 0
    for ref in values:
        size = ref.shape[0]
        total += mm(grads[which][at : at + size, :], ref[...], 0, 0)
        at += size
        if at == grads[which].shape[0]:
            which, at = which + 1, 0
    refs[-1][...] = total.astype(BF)


def route_grad(grads, values):
    width = values[0].shape[1]
    lanes = grads[0].shape[1]
    return pl.pallas_call(
        functools.partial(route_grad_kernel, len(grads)),
        name="route_grad",
        grid=(1,),
        in_specs=[fixed(array.shape) for array in [*grads, *values]],
        out_specs=fixed((lanes, width)),
        out_shape=jax.ShapeDtypeStruct((lanes, width), BF),
        compiler_params=params(),
        cost_estimate=cost(lanes * width, lanes * width),
    )(*grads, *values)


def parts_kernel(lg_ref, x_ref, route_ref, gain_ref, o_ref):
    inner = lg_ref.shape[1]
    count = o_ref.shape[0] - inner - gain_ref.shape[0]
    o_ref[:inner, :] = mm(lg_ref[...], x_ref[...], 0, 0).astype(BF)
    o_ref[inner : inner + count, :] = route_ref[:count, :]
    o_ref[inner + count :, :] = gain_ref[...].astype(BF)


def parts_rows(latent_grad, values, route, gains, count):
    width = values.shape[1]
    shape = (latent_grad.shape[1] + count + gains.shape[0], width)
    return pl.pallas_call(
        parts_kernel,
        name="parts_rows",
        grid=(1,),
        in_specs=[fixed(array.shape) for array in (latent_grad, values, route, gains)],
        out_specs=fixed(shape),
        out_shape=jax.ShapeDtypeStruct(shape, BF),
        compiler_params=params(),
        cost_estimate=cost(width, width),
    )(latent_grad, values, route, gains)


def put_kernel(order_ref, place_ref, r_ref, o_ref):
    o_ref[...] = mm(place_ref[0], r_ref[...].reshape(-1, r_ref.shape[-1]), 1, 0).astype(BF)


def returned(first_ref, place_ref, r_ref, p_ref, pg_ref, w_ref):
    experts, rows = pg_ref.shape[0], pg_ref.shape[3]
    by_expert = jnp.concatenate(
        [pg_ref[i, 0] for i in range(experts)] + [jnp.zeros((1, rows), F32)] * (-experts % 8), axis=0
    )
    high = by_expert.astype(BF)
    low = (by_expert - high.astype(F32)).astype(BF)
    probs = p_ref[...]
    shape = (by_expert.shape[0], probs.shape[1])
    expert = lax.broadcasted_iota(jnp.int32, shape, 0)
    lane = lax.broadcasted_iota(jnp.int32, shape, 1)
    spread = (lane == first_ref[0] + expert) & (expert < experts)
    spread = spread.astype(F32).astype(BF)
    grad = mm(high, spread, 0, 0) + mm(low, spread, 0, 0)
    back = (probs * (grad - jnp.sum(probs * grad, axis=-1, keepdims=True))).astype(BF)
    total = mm(place_ref[0], r_ref[...].reshape(-1, r_ref.shape[-1]), 1, 0)
    return total + mm(back, w_ref[...], 1, 0), back


def put_route_kernel(
    order_ref, first_ref, place_ref, r_ref, p_ref, pg_ref, w_ref, *rest
):
    total, back = returned(first_ref, place_ref, r_ref, p_ref, pg_ref, w_ref)
    if len(rest) == 3:
        total += rest[0][...].astype(F32)
    rest[-2][...] = total.astype(BF)
    rest[-1][...] = back


def put_cross_kernel(
    order_ref, first_ref, place_ref, r_ref, p_ref, pg_ref, w_ref, add_ref,
    sx_ref, sy_ref, keep_ref, lg_ref,
):
    total, back = returned(first_ref, place_ref, r_ref, p_ref, pg_ref, w_ref)
    lg_ref[...] = back
    total = (total + add_ref[...].astype(F32)).astype(BF)
    half = total.shape[0] // 2
    top, bottom = total[:half], total[half:]
    step = pl.program_id(0)

    @pl.when(step == 0)
    def _():
        sx_ref[half:, :] = top
        keep_ref[half:, :] = bottom

    @pl.when(step == 1)
    def _():
        sy_ref[half:, :] = bottom
        keep_ref[:half, :] = top

    @pl.when(step == 2)
    def _():
        sx_ref[:half, :] = top
        sy_ref[:half, :] = bottom


def put_specs(places, picked):
    blocks, rows, slots = places.shape
    experts, width = picked.shape[0], picked.shape[3]
    return [
        pl.BlockSpec((1, rows, slots), lambda b, o: (b, 0, 0)),
        pl.BlockSpec((experts, 1, SLOTS, width), lambda b, o: (0, b, 0, 0)),
    ]


def put(order, places, picked):
    blocks, rows, _ = places.shape
    width = picked.shape[3]
    return pl.pallas_call(
        put_kernel,
        name="put",
        grid_spec=pltpu.PrefetchScalarGridSpec(
            num_scalar_prefetch=1,
            grid=(blocks,),
            in_specs=put_specs(places, picked),
            out_specs=pl.BlockSpec((rows, width), lambda b, o: (o[b], 0)),
        ),
        out_shape=jax.ShapeDtypeStruct((blocks * rows, width), BF),
        compiler_params=params(),
        cost_estimate=cost(blocks * rows * width, blocks * rows * width),
    )(order, places, picked)


def put_route(order, absolute, first, places, picked, probs, probs_grad, router_rows, added):
    _, rows, slots = places.shape
    blocks = order.shape[0]
    experts, width = picked.shape[0], picked.shape[3]
    lanes = probs.shape[1]
    come = (lambda b, o: b) if absolute else (lambda b, o: o[b])
    go = (lambda b, o: o[b]) if absolute else (lambda b, o: b)
    cross = added is not None and blocks == 3
    whole = pl.BlockSpec((rows, width), lambda b, o: (0, 0))
    out_specs = [whole] * 3 if cross else [pl.BlockSpec((rows, width), lambda b, o: (go(b, o), 0))]
    sizes = [rows] * 3 if cross else [blocks * rows]
    more = [] if added is None else [added]
    return pl.pallas_call(
        put_cross_kernel if cross else put_route_kernel,
        name="put_route",
        grid_spec=pltpu.PrefetchScalarGridSpec(
            num_scalar_prefetch=1,
            grid=(blocks,),
            in_specs=[
                smem(),
                pl.BlockSpec((1, rows, slots), lambda b, o: (come(b, o), 0, 0)),
                pl.BlockSpec((experts, 1, SLOTS, width), lambda b, o: (0, come(b, o), 0, 0)),
                pl.BlockSpec((rows, lanes), lambda b, o: (come(b, o), 0)),
                pl.BlockSpec((experts, 1, 1, rows), lambda b, o: (0, come(b, o), 0, 0)),
                fixed(router_rows.shape),
            ]
            + [pl.BlockSpec((rows, width), lambda b, o: (b, 0)) for _ in more],
            out_specs=out_specs + [pl.BlockSpec((rows, lanes), lambda b, o: (b, 0))],
        ),
        out_shape=[jax.ShapeDtypeStruct((size, width), BF) for size in sizes]
        + [jax.ShapeDtypeStruct((blocks * rows, lanes), BF)],
        compiler_params=params(),
        cost_estimate=cost(blocks * rows * width, blocks * rows * width),
    )(order, first, places, picked, probs, probs_grad, router_rows, *more)


def down_back_kernel(x_ref, w_ref, o_ref):
    ff = w_ref.shape[1]
    wide = o_ref.shape[-1]
    back = mm(x_ref[...].reshape(-1, x_ref.shape[-1]), w_ref[0], 1, 1)
    o_ref[0, :, :ff] = back
    if wide > ff:
        o_ref[0, :, ff:] = jnp.zeros((o_ref.shape[1], wide - ff), F32)


def down_back(rows, down):
    experts, blocks, slots, width = rows.shape
    ff = down.shape[1]
    wide = -(-ff // 128) * 128
    count = blocks * slots
    return pl.pallas_call(
        down_back_kernel,
        name="down_back",
        grid=(experts,),
        in_specs=[
            pl.BlockSpec((1, blocks, slots, width), lambda e: (e, 0, 0, 0)),
            pl.BlockSpec((1, ff, width), lambda e: (e, 0, 0)),
        ],
        out_specs=pl.BlockSpec((1, count, wide), lambda e: (e, 0, 0)),
        out_shape=jax.ShapeDtypeStruct((experts, count, wide), F32),
        compiler_params=params(),
        cost_estimate=cost(
            experts * count * width,
            experts * count * ff,
        ),
    )(rows, down)


def row_out_kernel(x_ref, w_ref, o_ref):
    ff = w_ref.shape[1]
    o_ref[...] = mm(x_ref[0, :, :ff], w_ref[0], 1, 0).astype(BF).reshape(o_ref.shape)


def row_out(active, down, blocks):
    experts, count, wide = active.shape
    ff, width = down.shape[1:]
    slots = count // blocks
    return pl.pallas_call(
        row_out_kernel,
        name="row_out",
        grid=(experts,),
        in_specs=[
            pl.BlockSpec((1, count, wide), lambda e: (e, 0, 0)),
            pl.BlockSpec((1, ff, width), lambda e: (e, 0, 0)),
        ],
        out_specs=pl.BlockSpec((1, blocks, slots, width), lambda e: (e, 0, 0, 0)),
        out_shape=jax.ShapeDtypeStruct((experts, blocks, slots, width), BF),
        compiler_params=params(),
        cost_estimate=cost(count * width, count * width),
    )(active, down)


def expert_kernel(
    x_ref, gate_ref, up_ref, back_ref, slot_ref, sg_ref,
    ga_ref, dg_ref, du_ref, dx_ref, pg_ref, w_ref, d_ref,
):
    ff = gate_ref.shape[1]
    wide = back_ref.shape[2]
    blocks, rows = slot_ref.shape[1], slot_ref.shape[3]

    @pl.when(pl.program_id(0) == 0)
    def _():
        w_ref[...] = jnp.zeros_like(w_ref)

    w_ref[:ff, :] = gate_ref[0]
    w_ref[wide : wide + ff, :] = up_ref[0]
    x = x_ref[...].reshape(-1, x_ref.shape[-1])
    both = mm(x, w_ref[...], 1, 1)
    a = both[:, :wide]
    b = both[:, wide:]
    place = lax.broadcasted_iota(jnp.int32, (SLOTS, rows), 0)
    slot_gate = sg_ref[...].reshape(-1, 1)
    back = back_ref[0]
    sig = jax.nn.sigmoid(a)
    swish = a * sig
    active = swish * b
    gate_grad = jnp.sum(active * back, axis=-1, keepdims=True)
    for i in range(blocks):
        part = gate_grad[i * SLOTS : (i + 1) * SLOTS, :]
        pg_ref[0, i] = jnp.sum(
            jnp.where(slot_ref[0, i] == place, part, 0.0), axis=0, keepdims=True
        )
    gated = back * slot_gate
    ga_ref[0] = (active * slot_gate).astype(BF)
    dg = (gated * b * (sig + swish * (1.0 - sig))).astype(BF)
    du = (gated * swish).astype(BF)
    dg_ref[0] = dg
    du_ref[0] = du
    d_ref[:, :wide] = dg
    d_ref[:, wide:] = du
    dx_ref[...] = mm(d_ref[...], w_ref[...], 1, 0).astype(BF).reshape(dx_ref.shape)


def expert_step(rows, gate_t, up_t, back, slot, slot_gates):
    experts, blocks, slots, width = rows.shape
    ff = gate_t.shape[1]
    wide = back.shape[2]
    count = blocks * slots
    whole = pl.BlockSpec((1, blocks, slots, width), lambda e: (e, 0, 0, 0))
    flat = lambda n: pl.BlockSpec((1, count, n), lambda e: (e, 0, 0))
    shape = lambda n, dtype: jax.ShapeDtypeStruct((experts, count, n), dtype)
    weight = pl.BlockSpec((1, ff, width), lambda e: (e, 0, 0))
    by_token = pl.BlockSpec((1,) + slot.shape[1:], lambda e: (e, 0, 0, 0))
    return pl.pallas_call(
        expert_kernel,
        name="expert_step",
        grid=(experts,),
        in_specs=[
            whole,
            weight,
            weight,
            flat(wide),
            by_token,
            pl.BlockSpec((1, blocks, slots, 1), lambda e: (e, 0, 0, 0)),
        ],
        out_specs=[flat(wide), flat(wide), flat(wide), whole, by_token],
        out_shape=[
            shape(wide, BF),
            shape(wide, BF),
            shape(wide, BF),
            jax.ShapeDtypeStruct(rows.shape, BF),
            jax.ShapeDtypeStruct(slot.shape, F32),
        ],
        scratch_shapes=[pltpu.VMEM((2 * wide, width), BF), pltpu.VMEM((count, 2 * wide), BF)],
        compiler_params=params(),
        cost_estimate=cost(
            8 * experts * count * width * wide,
            2 * experts * (2 * count * width + 2 * width * wide + 5 * count * wide),
            experts * count * wide,
        ),
    )(rows, gate_t, up_t, back, slot, slot_gates)


def norm_kernel(x_ref, add_ref, gain_ref, sum_ref, top_ref, bottom_ref):
    x = x_ref[...].astype(F32) + add_ref[...].astype(F32)
    sum_ref[...] = x
    scale = lax.rsqrt(jnp.mean(x * x, axis=-1, keepdims=True) + epsilon)
    out = (x * scale * gain_ref[...]).astype(BF)

    @pl.when(pl.program_id(0) < 2)
    def _():
        top_ref[...] = out

    @pl.when(pl.program_id(0) >= 2)
    def _():
        bottom_ref[...] = out


def norm_sum(values, added, gain):
    rows, width = values.shape
    block = pl.BlockSpec((rows // 4, width), lambda i: (i, 0))
    half = jax.ShapeDtypeStruct((rows // 2, width), BF)
    return pl.pallas_call(
        norm_kernel,
        name="norm_sum",
        grid=(4,),
        in_specs=[block, block, fixed((1, width))],
        out_specs=[
            block,
            pl.BlockSpec((rows // 4, width), lambda i: (jnp.minimum(i, 1), 0)),
            pl.BlockSpec((rows // 4, width), lambda i: (jnp.maximum(i - 2, 0), 0)),
        ],
        out_shape=[jax.ShapeDtypeStruct((rows, width), F32), half, half],
        compiler_params=params(),
        cost_estimate=cost(8 * rows * width, 10 * rows * width),
    )(values, added, gain.reshape(1, width))


def norm_back_kernel(x_ref, up_ref, res_ref, gain_ref, *rest):
    x = x_ref[...].astype(F32)
    up = up_ref[...].astype(F32)
    scale = lax.rsqrt(jnp.mean(x * x, axis=-1, keepdims=True) + epsilon)
    scaled = x * scale
    if len(rest) > 1:
        gain_grad_ref = rest[4]

        @pl.when(pl.program_id(0) == 0)
        def _():
            gain_grad_ref[...] = jnp.zeros_like(gain_grad_ref)

        gain_grad_ref[...] += jnp.sum(up * scaled, axis=0, keepdims=True)
    up = up * gain_ref[...]
    back = scale * (up - scaled * jnp.mean(up * scaled, axis=-1, keepdims=True))
    total = res_ref[...].astype(F32) + back
    if len(rest) == 1:
        rest[0][...] = total.astype(BF)
        return
    w_ref, low_ref, total_ref, out_ref = rest[:4]
    low = total.astype(BF)
    low_ref[...] = low
    total_ref[...] = total
    out_ref[...] = mm(low, w_ref[...], 1, 1).astype(BF)


def norm_back(values, upstream, residual, gain, weight):
    rows, width = values.shape
    block = pl.BlockSpec((rows // 4, width), lambda i: (i, 0))
    in_specs = [block, block, block, fixed((1, width))]
    out_specs = [block]
    shapes = [jax.ShapeDtypeStruct((rows, width), BF)]
    more = []
    if weight is not None:
        inner = weight.shape[0]
        more = [weight]
        in_specs += [fixed(weight.shape)]
        out_specs += [
            block,
            pl.BlockSpec((rows // 4, inner), lambda i: (i, 0)),
            fixed((1, width)),
        ]
        shapes += [
            jax.ShapeDtypeStruct((rows, width), F32),
            jax.ShapeDtypeStruct((rows, inner), BF),
            jax.ShapeDtypeStruct((1, width), F32),
        ]
    return pl.pallas_call(
        norm_back_kernel,
        name="norm_back",
        grid=(4,),
        in_specs=in_specs,
        out_specs=out_specs,
        out_shape=shapes,
        compiler_params=params(),
        cost_estimate=cost(12 * rows * width, 12 * rows * width),
    )(values, upstream, residual, gain.reshape(1, width), *more)


def shared_kernel(top_ref, bottom_ref, up_ref, wg_ref, wu_ref, wd_ref, act_ref, dg_ref, du_ref, grad_ref):
    ff = wd_ref.shape[0]
    x = jnp.concatenate([top_ref[...], bottom_ref[...]], axis=0)
    upstream = up_ref[...]
    a = mm(x, wg_ref[...], 1, 1)
    b = mm(x, wu_ref[...], 1, 1)
    back = mm(upstream, wd_ref[...], 1, 1)
    sig = jax.nn.sigmoid(a)
    swish = a * sig
    active = (swish * b).astype(BF)
    dg = (back * b * (sig + swish * (1.0 - sig))).astype(BF)
    du = (back * swish).astype(BF)
    act_ref[...] = active
    dg_ref[...] = dg
    du_ref[...] = du
    grad_ref[:ff, :] = mm(active, upstream, 0, 0).astype(BF)
    grad_ref[ff : 2 * ff, :] = mm(dg, x, 0, 0).astype(BF)
    grad_ref[2 * ff :, :] = mm(du, x, 0, 0).astype(BF)


def shared_step(top, bottom, upstream, gate_t, up_t, down):
    rows, width = upstream.shape
    ff = down.shape[0]
    inner = jax.ShapeDtypeStruct((rows, ff), BF)
    return pl.pallas_call(
        shared_kernel,
        name="shared_step",
        grid=(1,),
        in_specs=[fixed(top.shape)] * 2 + [fixed((rows, width))] + [fixed((ff, width))] * 3,
        out_specs=[fixed((rows, ff))] * 3 + [fixed((3 * ff, width))],
        out_shape=[inner, inner, inner, jax.ShapeDtypeStruct((3 * ff, width), BF)],
        compiler_params=params(),
        cost_estimate=cost(rows * width, rows * width),
    )(top, bottom, upstream, gate_t, up_t, down)


def finals_kernel(x_ref, proj_ref, query_ref, expand_ref):
    inner, rows = proj_ref.shape
    wide = query_ref.shape[1]
    part = x_ref.shape[1] - inner - wide
    count = expand_ref.shape[0]
    proj_ref[...] = x_ref[:, :inner].astype(F32).T
    query_ref[...] = x_ref[:, inner : inner + wide].astype(F32)
    for i in range(rows // count):
        expand_ref[:, i * part : (i + 1) * part] = x_ref[
            i * count : (i + 1) * count, inner + wide :
        ].astype(F32)


def finals(joined, inner, wide, count):
    rows = joined.shape[0]
    part = joined.shape[1] - inner - wide
    shapes = [(inner, rows), (rows, wide), (count, rows // count * part)]
    return pl.pallas_call(
        finals_kernel,
        name="finals",
        grid=(1,),
        in_specs=[fixed(joined.shape)],
        out_specs=[fixed(shape) for shape in shapes],
        out_shape=[jax.ShapeDtypeStruct(shape, F32) for shape in shapes],
        compiler_params=params(),
        cost_estimate=cost(rows, rows),
    )(joined)


def weight_grad_kernel(a_ref, x_ref, o_ref):
    ff = o_ref.shape[1]
    x = x_ref[...].reshape(-1, x_ref.shape[-1])
    o_ref[0] = mm(a_ref[0, :, :ff], x, 0, 0)


def weight_grad(active, rows, ff):
    experts, blocks, slots, width = rows.shape
    count, wide = active.shape[1:]
    return pl.pallas_call(
        weight_grad_kernel,
        name="weight_grad",
        grid=(experts,),
        in_specs=[
            pl.BlockSpec((1, count, wide), lambda e: (e, 0, 0)),
            pl.BlockSpec((1, blocks, slots, width), lambda e: (e, 0, 0, 0)),
        ],
        out_specs=pl.BlockSpec((1, ff, width), lambda e: (e, 0, 0)),
        out_shape=jax.ShapeDtypeStruct((experts, ff, width), F32),
        compiler_params=params(),
        cost_estimate=cost(count * width, count * width),
    )(active, rows)


def split_kernel(x_ref, *outs):
    at = 0
    for out in outs:
        out[...] = x_ref[at : at + out.shape[0], :].astype(F32)
        at += out.shape[0]


def split_rows(joined, sizes):
    width = joined.shape[1]
    return pl.pallas_call(
        split_kernel,
        name="split_rows",
        grid=(1,),
        in_specs=[fixed(joined.shape)],
        out_specs=[fixed((size, width)) for size in sizes],
        out_shape=[jax.ShapeDtypeStruct((size, width), F32) for size in sizes],
        compiler_params=params(),
        cost_estimate=cost(width, width),
    )(joined)


def dot(eq, a, b):
    return jnp.einsum(eq, a, b, preferred_element_type=F32)


def passed_along(shard, axis, by):
    peers = lax.axis_size(axis)
    pairs = [(i, i + by) for i in range(peers) if 0 <= i + by < peers]
    return lax.ppermute(shard, axis, pairs)


def normed(values, norm_gain):
    return (
        values * lax.rsqrt(jnp.mean(values * values, axis=-1, keepdims=True) + epsilon) * norm_gain
    )


def norm_backward(values, norm_gain, upstream):
    _, pullback = jax.vjp(normed, values, norm_gain)
    return pullback(upstream)


def rotate(values, cosine, sine):
    half = values.shape[-1] // 2
    front, back = values[..., :half], values[..., half:]
    return jnp.concatenate([front * cosine - back * sine, back * cosine + front * sine], axis=-1)


def rotate_back(upstream, cosine, sine):
    return rotate(upstream, cosine, -sine)


def silu_gate(gate_val, up_val):
    return gate_val * jax.nn.sigmoid(gate_val) * up_val


def silu_backward(gate_val, up_val, upstream):
    _, pullback = jax.vjp(silu_gate, gate_val, up_val)
    return pullback(upstream)


def rope_tables(seq_all, seq_here, index_here):
    starts = jnp.sum((seq_all[None, :] < seq_here[:, None]).astype(jnp.int32), axis=1)
    position = (index_here - starts).astype(F32)
    frequency = 10000.0 ** (-(jnp.arange(DR // 2, dtype=F32) * 2.0) / DR)
    angle = position[:, None] * frequency[None, :]
    return jnp.cos(angle), jnp.sin(angle)


def turned(value, by):
    return lax.ppermute(value, "dp", [(i, i ^ by) for i in range(lax.axis_size("dp"))])


def swapped(value):
    return turned(value, 1)


def after(value, *others):
    return lax.optimization_barrier((value,) + others)[0]


def scatter_sum(parts):
    joined = parts if not isinstance(parts, list) else jnp.concatenate(parts, axis=1)
    return lax.psum_scatter(joined, "dp", scatter_dimension=0, tiled=True)


def tensor_sum(value, first):
    peers = lax.axis_size("tensor")
    rank = lax.axis_index("tensor")
    size = value.shape[0] // peers
    piece = lambda at: lax.dynamic_slice_in_dim(value, at * size, size, 0)
    turn = lambda piece, by: lax.ppermute(
        piece, "tensor", [(i, (i + by) % peers) for i in range(peers)]
    )
    total = piece(rank).astype(F32)
    for by in range(1, peers):
        total = total + turn(piece((rank + by) % peers), by).astype(F32)
    mine = after(total.astype(BF), first)
    around = [turn(mine, by) for by in range(peers - 1, 0, -1)] + [mine]
    both = jnp.concatenate(around + around[:-1], axis=0)
    return lax.dynamic_slice_in_dim(both, (peers - 1 - rank) * size, value.shape[0], 0)


def shards(
    tokens,
    seq_ids,
    route_ids,
    cotangent,
    input_gain,
    w_query,
    w_latent,
    latent_gain,
    w_expand,
    w_out,
    middle_gain,
    w_router,
    expert_gate,
    expert_up,
    expert_down,
    shared_gate,
    shared_up,
    shared_down,
):
    devices = lax.axis_size("dp")
    rank_dp = lax.axis_index("dp")
    tok_rows, width = tokens.shape
    experts_local = expert_gate.shape[0]
    all_experts = w_router.shape[1]
    ff_local = expert_gate.shape[2]
    heads_local = w_query.shape[1] // (DN + DR)

    direct = devices == 8
    apart = jnp.array([0, 1, 2, 4, 3, 5, 6, 7] if direct else list(range(devices)), jnp.int32)
    order = (rank_dp ^ apart) if direct else apart

    index_here = rank_dp * tok_rows + jnp.arange(tok_rows, dtype=jnp.int32)
    seq_here = lax.dynamic_slice_in_dim(seq_ids, rank_dp * tok_rows, tok_rows, 0)
    cosine, sine = rope_tables(seq_ids, seq_here, index_here)
    token_features = tokens.astype(F32)
    hidden_in = normed(token_features, input_gain).astype(BF)
    latent_full = jnp.dot(hidden_in, w_latent, preferred_element_type=F32)
    latent_raw = latent_full[:, :KVR]
    latent = normed(latent_raw, latent_gain).astype(BF)
    rope_key = rotate(latent_full[:, KVR:], cosine, sine).astype(BF)
    fill = jnp.zeros((tok_rows, -(KVR + DR) % 128), BF)
    own_keys = jnp.concatenate([latent, rope_key, fill], axis=1)
    odd = rank_dp % 2
    blocks = jnp.stack(
        [rank_dp - 4, rank_dp - 2, (rank_dp - 2) ^ 1, rank_dp - 3 + 2 * odd, rank_dp]
    ).astype(jnp.int32)
    place_q = jnp.stack([seq_here, index_here], axis=1)
    sequences = seq_ids.reshape(1, -1)
    before_two = passed_along(own_keys, "dp", 2)
    before_four = passed_along(own_keys, "dp", 4)
    query_pre = jnp.dot(hidden_in, w_query, preferred_element_type=F32)
    route_all = lax.all_gather(after(route_ids, query_pre), "dp", tiled=True)
    before_four = after(before_four, query_pre, place_q, route_all)
    from_pair = swapped(jnp.where(odd == 0, own_keys, before_four))
    keys = [before_four, before_two, swapped(before_two), from_pair, own_keys]
    cot_all = lax.all_gather(after(cotangent, before_two, before_four), "dp", tiled=True)
    attended, lse, kv = attend(query_pre, cosine, sine, w_expand, blocks, place_q, sequences, keys)
    attention_part = jnp.dot(attended, w_out, preferred_element_type=F32).astype(BF)
    attention = lax.psum(attention_part, "tensor")

    local_ids = rank_dp * experts_local + jnp.arange(experts_local, dtype=jnp.int32)
    routes = jnp.take(route_all.reshape(devices, tok_rows, -1), order, axis=0)
    named_block = jnp.any(routes[..., None] == local_ids, axis=2)
    before = jnp.tril(jnp.ones((tok_rows, tok_rows), BF), -1)
    rank_within = dot("ts,bse->bte", before, named_block.astype(BF))
    slot_of = jnp.where(named_block, rank_within, -1.0)
    slot = slot_of.astype(jnp.int32).transpose(2, 0, 1)[:, :, None, :]
    columns = jnp.arange(experts_local * SLOTS, dtype=jnp.int32)
    spread = (columns[None, :] // SLOTS == jnp.arange(experts_local, dtype=jnp.int32)[:, None]).astype(
        BF
    )
    places = (
        dot("bte,en->btn", slot_of.astype(BF), spread) == (columns % SLOTS).astype(F32)
    ).astype(BF)
    gate_t = expert_gate.swapaxes(1, 2)
    up_t = expert_up.swapaxes(1, 2)
    cot_rows = pick(order, slot, cot_all)
    back = down_back(cot_rows, expert_down)

    attention = after(attention, cot_rows, places)
    middle, *hidden_mid = norm_sum(tokens, attention, middle_gain)
    first = (rank_dp * experts_local).astype(jnp.int32).reshape(1)
    router_rows = jnp.pad(w_router.T, ((0, -all_experts % 128), (0, 0)))
    if direct:
        pair = [swapped(part) for part in hidden_mid]
        by_x = [turned(part, 2) for part in hidden_mid]
        by_y = [turned(part, 4) for part in hidden_mid]
        held = pick_route(first, slot, [hidden_mid, pair], router_rows, all_experts, 0, 1, [])
    else:
        hidden_all = lax.all_gather(jnp.concatenate(hidden_mid, axis=0), "dp", tiled=True)

    top, bottom = hidden_mid
    if direct:
        top = after(top, pair[0])
    shared_active, shared_gate_grad, shared_up_grad, shared_grads = shared_step(
        top, bottom, cotangent, shared_gate.T, shared_up.T, shared_down
    )
    shared_result = jnp.dot(shared_active, shared_down, preferred_element_type=F32)
    if direct:
        x_top, x_bottom, y_top, y_bottom = lax.optimization_barrier(
            (*by_x, *by_y, held[0], back, shared_grads)
        )[:4]
        by_x, by_y = [x_top, x_bottom], [y_top, y_bottom]
        corner = [turned(y_top, 2), turned(x_bottom, 4)]
        pair_x = [swapped(part) for part in by_x]
        pair_y = [swapped(part) for part in by_y]
        held = pick_route(first, slot, [by_x, by_y], router_rows, all_experts, 2, 1, held)
        held = pick_route(first, slot, [pair_x, pair_y], router_rows, all_experts, 4, 1, held)
        corner[0] = after(corner[0], held[0])
        pair_corner = [swapped(part) for part in corner]
        held = pick_route(first, slot, [corner], router_rows, all_experts, 6, 1, held)
        held = pick_route(first, slot, [pair_corner], router_rows, all_experts, 7, 1, held)
        rows, router_probs, slot_gates = held
        hidden_parts = [*hidden_mid, *pair, *by_x, *by_y, *corner, *pair_x, *pair_y, *pair_corner]
    else:
        rows, router_probs, slot_gates = pick_route(
            first, slot, [[hidden_all]], router_rows, all_experts, 0, devices, []
        )
        hidden_parts = [hidden_all]
    shared_sums = lax.psum_scatter(
        after(shared_grads, rows), "dp", scatter_dimension=1, tiled=True
    )
    gated_active, gate_val_grad, up_val_grad, row_grad, probs_grad = expert_step(
        rows, gate_t, up_t, back, slot, slot_gates
    )
    if direct:
        put_args = (first, places, row_grad, router_probs, probs_grad, router_rows)
        some = lambda *at: jnp.array(at, jnp.int32)
        to_pair, logits_pair = put_route(some(4, 5, 7), False, *put_args, None)
        from_pair = swapped(to_pair)
        to_sibling, logits_sibling = put_route(some(1), False, *put_args, None)
        from_sibling = swapped(to_sibling)
        send_x, send_y, kept, logits_cross = put_route(some(2, 3, 6), False, *put_args, from_pair)
        send_x, shared_sums = lax.optimization_barrier((send_x, shared_sums))
        got_x = turned(send_x, 2)
        got_y = turned(send_y, 4)
        routed_part = put(order, places, row_out(gated_active, expert_down, devices))
        got_x, got_y, routed_part, from_sibling = lax.optimization_barrier(
            (got_x, got_y, routed_part, from_sibling)
        )
        shared_gate_grad = after(shared_gate_grad, routed_part)
        mid_from_shared = dot("tf,df->td", shared_gate_grad, shared_gate) + dot(
            "tf,df->td", shared_up_grad, shared_up
        )
        own, logits_own = put_route(some(0), False, *put_args, from_sibling)
        half = tok_rows // 2
        plus = lambda *terms: sum(term.astype(F32) for term in terms)
        last_y = turned(plus(kept[:half], got_x[:half]).astype(BF), 4)
        last_x = turned(plus(kept[half:], got_y[:half]).astype(BF), 2)
        last_y, last_x = lax.optimization_barrier((last_y, last_x, own, mid_from_shared))[:2]
        mid_block = jnp.concatenate(
            [plus(own[:half], got_x[half:], last_y), plus(own[half:], got_y[half:], last_x)], axis=0
        )
        logit_grads = [logits_own, logits_sibling, logits_cross, logits_pair]
    else:
        mid_part, logit_grad = put_route(
            order, True, first, places, row_grad, router_probs, probs_grad, router_rows, None
        )
        mid_block = scatter_sum(after(mid_part, shared_sums)).astype(F32)
        routed_part = put(order, places, row_out(gated_active, expert_down, devices))
        mid_block = after(mid_block, routed_part)
        shared_gate_grad = after(shared_gate_grad, routed_part)
        mid_from_shared = dot("tf,df->td", shared_gate_grad, shared_gate) + dot(
            "tf,df->td", shared_up_grad, shared_up
        )
        logit_grads = [logit_grad]
    mid_sum = (mid_block + mid_from_shared).astype(BF)
    routed_block = scatter_sum(routed_part)
    mid_grad = lax.psum(mid_sum, "tensor")
    grad_router = route_grad(logit_grads, hidden_parts)
    ff_part = (routed_block.astype(F32) + shared_result).astype(BF)
    feedforward = lax.psum(after(ff_part, mid_grad), "tensor")
    grad_expert_down = weight_grad(after(gated_active, mid_sum), cot_rows, ff_local)
    mid_grad = after(mid_grad, grad_router, ff_part, grad_expert_down)

    middle_low, middle_grad, attended_grad, grad_middle_gain = norm_back(
        middle, mid_grad, cotangent, middle_gain, w_out
    )
    attended_grad = after(attended_grad, ff_part)
    query_grad, expanded_grad, *window_grads = attend_back(
        query_pre, cosine, sine, w_expand, blocks, place_q, sequences, lse, attended_grad, kv, keys
    )
    four_grad, two_grad, pair_grad, last_grad, keys_grad = window_grads
    pair_grad = swapped(pair_grad)
    last_grad = swapped(last_grad).astype(F32)
    two_grad = (two_grad.astype(F32) + pair_grad.astype(F32)).astype(BF)
    four_grad = (four_grad.astype(F32) + jnp.where(odd == 1, last_grad, 0.0)).astype(BF)
    keys_grad = after(keys_grad, feedforward) + jnp.where(odd == 0, last_grad, 0.0)
    keys_grad = keys_grad + passed_along(two_grad, "dp", -2).astype(F32)
    keys_grad = keys_grad + passed_along(four_grad, "dp", -4).astype(F32)
    latent_raw_grad, grad_latent_gain = norm_backward(latent_raw, latent_gain, keys_grad[:, :KVR])
    rope_raw_grad = rotate_back(keys_grad[:, KVR : KVR + DR], cosine, sine)
    latent_full_grad = jnp.concatenate([latent_raw_grad, rope_raw_grad], axis=-1).astype(BF)
    input_part = dot("tc,dc->td", query_grad, w_query) + dot(
        "tc,dc->td", latent_full_grad, w_latent
    )
    _, grad_input_gain = norm_backward(token_features, input_gain, input_part)

    output = (middle + feedforward.astype(F32)).astype(BF)
    input_part, grad_input_gain = lax.optimization_barrier((input_part.astype(BF), grad_input_gain))
    input_part = after(input_part, feedforward)
    tensors = lax.axis_size("tensor")
    query_width = heads_local * (DN + DR)
    out_width = heads_local * DV
    expand_width = w_expand.shape[1] * KVR // width
    latent_width = KVR + DR
    gains = jnp.concatenate(
        [
            grad_middle_gain / tensors,
            grad_input_gain[None, :],
            jnp.repeat(grad_latent_gain, width // KVR)[None, :],
            jnp.zeros((61, width), F32),
        ],
        axis=0,
    )
    parts = parts_rows(latent_full_grad, hidden_in, grad_router, gains, all_experts)
    parts = lax.psum_scatter(parts, "dp", scatter_dimension=1, tiled=True)
    latents = jnp.concatenate([key[:, :KVR] for key in keys], axis=0)
    grad_expand = dot("wk,wc->kc", latents, after(expanded_grad, keys_grad)).astype(BF)
    share = KVR // devices
    grad_expand = (
        grad_expand.reshape(devices, share, -1, expand_width)
        .transpose(0, 2, 1, 3)
        .reshape(width, expand_width)
    )
    late = jnp.concatenate(
        [
            dot("td,tc->dc", middle_low, attended).astype(BF),
            dot("td,tc->dc", hidden_in, query_grad).astype(BF),
            grad_expand,
        ],
        axis=1,
    )
    rows_late = after(rows, late).reshape(experts_local, -1, width)
    grad_expert_gate = dot("ecd,ecf->edf", rows_late, gate_val_grad[..., :ff_local])
    grad_expert_up = dot("ecd,ecf->edf", rows_late, up_val_grad[..., :ff_local])
    late = scatter_sum(late)
    grad_out_proj, grad_query, grad_expand = finals(late, out_width, query_width, share)
    input_grad = lax.psum(input_part, "tensor")
    input_grad = after(input_grad, grad_expert_gate, grad_expert_up)
    (token_grad,) = norm_back(tokens, input_grad, middle_grad, input_gain, None)
    parts = tensor_sum(after(parts, input_grad), token_grad)
    latent_part, router_part, gain_part = split_rows(
        parts, [latent_width, all_experts, gains.shape[0]]
    )
    sw = shared_gate.shape[1]
    return (
        output,
        token_grad,
        gain_part[1],
        grad_query,
        latent_part.T,
        gain_part[2, :: width // KVR],
        grad_expand,
        grad_out_proj,
        gain_part[0],
        router_part.T,
        grad_expert_gate,
        grad_expert_up,
        grad_expert_down,
        shared_sums[sw : 2 * sw].astype(F32).T,
        shared_sums[2 * sw :].astype(F32).T,
        shared_sums[:sw].astype(F32),
    )


def solution(mesh):
    placed = (
        P("dp", None),
        P(),
        P("dp", None),
        P("dp", None),
        P(),
        P(None, "tensor"),
        P(),
        P(),
        P(None, "tensor"),
        P("tensor", None),
        P(),
        P(),
        P("dp", None, "tensor"),
        P("dp", None, "tensor"),
        P("dp", "tensor", None),
        P(None, "tensor"),
        P(None, "tensor"),
        P("tensor", None),
    )
    return jax.shard_map(
        shards,
        mesh=mesh,
        in_specs=placed,
        out_specs=(
            P("dp", None),
            P("dp", None),
            P("dp"),
            P("dp", "tensor"),
            P("dp", None),
            P("dp"),
            P("dp", "tensor"),
            P("tensor", "dp"),
            P("dp"),
            P("dp", None),
            P("dp", None, "tensor"),
            P("dp", None, "tensor"),
            P("dp", "tensor", None),
            P("dp", "tensor"),
            P("dp", "tensor"),
            P("tensor", "dp"),
        ),
        check_vma=False,
    )
```

```python
import functools

import jax
import jax.numpy as jnp
from jax import lax
from jax.experimental import pallas as pl
from jax.experimental.pallas import tpu as pltpu
from jax.sharding import PartitionSpec as P

DN = 128
DR = 64
DV = 128
KVR = 512
REACH = 4
SLOTS = 80
BF = jnp.bfloat16
F32 = jnp.float32
VMEM_BYTES = 60 * 1024 * 1024
epsilon = 1e-06


def mm(a, b, ca, cb):
    return lax.dot_general(a, b, (((ca,), (cb,)), ((), ())), preferred_element_type=F32)


def cost(flops, nbytes, trans=0):
    return pl.CostEstimate(flops=int(flops), bytes_accessed=int(nbytes), transcendentals=int(trans))


def smem():
    return pl.BlockSpec(memory_space=pltpu.SMEM)


def fixed(shape):
    return pl.BlockSpec(shape, lambda *at: (0,) * len(shape))


def params():
    return pltpu.CompilerParams(vmem_limit_bytes=VMEM_BYTES)


def attend_setup(
    head, heads, step, qp_ref, cos_ref, sin_ref, at_ref, sq_ref, seq_ref, keys, q_ref, key_ref, bias_ref
):
    rows = qp_ref.shape[0]

    @pl.when(head == 0)
    def _():
        for at in range(0, rows, step):
            part = pl.ds(at, step)
            for i in range(len(keys)):
                block = at_ref[i]
                where = pl.multiple_of(jnp.maximum(block, 0) * rows, 128)
                sequence = jnp.where(block >= 0, seq_ref[0:1, pl.ds(where, rows)], -1)
                position = block * rows + lax.broadcasted_iota(jnp.int32, (1, rows), 1)
                allowed = (sq_ref[part, 0:1] == sequence) & (position <= sq_ref[part, 1:2])
                bias_ref[part, i * rows : (i + 1) * rows] = jnp.where(allowed, 0.0, -1e30).astype(BF)
        for i, key in enumerate(keys):
            key_ref[i * rows : (i + 1) * rows, DN:] = key[:, KVR : KVR + DR]

    for k in range(heads):

        @pl.when(head == k)
        def _():
            at = k * (DN + DR)
            front = qp_ref[:, at + DN : at + DN + DR // 2]
            back = qp_ref[:, at + DN + DR // 2 : at + DN + DR]
            cosine, sine = cos_ref[...], sin_ref[...]
            q_ref[:, :DN] = qp_ref[:, at : at + DN].astype(BF)
            q_ref[:, DN : DN + DR // 2] = (front * cosine - back * sine).astype(BF)
            q_ref[:, DN + DR // 2 :] = (back * cosine + front * sine).astype(BF)


def attend_kernel(heads, step, qp_ref, cos_ref, sin_ref, wx_ref, at_ref, sq_ref, seq_ref, *rest):
    keys, (o_ref, lse_ref, kv_ref, q_ref, key_ref, bias_ref) = rest[:-6], rest[-6:]
    rows = qp_ref.shape[0]
    scale = (DN + DR) ** (-0.5)
    attend_setup(
        pl.program_id(0), heads, step, qp_ref, cos_ref, sin_ref, at_ref, sq_ref, seq_ref, keys,
        q_ref, key_ref, bias_ref,
    )
    for i, key in enumerate(keys):
        part = pl.ds(i * rows, rows)
        kv = mm(key[:, :KVR], wx_ref[...], 1, 0).astype(BF)
        kv_ref[part, :] = kv
        key_ref[part, :DN] = kv[:, :DN]
    for at in range(0, rows, step):
        part = pl.ds(at, step)
        s = mm(q_ref[part, :], key_ref[...], 1, 1) * scale + bias_ref[part, :].astype(F32)
        top = jnp.max(s, axis=-1, keepdims=True)
        p = jnp.exp(s - top)
        total = jnp.sum(p, axis=-1, keepdims=True)
        o_ref[part, :] = mm((p * (1.0 / total)).astype(BF), kv_ref[:, DN:], 1, 0).astype(BF)
        lse_ref[0, part, :] = top + jnp.log(total)


def attend_specs(query_pre, cosine, w_expand, blocks, place_q, sequences, keys):
    return [
        fixed(query_pre.shape),
        fixed(cosine.shape),
        fixed(cosine.shape),
        pl.BlockSpec((KVR, DN + DV), lambda h: (0, h)),
        smem(),
        fixed(place_q.shape),
        fixed(sequences.shape),
    ], [fixed(keys[0].shape) for _ in keys]


def attend(query_pre, cosine, sine, w_expand, blocks, place_q, sequences, keys):
    rows = query_pre.shape[0]
    heads = query_pre.shape[1] // (DN + DR)
    window = rows * len(keys)
    specs, key_specs = attend_specs(query_pre, cosine, w_expand, blocks, place_q, sequences, keys)
    return pl.pallas_call(
        functools.partial(attend_kernel, heads, rows // 2),
        name="attend",
        grid=(heads,),
        in_specs=specs + key_specs,
        out_specs=[
            pl.BlockSpec((rows, DV), lambda h: (0, h)),
            pl.BlockSpec((1, rows, 1), lambda h: (h, 0, 0)),
            pl.BlockSpec((window, DN + DV), lambda h: (0, h)),
        ],
        out_shape=[
            jax.ShapeDtypeStruct((rows, heads * DV), BF),
            jax.ShapeDtypeStruct((heads, rows, 1), F32),
            jax.ShapeDtypeStruct((window, heads * (DN + DV)), BF),
        ],
        scratch_shapes=[
            pltpu.VMEM((rows, DN + DR), BF),
            pltpu.VMEM((window, DN + DR), BF),
            pltpu.VMEM((rows, window), BF),
        ],
        compiler_params=params(),
        cost_estimate=cost(
            2 * heads * window * (rows * 384 + KVR * 256), 2 * window * 640, heads * rows * window
        ),
    )(query_pre, cosine, sine, w_expand, blocks, place_q, sequences, *keys)


def attend_back_kernel(
    heads, step, count, qp_ref, cos_ref, sin_ref, wx_ref, at_ref, sq_ref, seq_ref, lse_ref, do_ref, kv_ref,
    *rest
):
    keys, rest = rest[:count], rest[count:]
    dq_ref, dkv_ref = rest[:2]
    grads = rest[2 : 2 + count]
    q_ref, key_ref, bias_ref, dk_ref, dv_ref, acc_ref, dqs_ref = rest[2 + count :]
    rows = qp_ref.shape[0]
    head = pl.program_id(0)
    scale = (DN + DR) ** (-0.5)
    attend_setup(
        head, heads, step, qp_ref, cos_ref, sin_ref, at_ref, sq_ref, seq_ref, keys, q_ref, key_ref, bias_ref
    )
    key_ref[:, :DN] = kv_ref[:, :DN]

    @pl.when(head == 0)
    def _():
        acc_ref[...] = jnp.zeros_like(acc_ref)

    for at in range(0, rows, step):
        part = pl.ds(at, step)
        q = q_ref[part, :]
        do = do_ref[part, :]
        s = mm(q, key_ref[...], 1, 1) * scale + bias_ref[part, :].astype(F32)
        p = jnp.exp(s - lse_ref[0, part, :])
        dp = mm(do, kv_ref[:, DN:], 1, 1)
        ds = (p * (dp - jnp.sum(p * dp, axis=-1, keepdims=True))).astype(BF)
        dqs_ref[part, :] = mm(ds, key_ref[...], 1, 0) * scale
        dk = mm(ds, q, 0, 0) * scale
        dv = mm(p.astype(BF), do, 0, 0)
        if at == 0:
            dk_ref[...] = dk
            dv_ref[...] = dv
        else:
            dk_ref[...] += dk
            dv_ref[...] += dv
    dkv_ref[:, :DN] = dk_ref[:, :DN].astype(BF)
    dkv_ref[:, DN:] = dv_ref[...].astype(BF)
    acc_ref[:, :KVR] += mm(dkv_ref[...], wx_ref[...], 1, 1)
    acc_ref[:, KVR : KVR + DR] += dk_ref[:, DN:]
    for k in range(heads):

        @pl.when(head == k)
        def _():
            at = k * (DN + DR)
            front = dqs_ref[:, DN : DN + DR // 2]
            back = dqs_ref[:, DN + DR // 2 :]
            cosine, sine = cos_ref[...], sin_ref[...]
            dq_ref[:, at : at + DN] = dqs_ref[:, :DN].astype(BF)
            dq_ref[:, at + DN : at + DN + DR // 2] = (front * cosine + back * sine).astype(BF)
            dq_ref[:, at + DN + DR // 2 : at + DN + DR] = (back * cosine - front * sine).astype(BF)

    @pl.when(head == heads - 1)
    def _():
        for i, grad in enumerate(grads):
            grad[...] = acc_ref[i * rows : (i + 1) * rows, :].astype(grad.dtype)


def attend_back(query_pre, cosine, sine, w_expand, blocks, place_q, sequences, lse, attended_grad, kv, keys):
    rows = query_pre.shape[0]
    heads = query_pre.shape[1] // (DN + DR)
    window = rows * len(keys)
    count = len(keys)
    specs, key_specs = attend_specs(query_pre, cosine, w_expand, blocks, place_q, sequences, keys)
    wide = keys[0].shape[1]
    return pl.pallas_call(
        functools.partial(attend_back_kernel, heads, rows // 2, count),
        name="attend_back",
        grid=(heads,),
        in_specs=specs
        + [
            pl.BlockSpec((1, rows, 1), lambda h: (h, 0, 0)),
            pl.BlockSpec((rows, DV), lambda h: (0, h)),
            pl.BlockSpec((window, DN + DV), lambda h: (0, h)),
        ]
        + key_specs,
        out_specs=[fixed(query_pre.shape), pl.BlockSpec((window, DN + DV), lambda h: (0, h))]
        + [fixed((rows, wide)) for _ in keys],
        out_shape=[
            jax.ShapeDtypeStruct(query_pre.shape, BF),
            jax.ShapeDtypeStruct((window, w_expand.shape[1]), BF),
        ]
        + [jax.ShapeDtypeStruct((rows, wide), BF) for _ in keys[1:]]
        + [jax.ShapeDtypeStruct((rows, wide), F32)],
        scratch_shapes=[
            pltpu.VMEM((rows, DN + DR), BF),
            pltpu.VMEM((window, DN + DR), BF),
            pltpu.VMEM((rows, window), BF),
            pltpu.VMEM((window, DN + DR), F32),
            pltpu.VMEM((window, DV), F32),
            pltpu.VMEM((window, wide), F32),
            pltpu.VMEM((rows, DN + DR), F32),
        ],
        compiler_params=params(),
        cost_estimate=cost(window * rows, window * rows),
    )(query_pre, cosine, sine, w_expand, blocks, place_q, sequences, lse, attended_grad, kv, *keys)


def one_hot(slot_ref):
    experts, rows = slot_ref.shape[0], slot_ref.shape[-1]
    place = lax.broadcasted_iota(jnp.int32, (SLOTS, rows), 0)
    return jnp.concatenate(
        [(slot_ref[e, 0] == place).astype(F32).astype(BF) for e in range(experts)], axis=0
    )


def pick_kernel(order_ref, slot_ref, x_ref, o_ref):
    o_ref[...] = mm(one_hot(slot_ref), x_ref[...], 1, 0).astype(BF).reshape(o_ref.shape)


def pick(order, slot, values):
    experts, blocks, _, rows = slot.shape
    width = values.shape[1]
    return pl.pallas_call(
        pick_kernel,
        name="pick",
        grid_spec=pltpu.PrefetchScalarGridSpec(
            num_scalar_prefetch=1,
            grid=(blocks,),
            in_specs=[
                pl.BlockSpec((experts, 1, 1, rows), lambda b, o: (0, b, 0, 0)),
                pl.BlockSpec((rows, width), lambda b, o: (o[b], 0)),
            ],
            out_specs=pl.BlockSpec((experts, 1, SLOTS, width), lambda b, o: (0, b, 0, 0)),
        ),
        out_shape=jax.ShapeDtypeStruct((experts, blocks, SLOTS, width), BF),
        compiler_params=params(),
        cost_estimate=cost(
            2 * experts * blocks * SLOTS * rows * width,
            2 * blocks * width * (rows + experts * SLOTS),
        ),
    )(order, slot, values)


def pick_route_kernel(count, pieces, parts, first_ref, slot_ref, w_ref, *refs):
    o_ref, p_ref, g_ref = refs[-3:]
    experts, rows = slot_ref.shape[0], slot_ref.shape[3]
    size = rows // parts
    for n in range(pieces):
        place = lax.broadcasted_iota(jnp.int32, (SLOTS, rows), 0)
        chosen = jnp.concatenate(
            [(slot_ref[i, n] == place).astype(F32).astype(BF) for i in range(experts)], axis=0
        )
        picked, taken = 0.0, 0.0
        for m in range(parts):
            x = refs[n * parts + m][...]
            logits = mm(x, w_ref[...], 1, 1)
            lane = lax.broadcasted_iota(jnp.int32, logits.shape, 1)
            logits = jnp.where(lane < count, logits, -1e30)
            e = jnp.exp(logits - jnp.max(logits, axis=-1, keepdims=True))
            probs = e / jnp.sum(e, axis=-1, keepdims=True)
            p_ref[n * rows + m * size : n * rows + (m + 1) * size, :] = probs
            high = probs.astype(BF)
            low = (probs - high.astype(F32)).astype(BF)
            part = chosen[:, m * size : (m + 1) * size]
            picked += mm(part, x, 1, 0)
            taken += mm(part, high, 1, 0) + mm(part, low, 1, 0)
        o_ref[:, n] = picked.astype(BF).reshape(experts, SLOTS, -1)
        lane = lax.broadcasted_iota(jnp.int32, (SLOTS, taken.shape[1]), 1)
        for i in range(experts):
            part = taken[i * SLOTS : (i + 1) * SLOTS, :]
            g_ref[i, n] = jnp.sum(
                jnp.where(lane == first_ref[0] + i, part, 0.0), axis=-1, keepdims=True
            )


def pick_route(first, slot, values, router_rows, count, at, steps, earlier):
    experts, blocks, _, rows = slot.shape
    parts = len(values[0])
    pieces = len(values)
    values = [part for value in values for part in value]
    width = values[0].shape[1]
    lanes = router_rows.shape[0]
    at = at // pieces
    whole = pl.BlockSpec(memory_space=pl.ANY)
    return pl.pallas_call(
        functools.partial(pick_route_kernel, count, pieces, parts),
        name="pick_route",
        grid=(steps,),
        in_specs=[
            smem(),
            pl.BlockSpec((experts, pieces, 1, rows), lambda b: (0, at + b, 0, 0)),
            fixed(router_rows.shape),
        ]
        + [pl.BlockSpec((rows // parts, width), lambda b: (b, 0)) for _ in values]
        + [whole for _ in earlier],
        out_specs=[
            pl.BlockSpec((experts, pieces, SLOTS, width), lambda b: (0, at + b, 0, 0)),
            pl.BlockSpec((pieces * rows, lanes), lambda b: (at + b, 0)),
            pl.BlockSpec((experts, pieces, SLOTS, 1), lambda b: (0, at + b, 0, 0)),
        ],
        out_shape=[
            jax.ShapeDtypeStruct((experts, blocks, SLOTS, width), BF),
            jax.ShapeDtypeStruct((blocks * rows, lanes), F32),
            jax.ShapeDtypeStruct((experts, blocks, SLOTS, 1), F32),
        ],
        input_output_aliases={3 + len(values) + i: i for i in range(len(earlier))},
        compiler_params=params(),
        cost_estimate=cost(pieces * steps * rows * width, pieces * steps * width * rows),
    )(first, slot, router_rows, *values, *earlier)


def route_grad_kernel(count, *refs):
    total = 0.0
    grads, values = refs[:count], refs[count:-1]
    which, at = 0, 0
    for ref in values:
        size = ref.shape[0]
        total += mm(grads[which][at : at + size, :], ref[...], 0, 0)
        at += size
        if at == grads[which].shape[0]:
            which, at = which + 1, 0
    refs[-1][...] = total.astype(BF)


def route_grad(grads, values):
    width = values[0].shape[1]
    lanes = grads[0].shape[1]
    return pl.pallas_call(
        functools.partial(route_grad_kernel, len(grads)),
        name="route_grad",
        grid=(1,),
        in_specs=[fixed(array.shape) for array in [*grads, *values]],
        out_specs=fixed((lanes, width)),
        out_shape=jax.ShapeDtypeStruct((lanes, width), BF),
        compiler_params=params(),
        cost_estimate=cost(lanes * width, lanes * width),
    )(*grads, *values)


def parts_kernel(lg_ref, x_ref, route_ref, gain_ref, o_ref):
    inner = lg_ref.shape[1]
    count = o_ref.shape[0] - inner - gain_ref.shape[0]
    o_ref[:inner, :] = mm(lg_ref[...], x_ref[...], 0, 0).astype(BF)
    o_ref[inner : inner + count, :] = route_ref[:count, :]
    o_ref[inner + count :, :] = gain_ref[...].astype(BF)


def parts_rows(latent_grad, values, route, gains, count):
    width = values.shape[1]
    shape = (latent_grad.shape[1] + count + gains.shape[0], width)
    return pl.pallas_call(
        parts_kernel,
        name="parts_rows",
        grid=(1,),
        in_specs=[fixed(array.shape) for array in (latent_grad, values, route, gains)],
        out_specs=fixed(shape),
        out_shape=jax.ShapeDtypeStruct(shape, BF),
        compiler_params=params(),
        cost_estimate=cost(width, width),
    )(latent_grad, values, route, gains)


def put_kernel(order_ref, place_ref, r_ref, o_ref):
    o_ref[...] = mm(place_ref[0], r_ref[...].reshape(-1, r_ref.shape[-1]), 1, 0).astype(BF)


def returned(first_ref, place_ref, r_ref, p_ref, pg_ref, w_ref):
    experts, rows = pg_ref.shape[0], pg_ref.shape[3]
    by_expert = jnp.concatenate(
        [pg_ref[i, 0] for i in range(experts)] + [jnp.zeros((1, rows), F32)] * (-experts % 8), axis=0
    )
    high = by_expert.astype(BF)
    low = (by_expert - high.astype(F32)).astype(BF)
    probs = p_ref[...]
    shape = (by_expert.shape[0], probs.shape[1])
    expert = lax.broadcasted_iota(jnp.int32, shape, 0)
    lane = lax.broadcasted_iota(jnp.int32, shape, 1)
    spread = (lane == first_ref[0] + expert) & (expert < experts)
    spread = spread.astype(F32).astype(BF)
    grad = mm(high, spread, 0, 0) + mm(low, spread, 0, 0)
    back = (probs * (grad - jnp.sum(probs * grad, axis=-1, keepdims=True))).astype(BF)
    total = mm(place_ref[0], r_ref[...].reshape(-1, r_ref.shape[-1]), 1, 0)
    return total + mm(back, w_ref[...], 1, 0), back


def put_route_kernel(
    order_ref, first_ref, place_ref, r_ref, p_ref, pg_ref, w_ref, *rest
):
    total, back = returned(first_ref, place_ref, r_ref, p_ref, pg_ref, w_ref)
    if len(rest) == 3:
        total += rest[0][...].astype(F32)
    rest[-2][...] = total.astype(BF)
    rest[-1][...] = back


def put_cross_kernel(
    order_ref, first_ref, place_ref, r_ref, p_ref, pg_ref, w_ref, add_ref,
    sx_ref, sy_ref, keep_ref, lg_ref,
):
    total, back = returned(first_ref, place_ref, r_ref, p_ref, pg_ref, w_ref)
    lg_ref[...] = back
    total = (total + add_ref[...].astype(F32)).astype(BF)
    half = total.shape[0] // 2
    top, bottom = total[:half], total[half:]
    step = pl.program_id(0)

    @pl.when(step == 0)
    def _():
        sx_ref[half:, :] = top
        keep_ref[half:, :] = bottom

    @pl.when(step == 1)
    def _():
        sy_ref[half:, :] = bottom
        keep_ref[:half, :] = top

    @pl.when(step == 2)
    def _():
        sx_ref[:half, :] = top
        sy_ref[:half, :] = bottom


def put_specs(places, picked):
    blocks, rows, slots = places.shape
    experts, width = picked.shape[0], picked.shape[3]
    return [
        pl.BlockSpec((1, rows, slots), lambda b, o: (b, 0, 0)),
        pl.BlockSpec((experts, 1, SLOTS, width), lambda b, o: (0, b, 0, 0)),
    ]


def put(order, places, picked):
    blocks, rows, _ = places.shape
    width = picked.shape[3]
    return pl.pallas_call(
        put_kernel,
        name="put",
        grid_spec=pltpu.PrefetchScalarGridSpec(
            num_scalar_prefetch=1,
            grid=(blocks,),
            in_specs=put_specs(places, picked),
            out_specs=pl.BlockSpec((rows, width), lambda b, o: (o[b], 0)),
        ),
        out_shape=jax.ShapeDtypeStruct((blocks * rows, width), BF),
        compiler_params=params(),
        cost_estimate=cost(blocks * rows * width, blocks * rows * width),
    )(order, places, picked)


def put_route(order, absolute, first, places, picked, probs, probs_grad, router_rows, added):
    _, rows, slots = places.shape
    blocks = order.shape[0]
    experts, width = picked.shape[0], picked.shape[3]
    lanes = probs.shape[1]
    come = (lambda b, o: b) if absolute else (lambda b, o: o[b])
    go = (lambda b, o: o[b]) if absolute else (lambda b, o: b)
    cross = added is not None and blocks == 3
    whole = pl.BlockSpec((rows, width), lambda b, o: (0, 0))
    out_specs = [whole] * 3 if cross else [pl.BlockSpec((rows, width), lambda b, o: (go(b, o), 0))]
    sizes = [rows] * 3 if cross else [blocks * rows]
    more = [] if added is None else [added]
    return pl.pallas_call(
        put_cross_kernel if cross else put_route_kernel,
        name="put_route",
        grid_spec=pltpu.PrefetchScalarGridSpec(
            num_scalar_prefetch=1,
            grid=(blocks,),
            in_specs=[
                smem(),
                pl.BlockSpec((1, rows, slots), lambda b, o: (come(b, o), 0, 0)),
                pl.BlockSpec((experts, 1, SLOTS, width), lambda b, o: (0, come(b, o), 0, 0)),
                pl.BlockSpec((rows, lanes), lambda b, o: (come(b, o), 0)),
                pl.BlockSpec((experts, 1, 1, rows), lambda b, o: (0, come(b, o), 0, 0)),
                fixed(router_rows.shape),
            ]
            + [pl.BlockSpec((rows, width), lambda b, o: (b, 0)) for _ in more],
            out_specs=out_specs + [pl.BlockSpec((rows, lanes), lambda b, o: (b, 0))],
        ),
        out_shape=[jax.ShapeDtypeStruct((size, width), BF) for size in sizes]
        + [jax.ShapeDtypeStruct((blocks * rows, lanes), BF)],
        compiler_params=params(),
        cost_estimate=cost(blocks * rows * width, blocks * rows * width),
    )(order, first, places, picked, probs, probs_grad, router_rows, *more)


def down_back_kernel(x_ref, w_ref, o_ref):
    ff = w_ref.shape[1]
    wide = o_ref.shape[-1]
    back = mm(x_ref[...].reshape(-1, x_ref.shape[-1]), w_ref[0], 1, 1)
    o_ref[0, :, :ff] = back
    if wide > ff:
        o_ref[0, :, ff:] = jnp.zeros((o_ref.shape[1], wide - ff), F32)


def down_back(rows, down):
    experts, blocks, slots, width = rows.shape
    ff = down.shape[1]
    wide = -(-ff // 128) * 128
    count = blocks * slots
    return pl.pallas_call(
        down_back_kernel,
        name="down_back",
        grid=(experts,),
        in_specs=[
            pl.BlockSpec((1, blocks, slots, width), lambda e: (e, 0, 0, 0)),
            pl.BlockSpec((1, ff, width), lambda e: (e, 0, 0)),
        ],
        out_specs=pl.BlockSpec((1, count, wide), lambda e: (e, 0, 0)),
        out_shape=jax.ShapeDtypeStruct((experts, count, wide), F32),
        compiler_params=params(),
        cost_estimate=cost(
            experts * count * width,
            experts * count * ff,
        ),
    )(rows, down)


def row_out_kernel(x_ref, w_ref, o_ref):
    ff = w_ref.shape[1]
    o_ref[...] = mm(x_ref[0, :, :ff], w_ref[0], 1, 0).astype(BF).reshape(o_ref.shape)


def row_out(active, down, blocks):
    experts, count, wide = active.shape
    ff, width = down.shape[1:]
    slots = count // blocks
    return pl.pallas_call(
        row_out_kernel,
        name="row_out",
        grid=(experts,),
        in_specs=[
            pl.BlockSpec((1, count, wide), lambda e: (e, 0, 0)),
            pl.BlockSpec((1, ff, width), lambda e: (e, 0, 0)),
        ],
        out_specs=pl.BlockSpec((1, blocks, slots, width), lambda e: (e, 0, 0, 0)),
        out_shape=jax.ShapeDtypeStruct((experts, blocks, slots, width), BF),
        compiler_params=params(),
        cost_estimate=cost(count * width, count * width),
    )(active, down)


def expert_kernel(
    x_ref, gate_ref, up_ref, back_ref, slot_ref, sg_ref,
    ga_ref, dg_ref, du_ref, dx_ref, pg_ref, w_ref, d_ref,
):
    ff = gate_ref.shape[1]
    wide = back_ref.shape[2]
    blocks, rows = slot_ref.shape[1], slot_ref.shape[3]

    @pl.when(pl.program_id(0) == 0)
    def _():
        w_ref[...] = jnp.zeros_like(w_ref)

    w_ref[:ff, :] = gate_ref[0]
    w_ref[wide : wide + ff, :] = up_ref[0]
    x = x_ref[...].reshape(-1, x_ref.shape[-1])
    both = mm(x, w_ref[...], 1, 1)
    a = both[:, :wide]
    b = both[:, wide:]
    place = lax.broadcasted_iota(jnp.int32, (SLOTS, rows), 0)
    slot_gate = sg_ref[...].reshape(-1, 1)
    back = back_ref[0]
    sig = jax.nn.sigmoid(a)
    swish = a * sig
    active = swish * b
    gate_grad = jnp.sum(active * back, axis=-1, keepdims=True)
    for i in range(blocks):
        part = gate_grad[i * SLOTS : (i + 1) * SLOTS, :]
        pg_ref[0, i] = jnp.sum(
            jnp.where(slot_ref[0, i] == place, part, 0.0), axis=0, keepdims=True
        )
    gated = back * slot_gate
    ga_ref[0] = (active * slot_gate).astype(BF)
    dg = (gated * b * (sig + swish * (1.0 - sig))).astype(BF)
    du = (gated * swish).astype(BF)
    dg_ref[0] = dg
    du_ref[0] = du
    d_ref[:, :wide] = dg
    d_ref[:, wide:] = du
    dx_ref[...] = mm(d_ref[...], w_ref[...], 1, 0).astype(BF).reshape(dx_ref.shape)


def expert_step(rows, gate_t, up_t, back, slot, slot_gates):
    experts, blocks, slots, width = rows.shape
    ff = gate_t.shape[1]
    wide = back.shape[2]
    count = blocks * slots
    whole = pl.BlockSpec((1, blocks, slots, width), lambda e: (e, 0, 0, 0))
    flat = lambda n: pl.BlockSpec((1, count, n), lambda e: (e, 0, 0))
    shape = lambda n, dtype: jax.ShapeDtypeStruct((experts, count, n), dtype)
    weight = pl.BlockSpec((1, ff, width), lambda e: (e, 0, 0))
    by_token = pl.BlockSpec((1,) + slot.shape[1:], lambda e: (e, 0, 0, 0))
    return pl.pallas_call(
        expert_kernel,
        name="expert_step",
        grid=(experts,),
        in_specs=[
            whole,
            weight,
            weight,
            flat(wide),
            by_token,
            pl.BlockSpec((1, blocks, slots, 1), lambda e: (e, 0, 0, 0)),
        ],
        out_specs=[flat(wide), flat(wide), flat(wide), whole, by_token],
        out_shape=[
            shape(wide, BF),
            shape(wide, BF),
            shape(wide, BF),
            jax.ShapeDtypeStruct(rows.shape, BF),
            jax.ShapeDtypeStruct(slot.shape, F32),
        ],
        scratch_shapes=[pltpu.VMEM((2 * wide, width), BF), pltpu.VMEM((count, 2 * wide), BF)],
        compiler_params=params(),
        cost_estimate=cost(
            8 * experts * count * width * wide,
            2 * experts * (2 * count * width + 2 * width * wide + 5 * count * wide),
            experts * count * wide,
        ),
    )(rows, gate_t, up_t, back, slot, slot_gates)


def norm_kernel(x_ref, add_ref, gain_ref, sum_ref, top_ref, bottom_ref):
    x = x_ref[...].astype(F32) + add_ref[...].astype(F32)
    sum_ref[...] = x
    scale = lax.rsqrt(jnp.mean(x * x, axis=-1, keepdims=True) + epsilon)
    out = (x * scale * gain_ref[...]).astype(BF)

    @pl.when(pl.program_id(0) < 2)
    def _():
        top_ref[...] = out

    @pl.when(pl.program_id(0) >= 2)
    def _():
        bottom_ref[...] = out


def norm_sum(values, added, gain):
    rows, width = values.shape
    block = pl.BlockSpec((rows // 4, width), lambda i: (i, 0))
    half = jax.ShapeDtypeStruct((rows // 2, width), BF)
    return pl.pallas_call(
        norm_kernel,
        name="norm_sum",
        grid=(4,),
        in_specs=[block, block, fixed((1, width))],
        out_specs=[
            block,
            pl.BlockSpec((rows // 4, width), lambda i: (jnp.minimum(i, 1), 0)),
            pl.BlockSpec((rows // 4, width), lambda i: (jnp.maximum(i - 2, 0), 0)),
        ],
        out_shape=[jax.ShapeDtypeStruct((rows, width), F32), half, half],
        compiler_params=params(),
        cost_estimate=cost(8 * rows * width, 10 * rows * width),
    )(values, added, gain.reshape(1, width))


def norm_back_kernel(x_ref, up_ref, res_ref, gain_ref, *rest):
    x = x_ref[...].astype(F32)
    up = up_ref[...].astype(F32)
    scale = lax.rsqrt(jnp.mean(x * x, axis=-1, keepdims=True) + epsilon)
    scaled = x * scale
    if len(rest) > 1:
        gain_grad_ref = rest[4]

        @pl.when(pl.program_id(0) == 0)
        def _():
            gain_grad_ref[...] = jnp.zeros_like(gain_grad_ref)

        gain_grad_ref[...] += jnp.sum(up * scaled, axis=0, keepdims=True)
    up = up * gain_ref[...]
    back = scale * (up - scaled * jnp.mean(up * scaled, axis=-1, keepdims=True))
    total = res_ref[...].astype(F32) + back
    if len(rest) == 1:
        rest[0][...] = total.astype(BF)
        return
    w_ref, low_ref, total_ref, out_ref = rest[:4]
    low = total.astype(BF)
    low_ref[...] = low
    total_ref[...] = total
    out_ref[...] = mm(low, w_ref[...], 1, 1).astype(BF)


def norm_back(values, upstream, residual, gain, weight):
    rows, width = values.shape
    block = pl.BlockSpec((rows // 4, width), lambda i: (i, 0))
    in_specs = [block, block, block, fixed((1, width))]
    out_specs = [block]
    shapes = [jax.ShapeDtypeStruct((rows, width), BF)]
    more = []
    if weight is not None:
        inner = weight.shape[0]
        more = [weight]
        in_specs += [fixed(weight.shape)]
        out_specs += [
            block,
            pl.BlockSpec((rows // 4, inner), lambda i: (i, 0)),
            fixed((1, width)),
        ]
        shapes += [
            jax.ShapeDtypeStruct((rows, width), F32),
            jax.ShapeDtypeStruct((rows, inner), BF),
            jax.ShapeDtypeStruct((1, width), F32),
        ]
    return pl.pallas_call(
        norm_back_kernel,
        name="norm_back",
        grid=(4,),
        in_specs=in_specs,
        out_specs=out_specs,
        out_shape=shapes,
        compiler_params=params(),
        cost_estimate=cost(12 * rows * width, 12 * rows * width),
    )(values, upstream, residual, gain.reshape(1, width), *more)


def shared_kernel(top_ref, bottom_ref, up_ref, wg_ref, wu_ref, wd_ref, act_ref, dg_ref, du_ref, grad_ref):
    ff = wd_ref.shape[0]
    x = jnp.concatenate([top_ref[...], bottom_ref[...]], axis=0)
    upstream = up_ref[...]
    a = mm(x, wg_ref[...], 1, 1)
    b = mm(x, wu_ref[...], 1, 1)
    back = mm(upstream, wd_ref[...], 1, 1)
    sig = jax.nn.sigmoid(a)
    swish = a * sig
    active = (swish * b).astype(BF)
    dg = (back * b * (sig + swish * (1.0 - sig))).astype(BF)
    du = (back * swish).astype(BF)
    act_ref[...] = active
    dg_ref[...] = dg
    du_ref[...] = du
    grad_ref[:ff, :] = mm(active, upstream, 0, 0).astype(BF)
    grad_ref[ff : 2 * ff, :] = mm(dg, x, 0, 0).astype(BF)
    grad_ref[2 * ff :, :] = mm(du, x, 0, 0).astype(BF)


def shared_step(top, bottom, upstream, gate_t, up_t, down):
    rows, width = upstream.shape
    ff = down.shape[0]
    inner = jax.ShapeDtypeStruct((rows, ff), BF)
    return pl.pallas_call(
        shared_kernel,
        name="shared_step",
        grid=(1,),
        in_specs=[fixed(top.shape)] * 2 + [fixed((rows, width))] + [fixed((ff, width))] * 3,
        out_specs=[fixed((rows, ff))] * 3 + [fixed((3 * ff, width))],
        out_shape=[inner, inner, inner, jax.ShapeDtypeStruct((3 * ff, width), BF)],
        compiler_params=params(),
        cost_estimate=cost(rows * width, rows * width),
    )(top, bottom, upstream, gate_t, up_t, down)


def finals_kernel(x_ref, proj_ref, query_ref, expand_ref):
    inner, rows = proj_ref.shape
    wide = query_ref.shape[1]
    part = x_ref.shape[1] - inner - wide
    count = expand_ref.shape[0]
    proj_ref[...] = x_ref[:, :inner].astype(F32).T
    query_ref[...] = x_ref[:, inner : inner + wide].astype(F32)
    for i in range(rows // count):
        expand_ref[:, i * part : (i + 1) * part] = x_ref[
            i * count : (i + 1) * count, inner + wide :
        ].astype(F32)


def finals(joined, inner, wide, count):
    rows = joined.shape[0]
    part = joined.shape[1] - inner - wide
    shapes = [(inner, rows), (rows, wide), (count, rows // count * part)]
    return pl.pallas_call(
        finals_kernel,
        name="finals",
        grid=(1,),
        in_specs=[fixed(joined.shape)],
        out_specs=[fixed(shape) for shape in shapes],
        out_shape=[jax.ShapeDtypeStruct(shape, F32) for shape in shapes],
        compiler_params=params(),
        cost_estimate=cost(rows, rows),
    )(joined)


def weight_grad_kernel(a_ref, x_ref, o_ref):
    ff = o_ref.shape[1]
    x = x_ref[...].reshape(-1, x_ref.shape[-1])
    o_ref[0] = mm(a_ref[0, :, :ff], x, 0, 0)


def weight_grad(active, rows, ff):
    experts, blocks, slots, width = rows.shape
    count, wide = active.shape[1:]
    return pl.pallas_call(
        weight_grad_kernel,
        name="weight_grad",
        grid=(experts,),
        in_specs=[
            pl.BlockSpec((1, count, wide), lambda e: (e, 0, 0)),
            pl.BlockSpec((1, blocks, slots, width), lambda e: (e, 0, 0, 0)),
        ],
        out_specs=pl.BlockSpec((1, ff, width), lambda e: (e, 0, 0)),
        out_shape=jax.ShapeDtypeStruct((experts, ff, width), F32),
        compiler_params=params(),
        cost_estimate=cost(count * width, count * width),
    )(active, rows)


def split_kernel(x_ref, *outs):
    at = 0
    for out in outs:
        out[...] = x_ref[at : at + out.shape[0], :].astype(F32)
        at += out.shape[0]


def split_rows(joined, sizes):
    width = joined.shape[1]
    return pl.pallas_call(
        split_kernel,
        name="split_rows",
        grid=(1,),
        in_specs=[fixed(joined.shape)],
        out_specs=[fixed((size, width)) for size in sizes],
        out_shape=[jax.ShapeDtypeStruct((size, width), F32) for size in sizes],
        compiler_params=params(),
        cost_estimate=cost(width, width),
    )(joined)


def dot(eq, a, b):
    return jnp.einsum(eq, a, b, preferred_element_type=F32)


def passed_along(shard, axis, by):
    peers = lax.axis_size(axis)
    pairs = [(i, i + by) for i in range(peers) if 0 <= i + by < peers]
    return lax.ppermute(shard, axis, pairs)


def normed(values, norm_gain):
    return (
        values * lax.rsqrt(jnp.mean(values * values, axis=-1, keepdims=True) + epsilon) * norm_gain
    )


def norm_backward(values, norm_gain, upstream):
    _, pullback = jax.vjp(normed, values, norm_gain)
    return pullback(upstream)


def rotate(values, cosine, sine):
    half = values.shape[-1] // 2
    front, back = values[..., :half], values[..., half:]
    return jnp.concatenate([front * cosine - back * sine, back * cosine + front * sine], axis=-1)


def rotate_back(upstream, cosine, sine):
    return rotate(upstream, cosine, -sine)


def silu_gate(gate_val, up_val):
    return gate_val * jax.nn.sigmoid(gate_val) * up_val


def silu_backward(gate_val, up_val, upstream):
    _, pullback = jax.vjp(silu_gate, gate_val, up_val)
    return pullback(upstream)


def rope_tables(seq_all, seq_here, index_here):
    starts = jnp.sum((seq_all[None, :] < seq_here[:, None]).astype(jnp.int32), axis=1)
    position = (index_here - starts).astype(F32)
    frequency = 10000.0 ** (-(jnp.arange(DR // 2, dtype=F32) * 2.0) / DR)
    angle = position[:, None] * frequency[None, :]
    return jnp.cos(angle), jnp.sin(angle)


def turned(value, by):
    return lax.ppermute(value, "dp", [(i, i ^ by) for i in range(lax.axis_size("dp"))])


def swapped(value):
    return turned(value, 1)


def after(value, *others):
    return lax.optimization_barrier((value,) + others)[0]


def scatter_sum(parts):
    joined = parts if not isinstance(parts, list) else jnp.concatenate(parts, axis=1)
    return lax.psum_scatter(joined, "dp", scatter_dimension=0, tiled=True)


def tensor_sum(value, first):
    peers = lax.axis_size("tensor")
    rank = lax.axis_index("tensor")
    size = value.shape[0] // peers
    piece = lambda at: lax.dynamic_slice_in_dim(value, at * size, size, 0)
    turn = lambda piece, by: lax.ppermute(
        piece, "tensor", [(i, (i + by) % peers) for i in range(peers)]
    )
    total = piece(rank).astype(F32)
    for by in range(1, peers):
        total = total + turn(piece((rank + by) % peers), by).astype(F32)
    mine = after(total.astype(BF), first)
    around = [turn(mine, by) for by in range(peers - 1, 0, -1)] + [mine]
    both = jnp.concatenate(around + around[:-1], axis=0)
    return lax.dynamic_slice_in_dim(both, (peers - 1 - rank) * size, value.shape[0], 0)


def shards(
    tokens,
    seq_ids,
    route_ids,
    cotangent,
    input_gain,
    w_query,
    w_latent,
    latent_gain,
    w_expand,
    w_out,
    middle_gain,
    w_router,
    expert_gate,
    expert_up,
    expert_down,
    shared_gate,
    shared_up,
    shared_down,
):
    devices = lax.axis_size("dp")
    rank_dp = lax.axis_index("dp")
    tok_rows, width = tokens.shape
    experts_local = expert_gate.shape[0]
    all_experts = w_router.shape[1]
    ff_local = expert_gate.shape[2]
    heads_local = w_query.shape[1] // (DN + DR)

    direct = devices == 8
    apart = jnp.array([0, 1, 2, 4, 3, 5, 6, 7] if direct else list(range(devices)), jnp.int32)
    order = (rank_dp ^ apart) if direct else apart

    index_here = rank_dp * tok_rows + jnp.arange(tok_rows, dtype=jnp.int32)
    seq_here = lax.dynamic_slice_in_dim(seq_ids, rank_dp * tok_rows, tok_rows, 0)
    cosine, sine = rope_tables(seq_ids, seq_here, index_here)
    token_features = tokens.astype(F32)
    hidden_in = normed(token_features, input_gain).astype(BF)
    latent_full = jnp.dot(hidden_in, w_latent, preferred_element_type=F32)
    latent_raw = latent_full[:, :KVR]
    latent = normed(latent_raw, latent_gain).astype(BF)
    rope_key = rotate(latent_full[:, KVR:], cosine, sine).astype(BF)
    fill = jnp.zeros((tok_rows, -(KVR + DR) % 128), BF)
    own_keys = jnp.concatenate([latent, rope_key, fill], axis=1)
    odd = rank_dp % 2
    blocks = jnp.stack(
        [rank_dp - 4, rank_dp - 2, (rank_dp - 2) ^ 1, rank_dp - 3 + 2 * odd, rank_dp]
    ).astype(jnp.int32)
    place_q = jnp.stack([seq_here, index_here], axis=1)
    sequences = seq_ids.reshape(1, -1)
    before_two = passed_along(own_keys, "dp", 2)
    before_four = passed_along(own_keys, "dp", 4)
    query_pre = jnp.dot(hidden_in, w_query, preferred_element_type=F32)
    route_all = lax.all_gather(after(route_ids, query_pre), "dp", tiled=True)
    before_four = after(before_four, query_pre, place_q, route_all)
    from_pair = swapped(jnp.where(odd == 0, own_keys, before_four))
    keys = [before_four, before_two, swapped(before_two), from_pair, own_keys]
    cot_all = lax.all_gather(after(cotangent, before_two, before_four), "dp", tiled=True)
    attended, lse, kv = attend(query_pre, cosine, sine, w_expand, blocks, place_q, sequences, keys)
    attention_part = jnp.dot(attended, w_out, preferred_element_type=F32).astype(BF)
    attention = lax.psum(attention_part, "tensor")

    local_ids = rank_dp * experts_local + jnp.arange(experts_local, dtype=jnp.int32)
    routes = jnp.take(route_all.reshape(devices, tok_rows, -1), order, axis=0)
    named_block = jnp.any(routes[..., None] == local_ids, axis=2)
    before = jnp.tril(jnp.ones((tok_rows, tok_rows), BF), -1)
    rank_within = dot("ts,bse->bte", before, named_block.astype(BF))
    slot_of = jnp.where(named_block, rank_within, -1.0)
    slot = slot_of.astype(jnp.int32).transpose(2, 0, 1)[:, :, None, :]
    columns = jnp.arange(experts_local * SLOTS, dtype=jnp.int32)
    spread = (columns[None, :] // SLOTS == jnp.arange(experts_local, dtype=jnp.int32)[:, None]).astype(
        BF
    )
    places = (
        dot("bte,en->btn", slot_of.astype(BF), spread) == (columns % SLOTS).astype(F32)
    ).astype(BF)
    gate_t = expert_gate.swapaxes(1, 2)
    up_t = expert_up.swapaxes(1, 2)
    cot_rows = pick(order, slot, cot_all)
    back = down_back(cot_rows, expert_down)

    attention = after(attention, cot_rows, places)
    middle, *hidden_mid = norm_sum(tokens, attention, middle_gain)
    first = (rank_dp * experts_local).astype(jnp.int32).reshape(1)
    router_rows = jnp.pad(w_router.T, ((0, -all_experts % 128), (0, 0)))
    if direct:
        pair = [swapped(part) for part in hidden_mid]
        by_x = [turned(part, 2) for part in hidden_mid]
        by_y = [turned(part, 4) for part in hidden_mid]
        held = pick_route(first, slot, [hidden_mid, pair], router_rows, all_experts, 0, 1, [])
    else:
        hidden_all = lax.all_gather(jnp.concatenate(hidden_mid, axis=0), "dp", tiled=True)

    top, bottom = hidden_mid
    if direct:
        top = after(top, pair[0])
    shared_active, shared_gate_grad, shared_up_grad, shared_grads = shared_step(
        top, bottom, cotangent, shared_gate.T, shared_up.T, shared_down
    )
    shared_result = jnp.dot(shared_active, shared_down, preferred_element_type=F32)
    if direct:
        x_top, x_bottom, y_top, y_bottom = lax.optimization_barrier(
            (*by_x, *by_y, held[0], back, shared_grads)
        )[:4]
        by_x, by_y = [x_top, x_bottom], [y_top, y_bottom]
        corner = [turned(y_top, 2), turned(x_bottom, 4)]
        pair_x = [swapped(part) for part in by_x]
        pair_y = [swapped(part) for part in by_y]
        held = pick_route(first, slot, [by_x, by_y], router_rows, all_experts, 2, 1, held)
        held = pick_route(first, slot, [pair_x, pair_y], router_rows, all_experts, 4, 1, held)
        corner[0] = after(corner[0], held[0])
        pair_corner = [swapped(part) for part in corner]
        held = pick_route(first, slot, [corner], router_rows, all_experts, 6, 1, held)
        held = pick_route(first, slot, [pair_corner], router_rows, all_experts, 7, 1, held)
        rows, router_probs, slot_gates = held
        hidden_parts = [*hidden_mid, *pair, *by_x, *by_y, *corner, *pair_x, *pair_y, *pair_corner]
    else:
        rows, router_probs, slot_gates = pick_route(
            first, slot, [[hidden_all]], router_rows, all_experts, 0, devices, []
        )
        hidden_parts = [hidden_all]
    shared_sums = lax.psum_scatter(
        after(shared_grads, rows), "dp", scatter_dimension=1, tiled=True
    )
    gated_active, gate_val_grad, up_val_grad, row_grad, probs_grad = expert_step(
        rows, gate_t, up_t, back, slot, slot_gates
    )
    if direct:
        put_args = (first, places, row_grad, router_probs, probs_grad, router_rows)
        some = lambda *at: jnp.array(at, jnp.int32)
        to_pair, logits_pair = put_route(some(4, 5, 7), False, *put_args, None)
        from_pair = swapped(to_pair)
        to_sibling, logits_sibling = put_route(some(1), False, *put_args, None)
        from_sibling = swapped(to_sibling)
        send_x, send_y, kept, logits_cross = put_route(some(2, 3, 6), False, *put_args, from_pair)
        send_x, shared_sums = lax.optimization_barrier((send_x, shared_sums))
        got_x = turned(send_x, 2)
        got_y = turned(send_y, 4)
        routed_part = put(order, places, row_out(gated_active, expert_down, devices))
        got_x, got_y, routed_part, from_sibling = lax.optimization_barrier(
            (got_x, got_y, routed_part, from_sibling)
        )
        shared_gate_grad = after(shared_gate_grad, routed_part)
        mid_from_shared = dot("tf,df->td", shared_gate_grad, shared_gate) + dot(
            "tf,df->td", shared_up_grad, shared_up
        )
        own, logits_own = put_route(some(0), False, *put_args, from_sibling)
        half = tok_rows // 2
        plus = lambda *terms: sum(term.astype(F32) for term in terms)
        last_y = turned(plus(kept[:half], got_x[:half]).astype(BF), 4)
        last_x = turned(plus(kept[half:], got_y[:half]).astype(BF), 2)
        last_y, last_x = lax.optimization_barrier((last_y, last_x, own, mid_from_shared))[:2]
        mid_block = jnp.concatenate(
            [plus(own[:half], got_x[half:], last_y), plus(own[half:], got_y[half:], last_x)], axis=0
        )
        logit_grads = [logits_own, logits_sibling, logits_cross, logits_pair]
    else:
        mid_part, logit_grad = put_route(
            order, True, first, places, row_grad, router_probs, probs_grad, router_rows, None
        )
        mid_block = scatter_sum(after(mid_part, shared_sums)).astype(F32)
        routed_part = put(order, places, row_out(gated_active, expert_down, devices))
        mid_block = after(mid_block, routed_part)
        shared_gate_grad = after(shared_gate_grad, routed_part)
        mid_from_shared = dot("tf,df->td", shared_gate_grad, shared_gate) + dot(
            "tf,df->td", shared_up_grad, shared_up
        )
        logit_grads = [logit_grad]
    mid_sum = (mid_block + mid_from_shared).astype(BF)
    routed_block = scatter_sum(routed_part)
    mid_grad = lax.psum(mid_sum, "tensor")
    grad_router = route_grad(logit_grads, hidden_parts)
    ff_part = (routed_block.astype(F32) + shared_result).astype(BF)
    feedforward = lax.psum(after(ff_part, mid_grad), "tensor")
    grad_expert_down = weight_grad(after(gated_active, mid_sum), cot_rows, ff_local)
    mid_grad = after(mid_grad, grad_router, ff_part, grad_expert_down)

    middle_low, middle_grad, attended_grad, grad_middle_gain = norm_back(
        middle, mid_grad, cotangent, middle_gain, w_out
    )
    attended_grad = after(attended_grad, ff_part)
    query_grad, expanded_grad, *window_grads = attend_back(
        query_pre, cosine, sine, w_expand, blocks, place_q, sequences, lse, attended_grad, kv, keys
    )
    four_grad, two_grad, pair_grad, last_grad, keys_grad = window_grads
    pair_grad = swapped(pair_grad)
    last_grad = swapped(last_grad).astype(F32)
    two_grad = (two_grad.astype(F32) + pair_grad.astype(F32)).astype(BF)
    four_grad = (four_grad.astype(F32) + jnp.where(odd == 1, last_grad, 0.0)).astype(BF)
    keys_grad = after(keys_grad, feedforward) + jnp.where(odd == 0, last_grad, 0.0)
    keys_grad = keys_grad + passed_along(two_grad, "dp", -2).astype(F32)
    keys_grad = keys_grad + passed_along(four_grad, "dp", -4).astype(F32)
    latent_raw_grad, grad_latent_gain = norm_backward(latent_raw, latent_gain, keys_grad[:, :KVR])
    rope_raw_grad = rotate_back(keys_grad[:, KVR : KVR + DR], cosine, sine)
    latent_full_grad = jnp.concatenate([latent_raw_grad, rope_raw_grad], axis=-1).astype(BF)
    input_part = dot("tc,dc->td", query_grad, w_query) + dot(
        "tc,dc->td", latent_full_grad, w_latent
    )
    _, grad_input_gain = norm_backward(token_features, input_gain, input_part)

    output = (middle + feedforward.astype(F32)).astype(BF)
    input_part, grad_input_gain = lax.optimization_barrier((input_part.astype(BF), grad_input_gain))
    input_part = after(input_part, feedforward)
    tensors = lax.axis_size("tensor")
    query_width = heads_local * (DN + DR)
    out_width = heads_local * DV
    expand_width = w_expand.shape[1] * KVR // width
    latent_width = KVR + DR
    gains = jnp.concatenate(
        [
            grad_middle_gain / tensors,
            grad_input_gain[None, :],
            jnp.repeat(grad_latent_gain, width // KVR)[None, :],
            jnp.zeros((61, width), F32),
        ],
        axis=0,
    )
    parts = parts_rows(latent_full_grad, hidden_in, grad_router, gains, all_experts)
    parts = lax.psum_scatter(parts, "dp", scatter_dimension=1, tiled=True)
    latents = jnp.concatenate([key[:, :KVR] for key in keys], axis=0)
    grad_expand = dot("wk,wc->kc", latents, after(expanded_grad, keys_grad)).astype(BF)
    share = KVR // devices
    grad_expand = (
        grad_expand.reshape(devices, share, -1, expand_width)
        .transpose(0, 2, 1, 3)
        .reshape(width, expand_width)
    )
    late = jnp.concatenate(
        [
            dot("td,tc->dc", middle_low, attended).astype(BF),
            dot("td,tc->dc", hidden_in, query_grad).astype(BF),
            grad_expand,
        ],
        axis=1,
    )
    rows_late = after(rows, late).reshape(experts_local, -1, width)
    grad_expert_gate = dot("ecd,ecf->edf", rows_late, gate_val_grad[..., :ff_local])
    grad_expert_up = dot("ecd,ecf->edf", rows_late, up_val_grad[..., :ff_local])
    late = scatter_sum(late)
    grad_out_proj, grad_query, grad_expand = finals(late, out_width, query_width, share)
    input_grad = lax.psum(input_part, "tensor")
    input_grad = after(input_grad, grad_expert_gate, grad_expert_up, output)
    (token_grad,) = norm_back(tokens, input_grad, middle_grad, input_gain, None)
    parts = tensor_sum(after(parts, input_grad), token_grad)
    latent_part, router_part, gain_part = split_rows(
        parts, [latent_width, all_experts, gains.shape[0]]
    )
    sw = shared_gate.shape[1]
    return (
        output,
        token_grad,
        gain_part[1],
        grad_query,
        latent_part.T,
        gain_part[2, :: width // KVR],
        grad_expand,
        grad_out_proj,
        gain_part[0],
        router_part.T,
        grad_expert_gate,
        grad_expert_up,
        grad_expert_down,
        shared_sums[sw : 2 * sw].astype(F32).T,
        shared_sums[2 * sw :].astype(F32).T,
        shared_sums[:sw].astype(F32),
    )


def solution(mesh):
    placed = (
        P("dp", None),
        P(),
        P("dp", None),
        P("dp", None),
        P(),
        P(None, "tensor"),
        P(),
        P(),
        P(None, "tensor"),
        P("tensor", None),
        P(),
        P(),
        P("dp", None, "tensor"),
        P("dp", None, "tensor"),
        P("dp", "tensor", None),
        P(None, "tensor"),
        P(None, "tensor"),
        P("tensor", None),
    )
    return jax.shard_map(
        shards,
        mesh=mesh,
        in_specs=placed,
        out_specs=(
            P("dp", None),
            P("dp", None),
            P("dp"),
            P("dp", "tensor"),
            P("dp", None),
            P("dp"),
            P("dp", "tensor"),
            P("tensor", "dp"),
            P("dp"),
            P("dp", None),
            P("dp", None, "tensor"),
            P("dp", None, "tensor"),
            P("dp", "tensor", None),
            P("dp", "tensor"),
            P("dp", "tensor"),
            P("tensor", "dp"),
        ),
        check_vma=False,
    )
```
